32 devices in a mesh: seq: 4 (over x, core), chan: 8 (over z, y).
Axes of the slice: x: 2, y: 2, z: 4, core: 2. Of those that a mesh axis runs over, the one named last changes fastest.
Arguments:
- features: bfloat16 [3, 4096, 512], P(None, 'chan', 'seq'), may hold values from -6 to 6
- cotangent: bfloat16 [4096, 512], P('chan', 'seq'), may hold values from -6 to 6
- long_filter: bfloat16 [4096, 512], P('chan', 'seq'), may hold values from -0.25 to 0.25
- short_filters: float32 [3, 4096, 3], P(None, 'chan'), may hold values from -3.5 to 3.5
- skip_gain: float32 [4096], P('chan'), may hold values from -4 to 4
Outputs:
- gated_out: bfloat16 [4096, 512], P('chan', 'seq')
- feature_grad: bfloat16 [3, 4096, 512], P(None, 'chan', 'seq')
- long_grad: bfloat16 [4096, 512], P('chan', 'seq')
- short_grad: float32 [3, 4096, 3], P(None, 'chan')
- skip_grad: float32 [4096], P('chan')
The draws below stay inside these ranges and needn't reach their ends.
All inputs are finite; a program needn't handle non-finite values.
Results may differ from the reference program's by a relative error of at most 0.015.
Values may be sent and summed in bfloat16 or wider, within the bound.
A program may use at most 64 MiB of HBM per device.

```python
import math
import jax
import jax.numpy as jnp
from jax import lax

D = 4096
TAPS = 3
LEN = 512


def block_levels(stream_key, extent, pieces, least, largest):
    factor_of = 1.0
    for position, parts in pieces:
        heights = jax.random.uniform(jax.random.fold_in(jax.random.fold_in(stream_key, 6), position), (parts,), jnp.float32, least / len(pieces), largest / len(pieces))
        factor_of = factor_of * jnp.repeat(jnp.exp(heights), extent[position] // parts).reshape((-1,) + (1,) * (len(extent) - 1 - position))
    return factor_of


def gaussian(stream_key, extent, spread, bound, pieces=(), kind=jnp.bfloat16):
    drawn = spread * jax.random.normal(stream_key, extent, jnp.float32)
    if pieces:
        drawn = drawn * block_levels(stream_key, extent, pieces, -0.22, 0.18)
    return jnp.clip(drawn, -bound, bound).astype(kind)


def setup_inputs(seed: int = 0) -> dict:
    keys = jax.random.split(jax.random.key(seed), 6)
    features = gaussian(keys[0], (3, D, LEN), 1.0, 6.0, ((1, 8), (2, 4)))
    cotangent = gaussian(keys[1], (D, LEN), 1.0, 6.0, ((0, 8), (1, 4)))
    long_filter = gaussian(keys[2], (D, LEN), LEN ** -0.5, 0.25, ((0, 8), (1, 4)))
    short_filters = gaussian(keys[3], (3, D, TAPS), TAPS ** -0.5, 3.5, ((1, 8),), jnp.float32)
    skip_gain = gaussian(keys[4], (D,), 1.0, 4.0, ((0, 8),), jnp.float32)
    return dict(features=features, cotangent=cotangent, long_filter=long_filter, short_filters=short_filters, skip_gain=skip_gain)


def delayed(values, offset):
    if offset == 0:
        return values
    padding = jnp.zeros(values.shape[:-1] + (offset,), values.dtype)
    return jnp.concatenate([padding, values[..., :-offset]], axis=-1)


def advanced(values, offset):
    if offset == 0:
        return values
    padding = jnp.zeros(values.shape[:-1] + (offset,), values.dtype)
    return jnp.concatenate([values[..., offset:], padding], axis=-1)


def long_terms(block):
    mixed_block, gated_block, kernel_block = block
    length = mixed_block.shape[-1]
    mixed_freq = jnp.fft.rfft(mixed_block, n=2 * length, axis=-1)
    gated_freq = jnp.fft.rfft(gated_block, n=2 * length, axis=-1)
    kernel_freq = jnp.fft.rfft(kernel_block, n=2 * length, axis=-1)
    conv_part = jnp.fft.irfft(mixed_freq * kernel_freq, n=2 * length, axis=-1)[:, :length]
    corr_part = jnp.fft.irfft(gated_freq * jnp.conj(kernel_freq), n=2 * length, axis=-1)[:, :length]
    cross_part = jnp.fft.irfft(gated_freq * jnp.conj(mixed_freq), n=2 * length, axis=-1)[:, :length]
    return conv_part.astype(jnp.float32), corr_part.astype(jnp.float32), cross_part.astype(jnp.float32)


def reference(features, cotangent, long_filter, short_filters, skip_gain):
    wide = features.astype(jnp.float32)
    primed = short_filters[:, :, 0:1] * wide
    for offset in range(1, TAPS):
        primed = primed + short_filters[:, :, offset:offset + 1] * delayed(wide, offset)
    mixed_term = (primed[1] * primed[2]).astype(jnp.bfloat16)
    cot_wide = cotangent.astype(jnp.float32)
    gated_grad = (cot_wide * primed[0]).astype(jnp.bfloat16)
    mixed_wide = mixed_term.astype(jnp.float32)
    gated_wide = gated_grad.astype(jnp.float32)
    block_rows = math.gcd(D, 256)
    block_count = D // block_rows
    blocks = (mixed_wide.reshape(block_count, block_rows, LEN),
              gated_wide.reshape(block_count, block_rows, LEN),
              long_filter.astype(jnp.float32).reshape(block_count, block_rows, LEN))
    conv_part, corr_part, cross_part = lax.map(long_terms, blocks)
    conv_part = conv_part.reshape(D, LEN)
    corr_part = corr_part.reshape(D, LEN)
    cross_part = cross_part.reshape(D, LEN)
    gain_column = skip_gain[:, None]
    long_out = (conv_part + gain_column * mixed_wide).astype(jnp.bfloat16)
    mixed_grad = (corr_part + gain_column * gated_wide).astype(jnp.bfloat16)
    long_wide = long_out.astype(jnp.float32)
    gated_out = (primed[0] * long_wide).astype(jnp.bfloat16)
    mixed_back = mixed_grad.astype(jnp.float32)
    primed_grad = jnp.stack([cot_wide * long_wide, mixed_back * primed[2], mixed_back * primed[1]])
    feature_grad = short_filters[:, :, 0:1] * primed_grad
    for offset in range(1, TAPS):
        feature_grad = feature_grad + short_filters[:, :, offset:offset + 1] * advanced(primed_grad, offset)
    short_grad = jnp.stack([jnp.sum(primed_grad * delayed(wide, offset), axis=-1) for offset in range(TAPS)], axis=-1)
    skip_grad = jnp.sum(gated_wide * mixed_wide, axis=-1)
    return gated_out, feature_grad.astype(jnp.bfloat16), cross_part.astype(jnp.bfloat16), short_grad, skip_grad
```

```python
import functools
import math

import jax
import jax.numpy as jnp
import numpy as np
from jax import lax
from jax.experimental import pallas as pl
from jax.experimental.pallas import tpu as pltpu
from jax.sharding import PartitionSpec as P

inner_length = 128
radix_width = 8
chunk_count = 2


def phase_tables(row_count, col_count, length, direction):
    phase_index = (
        lax.iota(jnp.int32, row_count)[:, None] * lax.iota(jnp.int32, col_count)[None, :] % length
    )
    angles = direction * 2.0 * math.pi / length * phase_index.astype(jnp.float32)
    return (jnp.cos(angles), jnp.sin(angles))


def last_axis(operand, matrix):
    return jnp.einsum("...n,nk->...k", operand, matrix, precision=lax.Precision.HIGH)


def first_axis(operand, matrix):
    return jnp.einsum("...ab,ak->...kb", operand, matrix, precision=lax.Precision.HIGH)


def transform(real_part, imag_part, direction):
    length = real_part.shape[-1]
    if length <= inner_length or length % radix_width != 0:
        cos_table, sin_table = phase_tables(length, length, length, direction)
        return (
            last_axis(real_part, cos_table) - last_axis(imag_part, sin_table),
            last_axis(real_part, sin_table) + last_axis(imag_part, cos_table),
        )
    rest_length = length // radix_width
    grid_shape = real_part.shape[:-1] + (radix_width, rest_length)
    real_grid = real_part.reshape(grid_shape)
    imag_grid = imag_part.reshape(grid_shape)
    cos_table, sin_table = phase_tables(radix_width, radix_width, radix_width, direction)
    section_real = first_axis(real_grid, cos_table) - first_axis(imag_grid, sin_table)
    section_imag = first_axis(real_grid, sin_table) + first_axis(imag_grid, cos_table)
    twist_cos, twist_sin = phase_tables(radix_width, rest_length, length, direction)
    turned_real = section_real * twist_cos - section_imag * twist_sin
    turned_imag = section_real * twist_sin + section_imag * twist_cos
    inner_real, inner_imag = transform(turned_real, turned_imag, direction)
    return (
        jnp.swapaxes(inner_real, -1, -2).reshape(real_part.shape),
        jnp.swapaxes(inner_imag, -1, -2).reshape(real_part.shape),
    )


def spectral(mixed_term, gated_grad, kernel, local_gain):
    length = mixed_term.shape[-1]
    mixed_wide = mixed_term.astype(jnp.float32)
    gated_wide = gated_grad.astype(jnp.float32)
    kernel_wide = kernel.astype(jnp.float32)
    extend = ((0, 0), (0, length))
    real_in = jnp.stack([jnp.pad(mixed_wide, extend), jnp.pad(kernel_wide, extend)])
    imag_in = jnp.stack(
        [jnp.pad(gated_wide, extend), jnp.zeros((kernel_wide.shape[0], 2 * length), jnp.float32)]
    )
    freq_real, freq_imag = transform(real_in, imag_in, -1.0)
    packed_real = freq_real[0]
    packed_imag = freq_imag[0]
    mirror_real = jnp.roll(jnp.flip(packed_real, -1), 1, -1)
    mirror_imag = jnp.roll(jnp.flip(packed_imag, -1), 1, -1)
    mix_real = 0.5 * (packed_real + mirror_real)
    mix_imag = 0.5 * (packed_imag - mirror_imag)
    grad_real = 0.5 * (packed_imag + mirror_imag)
    grad_imag = 0.5 * (mirror_real - packed_real)
    kern_real = freq_real[1]
    kern_imag = freq_imag[1]
    conv_real = mix_real * kern_real - mix_imag * kern_imag
    conv_imag = mix_real * kern_imag + mix_imag * kern_real
    corr_real = grad_real * kern_real + grad_imag * kern_imag
    corr_imag = grad_imag * kern_real - grad_real * kern_imag
    cross_real = grad_real * mix_real + grad_imag * mix_imag
    cross_imag = grad_imag * mix_real - grad_real * mix_imag
    back_real = jnp.stack([conv_real - corr_imag, cross_real])
    back_imag = jnp.stack([conv_imag + corr_real, cross_imag])
    time_real, time_imag = transform(back_real, back_imag, 1.0)
    inverse_scale = 1.0 / (2 * length)
    conv_part = time_real[0, :, :length] * inverse_scale
    corr_part = time_imag[0, :, :length] * inverse_scale
    cross_part = time_real[1, :, :length] * inverse_scale
    gain_column = local_gain[:, None]
    long_out = (conv_part + gain_column * mixed_wide).astype(jnp.bfloat16)
    mixed_grad = (corr_part + gain_column * gated_wide).astype(jnp.bfloat16)
    return (long_out, mixed_grad, cross_part.astype(jnp.bfloat16))


def featurize(history, weights, margin, span_count):
    running = weights[:, :, 0:1] * history[:, :, margin : margin + span_count]
    for offset in range(1, margin + 1):
        running = (
            running
            + weights[:, :, offset : offset + 1]
            * history[:, :, margin - offset : margin - offset + span_count]
        )
    return running


def unfeaturize(padded_grad, weights, span_count):
    running = weights[:, :, 0:1] * padded_grad[:, :, 0:span_count]
    for offset in range(1, weights.shape[2]):
        running = (
            running
            + weights[:, :, offset : offset + 1] * padded_grad[:, :, offset : offset + span_count]
        )
    return running


def tap_grads(primed_grad, history, margin, span_count):
    columns = []
    for offset in range(margin + 1):
        columns.append(
            jnp.sum(
                primed_grad * history[:, :, margin - offset : margin - offset + span_count], axis=-1
            )
        )
    return jnp.stack(columns, axis=-1)


def packed_tables(length):
    steps = np.arange(length)
    phase = (steps[:, None] * steps[None, :]) % (2 * length)
    angles = np.pi / length * phase
    sines = np.sin(angles)
    sines[:, 0] = 1.0 - 2.0 * (steps % 2)
    table = np.concatenate([np.cos(angles), sines], 1).astype(np.float32)
    high = table.astype(jnp.bfloat16)
    low = (table - high.astype(np.float32)).astype(jnp.bfloat16)
    return np.stack([high, low])


def fused_kernel(
    sizes,
    feat_hbm,
    cot_hbm,
    filt_hbm,
    short_hbm,
    gain_hbm,
    table_hbm,
    gated_hbm,
    grad_hbm,
    long_hbm,
    taps_hbm,
    skip_hbm,
    table,
    short_rows,
    gain_line,
    coef_rows,
    coef_cols,
    arrived,
    stacked,
    primed_buf,
    freq,
    back_both,
    back_time,
    results,
    sums,
    taps_out,
    skip_out,
    load_sem,
    own_in,
    own_out,
    in_send,
    in_recv,
    out_send,
    out_recv,
    small_own,
    small_send,
    small_recv,
):
    groups, rows, span, length, taps, chunks = sizes
    chunk_rows = rows // chunks
    me = lax.axis_index("seq")

    def at(index, extent):
        return pl.ds(pl.multiple_of(index * extent, extent), extent)

    def chan_rows(owner, chunk):
        start = owner * rows + chunk * chunk_rows
        return pl.ds(pl.multiple_of(start, chunk_rows), chunk_rows)

    barrier = pltpu.get_barrier_semaphore()
    for offset in range(1, groups):
        pl.semaphore_signal(
            barrier,
            inc=1,
            device_id={"seq": lax.rem(me + offset, groups)},
            device_id_type=pl.DeviceIdType.MESH,
        )
    loads = [
        pltpu.make_async_copy(short_hbm.at[:, :, at(me, rows)], short_rows, load_sem.at[0]),
        pltpu.make_async_copy(gain_hbm, gain_line, load_sem.at[1]),
        pltpu.make_async_copy(table_hbm, table, load_sem.at[2]),
    ]
    for load in loads:
        load.start()

    def in_pairs(owner, source, chunk):
        taken = chan_rows(owner, chunk)
        kept = pl.ds(chunk * chunk_rows, chunk_rows)
        return [
            (filt_hbm.at[taken, :], arrived.at[source, 4, kept, :]),
            (feat_hbm.at[:, taken, :], arrived.at[source, 0:3, kept, :]),
            (cot_hbm.at[taken, :], arrived.at[source, 3, kept, :]),
        ]

    def out_pairs(target, owner, chunk):
        kept = pl.ds(chunk * chunk_rows, chunk_rows)
        placed = chan_rows(owner, chunk)
        return [
            (results.at[target, 0, kept, :], gated_hbm.at[placed, :]),
            (results.at[target, 1:4, kept, :], grad_hbm.at[:, placed, :]),
            (results.at[target, 4, kept, :], long_hbm.at[placed, :]),
        ]

    def remote(pair, send_sem, recv_sem, peer):
        return pltpu.make_async_remote_copy(
            src_ref=pair[0],
            dst_ref=pair[1],
            send_sem=send_sem,
            recv_sem=recv_sem,
            device_id={"seq": peer},
            device_id_type=pl.DeviceIdType.MESH,
        )

    own_copies = []
    for chunk in range(chunks):
        for kind, pair in enumerate(in_pairs(me, me, chunk)):
            copy = pltpu.make_async_copy(pair[0], pair[1], own_in.at[chunk, kind])
            copy.start()
            own_copies.append(copy)

    pl.semaphore_wait(barrier, groups - 1)

    sent = []
    for chunk in range(chunks):
        for offset in range(1, groups):
            peer = lax.rem(me + offset, groups)
            for kind, pair in enumerate(in_pairs(peer, me, chunk)):
                copy = remote(
                    pair, in_send.at[chunk, kind, offset], in_recv.at[chunk, kind, offset], peer
                )
                copy.start()
                sent.append(copy)

    loads[0].wait()
    loads[1].wait()
    coef_rows[...] = jnp.zeros_like(coef_rows)
    for stream in range(3):
        coef_rows[stream * taps : (stream + 1) * taps, :] = short_rows[stream]
    gain_row = jnp.zeros((1, rows), jnp.float32)
    for group in range(groups):
        part = gain_line[:, group * rows : (group + 1) * rows]
        gain_row = gain_row + jnp.where(me == group, part, 0.0)
    coef_rows[3 * taps : 3 * taps + 1, :] = gain_row
    coef_cols[...] = coef_rows[...].T
    loads[2].wait()

    group_rows = 64
    scale = 1.0 / length

    def tokens_of(kind, picked):
        return jnp.concatenate([arrived[group, kind, picked, :] for group in range(groups)], 1)

    def finish(kind, picked, values):
        for group in range(groups):
            results[group, kind, picked, :] = values[:, group * span : (group + 1) * span].astype(
                jnp.bfloat16
            )

    def column(index, picked):
        return coef_cols[picked, index : index + 1]

    def delayed(values, offset):
        if offset == 0:
            return values
        lane = lax.broadcasted_iota(jnp.int32, values.shape, 1)
        return jnp.where(lane >= offset, pltpu.roll(values, offset, 1), 0.0)

    def advanced(values, offset):
        if offset == 0:
            return values
        lane = lax.broadcasted_iota(jnp.int32, values.shape, 1)
        moved = pltpu.roll(values, length - offset, 1)
        return jnp.where(lane < length - offset, moved, 0.0)

    def send_kinds(chunk, kinds):
        for offset in range(1, groups):
            peer = lax.rem(me + offset, groups)
            pairs = out_pairs(peer, me, chunk)
            for kind in kinds:
                copy = remote(
                    pairs[kind],
                    out_send.at[chunk, kind, offset],
                    out_recv.at[chunk, kind, offset],
                    peer,
                )
                copy.start()
                sent.append(copy)

    for chunk in range(chunks):
        base = chunk * chunk_rows
        for kind in range(3):
            own_copies[chunk * 3 + kind].wait()
        for offset in range(1, groups):
            source = lax.rem(me + groups - offset, groups)
            for kind, pair in enumerate(in_pairs(me, source, chunk)):
                remote(
                    pair, in_send.at[chunk, kind, offset], in_recv.at[chunk, kind, offset], source
                ).wait_recv()

        @pl.loop(0, chunk_rows // group_rows)
        def _(step):
            inner = pl.ds(pl.multiple_of(step * group_rows, group_rows), group_rows)
            picked = pl.ds(pl.multiple_of(base + step * group_rows, group_rows), group_rows)
            primed = []
            for stream in range(3):
                wide = tokens_of(stream, picked).astype(jnp.float32)
                running = column(stream * taps, picked) * wide
                for offset in range(1, taps):
                    running = running + column(stream * taps + offset, picked) * delayed(
                        wide, offset
                    )
                primed.append(running)
                primed_buf[stream, inner, :] = running
            stacked[0, inner, :] = (primed[1] * primed[2]).astype(jnp.bfloat16)
            cot_wide = tokens_of(3, picked).astype(jnp.float32)
            stacked[1, inner, :] = (cot_wide * primed[0]).astype(jnp.bfloat16)
            stacked[2, inner, :] = tokens_of(4, picked)

        tile = 512

        @pl.loop(0, 2 * length // tile)
        def _(step):
            columns = pl.ds(pl.multiple_of(step * tile, tile), tile)
            left = stacked[...].reshape(3 * chunk_rows, length)
            total = jnp.dot(left, table[0, :, columns], preferred_element_type=jnp.float32)
            total += jnp.dot(left, table[1, :, columns], preferred_element_type=jnp.float32)
            freq[:, :, columns] = total.reshape(3, chunk_rows, tile)

        @pl.loop(0, chunk_rows // group_rows)
        def _(step):
            inner = pl.ds(pl.multiple_of(step * group_rows, group_rows), group_rows)
            first = lax.broadcasted_iota(jnp.int32, (group_rows, length), 1) == 0
            weight = jnp.where(first, 0.5 * scale, scale)
            mix_c, mix_s = freq[0, inner, :length], freq[0, inner, length:]
            grad_c, grad_s = freq[1, inner, :length], freq[1, inner, length:]
            kern_c, kern_s = freq[2, inner, :length], freq[2, inner, length:]

            def put(slot, left_c, left_s, right_c, right_s, sign):
                both = left_s * right_s
                even = left_c * right_c + sign * jnp.where(first, 0.0, both)
                odd = jnp.where(first, both, left_s * right_c - sign * (left_c * right_s))
                for half, part in enumerate((even, odd)):
                    value = part * weight
                    high = value.astype(jnp.bfloat16)
                    low = (value - high.astype(jnp.float32)).astype(jnp.bfloat16)
                    back_both[slot, inner, half * length : (half + 1) * length] = high
                    back_both[3 + slot, inner, half * length : (half + 1) * length] = low

            put(0, mix_c, mix_s, kern_c, kern_s, -1.0)
            put(1, grad_c, grad_s, kern_c, kern_s, 1.0)
            put(2, grad_c, grad_s, mix_c, mix_s, 1.0)

        @pl.loop(0, length // tile)
        def _(step):
            picked = pl.ds(pl.multiple_of(step * tile, tile), tile)
            both = back_both[...].reshape(6 * chunk_rows, 2 * length)
            high = both[: 3 * chunk_rows]
            turned = (((1,), (1,)), ((), ()))
            pair = lax.dot_general(
                both, table[0, picked, :], turned, preferred_element_type=jnp.float32
            )
            total = pair[: 3 * chunk_rows] + pair[3 * chunk_rows :]
            total += lax.dot_general(
                high, table[1, picked, :], turned, preferred_element_type=jnp.float32
            )
            back_time[:, :, picked] = total.reshape(3, chunk_rows, tile)

        finish(4, pl.ds(base, chunk_rows), back_time[2])
        send_kinds(chunk, (2,))
        whole = pl.ds(base, chunk_rows)
        with_gain = back_time[0] + column(3 * taps, whole) * stacked[0].astype(jnp.float32)
        back_time[0] = with_gain.astype(jnp.bfloat16).astype(jnp.float32)
        finish(0, whole, primed_buf[0] * back_time[0])
        send_kinds(chunk, (0,))

        @pl.loop(0, chunk_rows // group_rows)
        def _(step):
            inner = pl.ds(pl.multiple_of(step * group_rows, group_rows), group_rows)
            picked = pl.ds(pl.multiple_of(base + step * group_rows, group_rows), group_rows)
            mixed = stacked[0, inner, :].astype(jnp.float32)
            gated = stacked[1, inner, :].astype(jnp.float32)
            gain = column(3 * taps, picked)
            long_wide = back_time[0, inner, :]
            mixed_back = (
                (back_time[1, inner, :] + gain * gated).astype(jnp.bfloat16).astype(jnp.float32)
            )
            cot_wide = tokens_of(3, picked).astype(jnp.float32)
            primed_grad = [
                cot_wide * long_wide,
                mixed_back * primed_buf[2, inner, :],
                mixed_back * primed_buf[1, inner, :],
            ]
            lane = lax.broadcasted_iota(jnp.int32, (group_rows, sums.shape[1]), 1)
            line = jnp.zeros((group_rows, sums.shape[1]), jnp.float32)
            for stream in range(3):
                moving = primed_grad[stream]
                wide = tokens_of(stream, picked).astype(jnp.float32)
                running = column(stream * taps, picked) * moving
                for offset in range(taps):
                    if offset:
                        running = running + column(stream * taps + offset, picked) * advanced(
                            moving, offset
                        )
                    total = jnp.sum(moving * delayed(wide, offset), axis=1, keepdims=True)
                    line = jnp.where(lane == stream * taps + offset, total, line)
                finish(1 + stream, picked, running)
            total = jnp.sum(gated * mixed, axis=1, keepdims=True)
            sums[picked, :] = jnp.where(lane == 3 * taps, total, line)

        send_kinds(chunk, (1,))
        for kind, pair in enumerate(out_pairs(me, me, chunk)):
            copy = pltpu.make_async_copy(pair[0], pair[1], own_out.at[chunk, kind])
            copy.start()
            own_copies.append(copy)

    turned_sums = sums[...].T
    for stream in range(3):
        taps_out[stream] = turned_sums[stream * taps : (stream + 1) * taps, :]
    skip_out[...] = turned_sums[3 * taps : 3 * taps + 1, :]

    def small_pairs(owner):
        return [
            (taps_out, taps_hbm.at[:, :, at(owner, rows)]),
            (skip_out, skip_hbm.at[:, at(owner, rows)]),
        ]

    for kind, pair in enumerate(small_pairs(me)):
        copy = pltpu.make_async_copy(pair[0], pair[1], small_own.at[kind])
        copy.start()
        own_copies.append(copy)
        for offset in range(1, groups):
            peer = lax.rem(me + offset, groups)
            copy = remote(pair, small_send.at[kind, offset], small_recv.at[kind, offset], peer)
            copy.start()
            sent.append(copy)
    for copy in sent:
        copy.wait_send()
    for copy in own_copies[3 * chunks :]:
        copy.wait()
    for offset in range(1, groups):
        source = lax.rem(me + groups - offset, groups)
        for chunk in range(chunks):
            for kind, pair in enumerate(out_pairs(me, source, chunk)):
                remote(
                    pair, out_send.at[chunk, kind, offset], out_recv.at[chunk, kind, offset], source
                ).wait_recv()
        for kind, pair in enumerate(small_pairs(source)):
            remote(
                pair, small_send.at[kind, offset], small_recv.at[kind, offset], source
            ).wait_recv()


def settle_kernel(*refs):
    count = len(refs) // 2
    finished = refs[2 * count]
    copies = []
    for index in range(count):
        copy = pltpu.make_async_copy(refs[index], refs[count + index], finished.at[index])
        copy.start()
        copies.append(copy)
    for copy in copies:
        copy.wait()


def settle(values):
    return pl.pallas_call(
        settle_kernel,
        out_shape=tuple(jax.ShapeDtypeStruct(value.shape, value.dtype) for value in values),
        in_specs=[pl.BlockSpec(memory_space=pltpu.VMEM)] * len(values),
        out_specs=(pl.BlockSpec(memory_space=pltpu.HBM),) * len(values),
        scratch_shapes=[pltpu.SemaphoreType.DMA((len(values),))],
    )(*[pltpu.with_memory_space_constraint(value, pltpu.VMEM) for value in values])


def fused(features, cotangent, long_filter, short_filters, skip_gain, groups, chunks):
    channels, span = cotangent.shape
    rows = channels // groups
    length = span * groups
    taps = short_filters.shape[2]
    chunk_rows = rows // chunks
    hbm = pl.BlockSpec(memory_space=pltpu.HBM)
    dma = pltpu.SemaphoreType.DMA
    narrow = jnp.bfloat16
    outputs = pl.pallas_call(
        functools.partial(fused_kernel, (groups, rows, span, length, taps, chunks)),
        out_shape=(
            pltpu.VMEM((channels, span), narrow),
            pltpu.VMEM((3, channels, span), narrow),
            pltpu.VMEM((channels, span), narrow),
            pltpu.VMEM((3, taps, channels), jnp.float32),
            pltpu.VMEM((1, channels), jnp.float32),
        ),
        in_specs=[hbm] * 6,
        out_specs=(pl.BlockSpec(memory_space=pltpu.VMEM),) * 5,
        scratch_shapes=[
            pltpu.VMEM((2, length, 2 * length), narrow),
            pltpu.VMEM((3, taps, rows), jnp.float32),
            pltpu.VMEM((1, channels), jnp.float32),
            pltpu.VMEM((rows, rows), jnp.float32),
            pltpu.VMEM((rows, rows), jnp.float32),
            pltpu.VMEM((groups, 5, rows, span), narrow),
            pltpu.VMEM((3, chunk_rows, length), narrow),
            pltpu.VMEM((3, chunk_rows, length), jnp.float32),
            pltpu.VMEM((3, chunk_rows, 2 * length), jnp.float32),
            pltpu.VMEM((6, chunk_rows, 2 * length), narrow),
            pltpu.VMEM((3, chunk_rows, length), jnp.float32),
            pltpu.VMEM((groups, 5, rows, span), narrow),
            pltpu.VMEM((rows, rows), jnp.float32),
            pltpu.VMEM((3, taps, rows), jnp.float32),
            pltpu.VMEM((1, rows), jnp.float32),
            dma((3,)),
            dma((chunks, 3)),
            dma((chunks, 3)),
            dma((chunks, 3, groups)),
            dma((chunks, 3, groups)),
            dma((chunks, 3, groups)),
            dma((chunks, 3, groups)),
            dma((2,)),
            dma((2, groups)),
            dma((2, groups)),
        ],
        compiler_params=pltpu.CompilerParams(
            collective_id=0, has_side_effects=True
        ),
    )(
        features,
        cotangent,
        long_filter,
        jnp.swapaxes(short_filters, 1, 2),
        skip_gain[None],
        packed_tables(length),
    )
    gated_out, feature_grad, long_grad, taps_grad, gain_grad = settle(outputs)
    return gated_out, feature_grad, long_grad, jnp.swapaxes(taps_grad, 1, 2), gain_grad[0]


def dense_fits(features, short_filters, groups):
    channels, span = features.shape[1:]
    rows, length = channels // groups, span * groups
    return (
        channels % groups == 0
        and rows % 128 == 0
        and span % 128 == 0
        and length % 512 == 0
        and length <= 1024
        and rows <= 256
        and 3 * short_filters.shape[2] < 16
    )


def shards(features, cotangent, long_filter, short_filters, skip_gain):
    groups = lax.axis_size("seq")
    if dense_fits(features, short_filters, groups):
        return fused(
            features, cotangent, long_filter, short_filters, skip_gain, groups, chunk_count
        )
    seq_index = lax.axis_index("seq")
    channels = features.shape[1]
    per_group = channels // groups
    margin = short_filters.shape[2] - 1
    local_gain = lax.dynamic_slice_in_dim(skip_gain, seq_index * per_group, per_group, 0)
    stacked = jnp.concatenate([features, cotangent[None], long_filter[None]], 0)
    columns = lax.all_to_all(stacked, "seq", split_axis=1, concat_axis=2, tiled=True)
    weights = lax.dynamic_slice_in_dim(short_filters, seq_index * per_group, per_group, 1)
    length = columns.shape[2]
    history = jnp.pad(columns[:3].astype(jnp.float32), ((0, 0), (0, 0), (margin, 0)))
    primed = featurize(history, weights, margin, length)
    mixed_term = (primed[1] * primed[2]).astype(jnp.bfloat16)
    cot_wide = columns[3].astype(jnp.float32)
    gated_grad = (cot_wide * primed[0]).astype(jnp.bfloat16)
    long_out, mixed_grad, kernel_grad = spectral(mixed_term, gated_grad, columns[4], local_gain)
    long_wide = long_out.astype(jnp.float32)
    mixed_back = mixed_grad.astype(jnp.float32)
    gated_out = (primed[0] * long_wide).astype(jnp.bfloat16)
    primed_grad = jnp.stack([cot_wide * long_wide, mixed_back * primed[2], mixed_back * primed[1]])
    padded_grad = jnp.pad(primed_grad, ((0, 0), (0, 0), (0, margin)))
    feature_grad = unfeaturize(padded_grad, weights, length).astype(jnp.bfloat16)
    taps_grad = tap_grads(primed_grad, history, margin, length)
    gain_grad = jnp.sum(gated_grad.astype(jnp.float32) * mixed_term.astype(jnp.float32), axis=-1)
    results = jnp.concatenate([gated_out[None], feature_grad, kernel_grad[None]], 0)
    row_blocks = lax.all_to_all(results, "seq", split_axis=2, concat_axis=1, tiled=True)
    short_grad, skip_grad = (
        lax.all_gather(taps_grad, "seq", axis=1, tiled=True),
        lax.all_gather(gain_grad, "seq", axis=0, tiled=True),
    )
    return (row_blocks[0], row_blocks[1:4], row_blocks[4], short_grad, skip_grad)


def solution(mesh):
    placed = (
        P(None, "chan", "seq"),
        P("chan", "seq"),
        P("chan", "seq"),
        P(None, "chan", None),
        P("chan"),
    )
    return jax.shard_map(
        shards,
        mesh=mesh,
        in_specs=placed,
        out_specs=(
            P("chan", "seq"),
            P(None, "chan", "seq"),
            P("chan", "seq"),
            P(None, "chan", None),
            P("chan"),
        ),
        check_vma=False,
    )
```

```python
import functools
import math

import jax
import jax.numpy as jnp
import numpy as np
from jax import lax
from jax.experimental import pallas as pl
from jax.experimental.pallas import tpu as pltpu
from jax.sharding import PartitionSpec as P

inner_length = 128
radix_width = 8


def phase_tables(row_count, col_count, length, direction):
    phase_index = (
        lax.iota(jnp.int32, row_count)[:, None] * lax.iota(jnp.int32, col_count)[None, :] % length
    )
    angles = direction * 2.0 * math.pi / length * phase_index.astype(jnp.float32)
    return (jnp.cos(angles), jnp.sin(angles))


def last_axis(operand, matrix):
    return jnp.einsum("...n,nk->...k", operand, matrix, precision=lax.Precision.HIGH)


def first_axis(operand, matrix):
    return jnp.einsum("...ab,ak->...kb", operand, matrix, precision=lax.Precision.HIGH)


def transform(real_part, imag_part, direction):
    length = real_part.shape[-1]
    if length <= inner_length or length % radix_width != 0:
        cos_table, sin_table = phase_tables(length, length, length, direction)
        return (
            last_axis(real_part, cos_table) - last_axis(imag_part, sin_table),
            last_axis(real_part, sin_table) + last_axis(imag_part, cos_table),
        )
    rest_length = length // radix_width
    grid_shape = real_part.shape[:-1] + (radix_width, rest_length)
    real_grid = real_part.reshape(grid_shape)
    imag_grid = imag_part.reshape(grid_shape)
    cos_table, sin_table = phase_tables(radix_width, radix_width, radix_width, direction)
    section_real = first_axis(real_grid, cos_table) - first_axis(imag_grid, sin_table)
    section_imag = first_axis(real_grid, sin_table) + first_axis(imag_grid, cos_table)
    twist_cos, twist_sin = phase_tables(radix_width, rest_length, length, direction)
    turned_real = section_real * twist_cos - section_imag * twist_sin
    turned_imag = section_real * twist_sin + section_imag * twist_cos
    inner_real, inner_imag = transform(turned_real, turned_imag, direction)
    return (
        jnp.swapaxes(inner_real, -1, -2).reshape(real_part.shape),
        jnp.swapaxes(inner_imag, -1, -2).reshape(real_part.shape),
    )


def spectral(mixed_term, gated_grad, kernel, local_gain):
    length = mixed_term.shape[-1]
    mixed_wide = mixed_term.astype(jnp.float32)
    gated_wide = gated_grad.astype(jnp.float32)
    kernel_wide = kernel.astype(jnp.float32)
    extend = ((0, 0), (0, length))
    real_in = jnp.stack([jnp.pad(mixed_wide, extend), jnp.pad(kernel_wide, extend)])
    imag_in = jnp.stack(
        [jnp.pad(gated_wide, extend), jnp.zeros((kernel_wide.shape[0], 2 * length), jnp.float32)]
    )
    freq_real, freq_imag = transform(real_in, imag_in, -1.0)
    packed_real = freq_real[0]
    packed_imag = freq_imag[0]
    mirror_real = jnp.roll(jnp.flip(packed_real, -1), 1, -1)
    mirror_imag = jnp.roll(jnp.flip(packed_imag, -1), 1, -1)
    mix_real = 0.5 * (packed_real + mirror_real)
    mix_imag = 0.5 * (packed_imag - mirror_imag)
    grad_real = 0.5 * (packed_imag + mirror_imag)
    grad_imag = 0.5 * (mirror_real - packed_real)
    kern_real = freq_real[1]
    kern_imag = freq_imag[1]
    conv_real = mix_real * kern_real - mix_imag * kern_imag
    conv_imag = mix_real * kern_imag + mix_imag * kern_real
    corr_real = grad_real * kern_real + grad_imag * kern_imag
    corr_imag = grad_imag * kern_real - grad_real * kern_imag
    cross_real = grad_real * mix_real + grad_imag * mix_imag
    cross_imag = grad_imag * mix_real - grad_real * mix_imag
    back_real = jnp.stack([conv_real - corr_imag, cross_real])
    back_imag = jnp.stack([conv_imag + corr_real, cross_imag])
    time_real, time_imag = transform(back_real, back_imag, 1.0)
    inverse_scale = 1.0 / (2 * length)
    conv_part = time_real[0, :, :length] * inverse_scale
    corr_part = time_imag[0, :, :length] * inverse_scale
    cross_part = time_real[1, :, :length] * inverse_scale
    gain_column = local_gain[:, None]
    long_out = (conv_part + gain_column * mixed_wide).astype(jnp.bfloat16)
    mixed_grad = (corr_part + gain_column * gated_wide).astype(jnp.bfloat16)
    return (long_out, mixed_grad, cross_part.astype(jnp.bfloat16))


def featurize(history, weights, margin, span_count):
    running = weights[:, :, 0:1] * history[:, :, margin : margin + span_count]
    for offset in range(1, margin + 1):
        running = (
            running
            + weights[:, :, offset : offset + 1]
            * history[:, :, margin - offset : margin - offset + span_count]
        )
    return running


def unfeaturize(padded_grad, weights, span_count):
    running = weights[:, :, 0:1] * padded_grad[:, :, 0:span_count]
    for offset in range(1, weights.shape[2]):
        running = (
            running
            + weights[:, :, offset : offset + 1] * padded_grad[:, :, offset : offset + span_count]
        )
    return running


def tap_grads(primed_grad, history, margin, span_count):
    columns = []
    for offset in range(margin + 1):
        columns.append(
            jnp.sum(
                primed_grad * history[:, :, margin - offset : margin - offset + span_count], axis=-1
            )
        )
    return jnp.stack(columns, axis=-1)


def packed_tables(length):
    steps = np.arange(length)
    phase = (steps[:, None] * steps[None, :]) % (2 * length)
    angles = np.pi / length * phase
    sines = np.sin(angles)
    sines[:, 0] = 1.0 - 2.0 * (steps % 2)
    table = np.concatenate([np.cos(angles), sines], 1)
    weights = np.full(2 * length, 1.0 / length)
    weights[0] = weights[length] = 0.5 / length
    split = []
    for exact in (table.T, table * weights):
        exact = exact.astype(np.float32)
        high = exact.astype(jnp.bfloat16)
        low = (exact - high.astype(np.float32)).astype(jnp.bfloat16)
        split.append(np.stack([high, low]))
    return split


def fused_kernel(
    sizes,
    feat_hbm,
    cot_hbm,
    filt_hbm,
    short_hbm,
    gain_hbm,
    fwd_hbm,
    back_hbm,
    gated_out,
    grad_out,
    long_out,
    sums_out,
    raw,
    short,
    gain_line,
    fwd,
    back,
    hist,
    cot,
    primed,
    moving,
    halo_out,
    halo_in,
    edge_out,
    edge_in,
    gate_out,
    mix_out,
    filt_in,
    gate_in,
    mix_in,
    tokens,
    freq,
    pair,
    res_grad,
    res_out,
    res_long,
    got_grad,
    got_out,
    load_sem,
    send_sem,
    recv_sem,
):
    groups, rows, span, length, taps = sizes
    me = lax.axis_index("seq")
    peers = range(1, groups)
    edge = 16
    FILT, GATE, MIX, GRAD, OUT, LONG, PART_A, PART_B, HALO, EDGE = range(10)

    def near(step):
        return lax.rem(me + step, groups)

    def block(index, extent, count=1):
        return pl.ds(pl.multiple_of(index * extent, extent), extent * count)

    def lanes(step):
        return block(near(step), rows)

    barrier = pltpu.get_barrier_semaphore()
    for step in peers:
        pl.semaphore_signal(
            barrier,
            inc=1,
            device_id={"seq": near(step)},
            device_id_type=pl.DeviceIdType.MESH,
        )
    pairs = [
        (feat_hbm, raw.at[0:3]),
        (cot_hbm, raw.at[3]),
        (short_hbm, short),
        (gain_hbm, gain_line),
        (filt_hbm.at[lanes(0), :], filt_in.at[0]),
        (fwd_hbm, fwd),
        (back_hbm, back),
    ]
    loads = [
        pltpu.make_async_copy(source, target, load_sem.at[index])
        for index, (source, target) in enumerate(pairs)
    ]
    for load in loads:
        load.start()

    def remote(source, target, kind, peer):
        return pltpu.make_async_remote_copy(
            src_ref=source,
            dst_ref=target,
            send_sem=send_sem.at[kind],
            recv_sem=recv_sem.at[kind],
            device_id={"seq": peer},
            device_id_type=pl.DeviceIdType.MESH,
        )

    def push(kind, source_of, target):
        for step in peers:
            remote(source_of(step), target.at[groups - step], kind, near(step)).start()

    def whole(kind, target):
        landed = target.at[1:groups]
        return remote(landed, landed, kind, near(1))

    pl.semaphore_wait(barrier, groups - 1)
    push(FILT, lambda step: filt_hbm.at[lanes(step), :], filt_in)

    loads[2].wait()
    loads[0].wait()

    halo_out[...] = jnp.zeros_like(halo_out)
    edge_out[...] = jnp.zeros_like(edge_out)
    for step in range(groups):
        for stream in range(3):
            wide = raw[stream, lanes(step), :].T.astype(jnp.float32)
            hist[step, stream, 8:, :] = wide
            halo_out[near(step), 2 * stream : 2 * stream + 2, :] = wide[span - 2 :, :]

    right, left = near(1), near(groups - 1)

    @pl.when(me < groups - 1)
    def _():
        remote(halo_out, halo_in, HALO, right).start()

    loads[1].wait()
    for step in range(groups):
        cot[step, :span, :] = raw[3, lanes(step), :].T.astype(jnp.float32)

    def coef(stream, offset, step):
        return short[stream, offset : offset + 1, lanes(step)]

    def featurize(step, stream, first, count):
        running = coef(stream, 0, step) * hist[step, stream, 8 + first : 8 + first + count, :]
        for offset in range(1, taps):
            start = 8 + first - offset
            running = (
                running
                + coef(stream, offset, step) * hist[step, stream, start : start + count, :]
            )
        primed[step, stream, first : first + count, :] = running
        return running

    def gate(step, first, count):
        value = featurize(step, 0, first, count) * cot[step, first : first + count, :]
        gate_out[step, first : first + count, :] = value.astype(jnp.bfloat16)

    def mix(step, first, count):
        value = featurize(step, 1, first, count) * featurize(step, 2, first, count)
        mix_out[step, first : first + count, :] = value.astype(jnp.bfloat16)

    for step in range(groups):
        gate(step, edge, span - edge)
    for step in range(groups):
        mix(step, edge, span - edge)

    @pl.when(me > 0)
    def _():
        remote(halo_in, halo_in, HALO, left).wait_recv()

    @pl.when(me == 0)
    def _():
        halo_in[...] = jnp.zeros_like(halo_in)

    for step in range(groups):
        for stream in range(3):
            hist[step, stream, 6:8, :] = halo_in[near(step), 2 * stream : 2 * stream + 2, :]
        gate(step, 0, edge)
    push(GATE, lambda step: gate_out.at[step], gate_in)
    for step in range(groups):
        mix(step, 0, edge)
    push(MIX, lambda step: mix_out.at[step], mix_in)
    for step in range(groups):
        edge_out[near(step), 0:2, :] = primed[step, 1, 0:2, :]
        edge_out[near(step), 2:4, :] = primed[step, 2, 0:2, :]
        edge_out[near(step), 4:6, :] = cot[step, 0:2, :]

    @pl.when(me > 0)
    def _():
        remote(edge_out, edge_in, EDGE, left).start()

    gate_in[0] = gate_out[0]
    mix_in[0] = mix_out[0]
    res_grad[length:, :] = jnp.zeros((edge, rows), jnp.bfloat16)
    res_out[length:, :] = jnp.zeros((edge, rows), jnp.bfloat16)
    sums_out[0, 0] = jnp.zeros(sums_out.shape[2:], jnp.float32)
    sums_out[1, 0] = jnp.zeros(sums_out.shape[2:], jnp.float32)
    for step in range(groups):
        local = gate_out[step].astype(jnp.float32) * mix_out[step].astype(jnp.float32)
        sums_out[0, 0, near(step), 2 * taps : 2 * taps + 1, :] = jnp.sum(
            local, axis=0, keepdims=True
        )

    tile = 512

    def forward(kind):
        @pl.loop(0, 2 * length // tile)
        def _(part):
            picked = block(part, tile)
            total = jnp.dot(fwd[0, picked, :], tokens[kind], preferred_element_type=jnp.float32)
            total += jnp.dot(fwd[1, picked, :], tokens[kind], preferred_element_type=jnp.float32)
            freq[kind, picked, :] = total

    def product(left_kind, right_kind, sign):
        strip = 128
        for start in range(0, length, strip):
            even_rows = slice(start, start + strip)
            odd_rows = slice(length + start, length + start + strip)
            left_c, left_s = freq[left_kind, even_rows, :], freq[left_kind, odd_rows, :]
            right_c, right_s = freq[right_kind, even_rows, :], freq[right_kind, odd_rows, :]
            both = left_s * right_s
            cross = left_s * right_c - sign * (left_c * right_s)
            if start == 0:
                first = lax.broadcasted_iota(jnp.int32, (strip, rows), 0) == 0
                even = left_c * right_c + sign * jnp.where(first, 0.0, both)
                odd = jnp.where(first, both, cross)
            else:
                even = left_c * right_c + sign * both
                odd = cross
            for value, placed in ((even, even_rows), (odd, odd_rows)):
                high = value.astype(jnp.bfloat16)
                low = (value - high.astype(jnp.float32)).astype(jnp.bfloat16)
                pair[placed, :rows] = high
                pair[placed, rows:] = low

    def inverse():
        both = jnp.dot(back[0], pair[...], preferred_element_type=jnp.float32)
        total = both[:, :rows] + both[:, rows:]
        total += jnp.dot(back[1], pair[:, :rows], preferred_element_type=jnp.float32)
        return total

    gates, mixes, kernels = range(3)

    loads[3].wait()
    loads[4].wait()
    loads[5].wait()
    gain = gain_line[:, lanes(0)]

    whole(FILT, filt_in).wait_recv()
    for step in range(groups):
        tokens[kernels, block(near(step), span), :] = filt_in[step].T
    forward(kernels)

    whole(GATE, gate_in).wait_recv()
    for step in range(groups):
        tokens[gates, block(near(step), span), :] = gate_in[step]
    forward(gates)
    product(gates, kernels, 1.0)
    loads[6].wait()
    res_grad[:length, :] = (inverse() + gain * tokens[gates].astype(jnp.float32)).astype(
        jnp.bfloat16
    )

    def spread(kind, result, target, extent):
        def taken(step):
            return pl.ds(pl.multiple_of(near(step) * span, span), extent)

        push(kind, lambda step: result.at[taken(step), :], target)
        target[0] = result[taken(0), :]

    spread(GRAD, res_grad, got_grad, span + edge)

    whole(MIX, mix_in).wait_recv()
    for step in range(groups):
        tokens[mixes, block(near(step), span), :] = mix_in[step]
    forward(mixes)
    product(mixes, kernels, -1.0)
    res_out[:length, :] = (inverse() + gain * tokens[mixes].astype(jnp.float32)).astype(
        jnp.bfloat16
    )
    spread(OUT, res_out, got_out, span + edge)

    product(gates, mixes, 1.0)
    res_long[...] = inverse().astype(jnp.bfloat16)
    spread(LONG, res_long, long_out, span)

    @pl.when(me < groups - 1)
    def _():
        remote(edge_in, edge_in, EDGE, right).wait_recv()

    @pl.when(me == groups - 1)
    def _():
        edge_in[...] = jnp.zeros_like(edge_in)

    for step in range(groups):
        primed[step, 1, span : span + 2, :] = edge_in[near(step), 0:2, :]
        primed[step, 2, span : span + 2, :] = edge_in[near(step), 2:4, :]
        cot[step, span : span + 2, :] = edge_in[near(step), 4:6, :]

    def settle_stream(step, stream, value, part, row):
        moving[...] = value
        running = coef(stream, 0, step) * moving[0:span, :]
        for offset in range(1, taps):
            running = running + coef(stream, offset, step) * moving[offset : offset + span, :]
        grad_out[stream, step] = running.astype(jnp.bfloat16)
        for offset in range(taps):
            start = 8 - offset
            total = jnp.sum(
                moving[0:span, :] * hist[step, stream, start : start + span, :],
                axis=0,
                keepdims=True,
            )
            sums_out[part, 0, near(step), row + offset : row + offset + 1, :] = total

    reach = span + 8
    whole(GRAD, got_grad).wait_recv()
    for step in range(groups):
        mixed_back = got_grad[step].astype(jnp.float32)[:reach, :]
        settle_stream(step, 1, mixed_back * primed[step, 2, :, :], 0, 0)
        settle_stream(step, 2, mixed_back * primed[step, 1, :, :], 0, taps)
    push(PART_A, lambda step: sums_out.at[0, 0], sums_out.at[0])

    whole(OUT, got_out).wait_recv()
    for step in range(groups):
        long_wide = got_out[step].astype(jnp.float32)[:reach, :]
        settle_stream(step, 0, long_wide * cot[step], 1, 0)
    push(PART_B, lambda step: sums_out.at[1, 0], sums_out.at[1])
    for step in range(groups):
        gated_out[step] = (
            primed[step, 0, :span, :] * got_out[step, :span, :].astype(jnp.float32)
        ).astype(jnp.bfloat16)

    whole(LONG, long_out).wait_recv()
    whole(PART_A, sums_out.at[0]).wait_recv()
    whole(PART_B, sums_out.at[1]).wait_recv()

    @pl.when(me < groups - 1)
    def _():
        remote(halo_out, halo_in, HALO, right).wait_send()

    @pl.when(me > 0)
    def _():
        remote(edge_out, edge_in, EDGE, left).wait_send()

    for kind, target in (
        (FILT, filt_in),
        (GATE, gate_in),
        (MIX, mix_in),
        (GRAD, got_grad),
        (OUT, got_out),
        (LONG, long_out),
        (PART_A, sums_out.at[0]),
        (PART_B, sums_out.at[1]),
    ):
        whole(kind, target).wait_send()


def settle_kernel(
    sizes, gated, grad, long, sums, gated_hbm, grad_hbm, long_hbm, taps_hbm, skip_hbm,
    wide, taps_line, skip_line, done,
):
    groups, rows, span, taps = sizes
    me = lax.axis_index("seq")
    copies = []

    def start(source, target):
        copy = pltpu.make_async_copy(source, target, done.at[len(copies)])
        copy.start()
        copies.append(copy)

    def turn(slot, source):
        for step in range(groups):
            owner = lax.rem(me + step, groups)
            picked = pl.ds(pl.multiple_of(owner * rows, rows), rows)
            wide[slot, picked, :] = source[step].T

    for stream in range(3):
        turn(stream, grad.at[stream])
    start(wide.at[0:3], grad_hbm)
    turn(3, gated)
    start(wide.at[3], gated_hbm)
    turn(4, long)
    start(wide.at[4], long_hbm)
    for group in range(groups):
        picked = slice(group * rows, (group + 1) * rows)
        totals = []
        for part in range(2):
            total = None
            for source in range(groups):
                slot = lax.rem(source + groups - me, groups)
                value = sums[part, slot, group]
                total = value if total is None else total + value
            totals.append(total)
        taps_line[0, :, picked] = totals[1][:taps]
        taps_line[1, :, picked] = totals[0][:taps]
        taps_line[2, :, picked] = totals[0][taps : 2 * taps]
        skip_line[:, picked] = totals[0][2 * taps : 2 * taps + 1]
    start(taps_line, taps_hbm)
    start(skip_line, skip_hbm)
    for copy in copies:
        copy.wait()


def fused(features, cotangent, long_filter, short_filters, skip_gain, groups):
    channels, span = cotangent.shape
    rows = channels // groups
    length = span * groups
    taps = short_filters.shape[2]
    hbm = pl.BlockSpec(memory_space=pltpu.HBM)
    vmem = pl.BlockSpec(memory_space=pltpu.VMEM)
    dma = pltpu.SemaphoreType.DMA
    narrow, wide = jnp.bfloat16, jnp.float32
    kinds = 10
    forward_table, back_table = packed_tables(length)
    middle = pl.pallas_call(
        functools.partial(fused_kernel, (groups, rows, span, length, taps)),
        out_shape=(
            pltpu.VMEM((groups, span, rows), narrow),
            pltpu.VMEM((3, groups, span, rows), narrow),
            pltpu.VMEM((groups, span, rows), narrow),
            pltpu.VMEM((2, groups, groups, 8, rows), wide),
        ),
        in_specs=[hbm] * 7,
        out_specs=(vmem,) * 4,
        scratch_shapes=[
            pltpu.VMEM((4, channels, span), narrow),
            pltpu.VMEM((3, taps, channels), wide),
            pltpu.VMEM((1, channels), wide),
            pltpu.VMEM((2, 2 * length, length), narrow),
            pltpu.VMEM((2, length, 2 * length), narrow),
            pltpu.VMEM((groups, 3, span + 8, rows), wide),
            pltpu.VMEM((groups, span + 8, rows), wide),
            pltpu.VMEM((groups, 3, span + 8, rows), wide),
            pltpu.VMEM((span + 8, rows), wide),
            pltpu.VMEM((groups, 8, rows), wide),
            pltpu.VMEM((groups, 8, rows), wide),
            pltpu.VMEM((groups, 8, rows), wide),
            pltpu.VMEM((groups, 8, rows), wide),
            pltpu.VMEM((groups, span, rows), narrow),
            pltpu.VMEM((groups, span, rows), narrow),
            pltpu.VMEM((groups, rows, span), narrow),
            pltpu.VMEM((groups, span, rows), narrow),
            pltpu.VMEM((groups, span, rows), narrow),
            pltpu.VMEM((3, length, rows), narrow),
            pltpu.VMEM((3, 2 * length, rows), wide),
            pltpu.VMEM((2 * length, 2 * rows), narrow),
            pltpu.VMEM((length + 16, rows), narrow),
            pltpu.VMEM((length + 16, rows), narrow),
            pltpu.VMEM((length, rows), narrow),
            pltpu.VMEM((groups, span + 16, rows), narrow),
            pltpu.VMEM((groups, span + 16, rows), narrow),
            dma((7,)),
            dma((kinds,)),
            dma((kinds,)),
        ],
        compiler_params=pltpu.CompilerParams(
            collective_id=0, has_side_effects=True, vmem_limit_bytes=40 * 2**20
        ),
    )(
        *[
            pltpu.with_memory_space_constraint(value, pltpu.HBM)
            for value in (
                features,
                cotangent,
                long_filter,
                jnp.swapaxes(short_filters, 1, 2),
                skip_gain[None],
                jnp.asarray(forward_table),
                jnp.asarray(back_table),
            )
        ]
    )
    gated_out, feature_grad, long_grad, taps_grad, gain_grad = pl.pallas_call(
        functools.partial(settle_kernel, (groups, rows, span, taps)),
        out_shape=(
            jax.ShapeDtypeStruct((channels, span), narrow),
            jax.ShapeDtypeStruct((3, channels, span), narrow),
            jax.ShapeDtypeStruct((channels, span), narrow),
            jax.ShapeDtypeStruct((3, taps, channels), wide),
            jax.ShapeDtypeStruct((1, channels), wide),
        ),
        in_specs=[vmem] * 4,
        out_specs=(hbm,) * 5,
        scratch_shapes=[
            pltpu.VMEM((5, channels, span), narrow),
            pltpu.VMEM((3, taps, channels), wide),
            pltpu.VMEM((1, channels), wide),
            dma((5,)),
        ],
    )(*[pltpu.with_memory_space_constraint(value, pltpu.VMEM) for value in middle])
    return gated_out, feature_grad, long_grad, jnp.swapaxes(taps_grad, 1, 2), gain_grad[0]


def dense_fits(features, short_filters, groups):
    channels, span = features.shape[1:]
    rows, length = channels // groups, span * groups
    return (
        channels % groups == 0
        and rows == 128
        and span == 128
        and length % 512 == 0
        and length <= 1024
        and 2 <= short_filters.shape[2] <= 3
    )


def shards(features, cotangent, long_filter, short_filters, skip_gain):
    groups = lax.axis_size("seq")
    if dense_fits(features, short_filters, groups):
        return fused(features, cotangent, long_filter, short_filters, skip_gain, groups)
    seq_index = lax.axis_index("seq")
    channels = features.shape[1]
    per_group = channels // groups
    margin = short_filters.shape[2] - 1
    local_gain = lax.dynamic_slice_in_dim(skip_gain, seq_index * per_group, per_group, 0)
    stacked = jnp.concatenate([features, cotangent[None], long_filter[None]], 0)
    columns = lax.all_to_all(stacked, "seq", split_axis=1, concat_axis=2, tiled=True)
    weights = lax.dynamic_slice_in_dim(short_filters, seq_index * per_group, per_group, 1)
    length = columns.shape[2]
    history = jnp.pad(columns[:3].astype(jnp.float32), ((0, 0), (0, 0), (margin, 0)))
    primed = featurize(history, weights, margin, length)
    mixed_term = (primed[1] * primed[2]).astype(jnp.bfloat16)
    cot_wide = columns[3].astype(jnp.float32)
    gated_grad = (cot_wide * primed[0]).astype(jnp.bfloat16)
    long_out, mixed_grad, kernel_grad = spectral(mixed_term, gated_grad, columns[4], local_gain)
    long_wide = long_out.astype(jnp.float32)
    mixed_back = mixed_grad.astype(jnp.float32)
    gated_out = (primed[0] * long_wide).astype(jnp.bfloat16)
    primed_grad = jnp.stack([cot_wide * long_wide, mixed_back * primed[2], mixed_back * primed[1]])
    padded_grad = jnp.pad(primed_grad, ((0, 0), (0, 0), (0, margin)))
    feature_grad = unfeaturize(padded_grad, weights, length).astype(jnp.bfloat16)
    taps_grad = tap_grads(primed_grad, history, margin, length)
    gain_grad = jnp.sum(gated_grad.astype(jnp.float32) * mixed_term.astype(jnp.float32), axis=-1)
    results = jnp.concatenate([gated_out[None], feature_grad, kernel_grad[None]], 0)
    row_blocks = lax.all_to_all(results, "seq", split_axis=2, concat_axis=1, tiled=True)
    short_grad, skip_grad = (
        lax.all_gather(taps_grad, "seq", axis=1, tiled=True),
        lax.all_gather(gain_grad, "seq", axis=0, tiled=True),
    )
    return (row_blocks[0], row_blocks[1:4], row_blocks[4], short_grad, skip_grad)


def solution(mesh):
    placed = (
        P(None, "chan", "seq"),
        P("chan", "seq"),
        P("chan", "seq"),
        P(None, "chan", None),
        P("chan"),
    )
    return jax.shard_map(
        shards,
        mesh=mesh,
        in_specs=placed,
        out_specs=(
            P("chan", "seq"),
            P(None, "chan", "seq"),
            P("chan", "seq"),
            P(None, "chan", None),
            P("chan"),
        ),
        check_vma=False,
    )
```

```python
import functools
import math

import jax
import jax.numpy as jnp
import numpy as np
from jax import lax
from jax.experimental import pallas as pl
from jax.experimental.pallas import tpu as pltpu
from jax.sharding import PartitionSpec as P

inner_length = 128
radix_width = 8


def phase_tables(row_count, col_count, length, direction):
    phase_index = (
        lax.iota(jnp.int32, row_count)[:, None] * lax.iota(jnp.int32, col_count)[None, :] % length
    )
    angles = direction * 2.0 * math.pi / length * phase_index.astype(jnp.float32)
    return (jnp.cos(angles), jnp.sin(angles))


def last_axis(operand, matrix):
    return jnp.einsum("...n,nk->...k", operand, matrix, precision=lax.Precision.HIGH)


def first_axis(operand, matrix):
    return jnp.einsum("...ab,ak->...kb", operand, matrix, precision=lax.Precision.HIGH)


def transform(real_part, imag_part, direction):
    length = real_part.shape[-1]
    if length <= inner_length or length % radix_width != 0:
        cos_table, sin_table = phase_tables(length, length, length, direction)
        return (
            last_axis(real_part, cos_table) - last_axis(imag_part, sin_table),
            last_axis(real_part, sin_table) + last_axis(imag_part, cos_table),
        )
    rest_length = length // radix_width
    grid_shape = real_part.shape[:-1] + (radix_width, rest_length)
    real_grid = real_part.reshape(grid_shape)
    imag_grid = imag_part.reshape(grid_shape)
    cos_table, sin_table = phase_tables(radix_width, radix_width, radix_width, direction)
    section_real = first_axis(real_grid, cos_table) - first_axis(imag_grid, sin_table)
    section_imag = first_axis(real_grid, sin_table) + first_axis(imag_grid, cos_table)
    twist_cos, twist_sin = phase_tables(radix_width, rest_length, length, direction)
    turned_real = section_real * twist_cos - section_imag * twist_sin
    turned_imag = section_real * twist_sin + section_imag * twist_cos
    inner_real, inner_imag = transform(turned_real, turned_imag, direction)
    return (
        jnp.swapaxes(inner_real, -1, -2).reshape(real_part.shape),
        jnp.swapaxes(inner_imag, -1, -2).reshape(real_part.shape),
    )


def spectral(mixed_term, gated_grad, kernel, local_gain):
    length = mixed_term.shape[-1]
    mixed_wide = mixed_term.astype(jnp.float32)
    gated_wide = gated_grad.astype(jnp.float32)
    kernel_wide = kernel.astype(jnp.float32)
    extend = ((0, 0), (0, length))
    real_in = jnp.stack([jnp.pad(mixed_wide, extend), jnp.pad(kernel_wide, extend)])
    imag_in = jnp.stack(
        [jnp.pad(gated_wide, extend), jnp.zeros((kernel_wide.shape[0], 2 * length), jnp.float32)]
    )
    freq_real, freq_imag = transform(real_in, imag_in, -1.0)
    packed_real = freq_real[0]
    packed_imag = freq_imag[0]
    mirror_real = jnp.roll(jnp.flip(packed_real, -1), 1, -1)
    mirror_imag = jnp.roll(jnp.flip(packed_imag, -1), 1, -1)
    mix_real = 0.5 * (packed_real + mirror_real)
    mix_imag = 0.5 * (packed_imag - mirror_imag)
    grad_real = 0.5 * (packed_imag + mirror_imag)
    grad_imag = 0.5 * (mirror_real - packed_real)
    kern_real = freq_real[1]
    kern_imag = freq_imag[1]
    conv_real = mix_real * kern_real - mix_imag * kern_imag
    conv_imag = mix_real * kern_imag + mix_imag * kern_real
    corr_real = grad_real * kern_real + grad_imag * kern_imag
    corr_imag = grad_imag * kern_real - grad_real * kern_imag
    cross_real = grad_real * mix_real + grad_imag * mix_imag
    cross_imag = grad_imag * mix_real - grad_real * mix_imag
    back_real = jnp.stack([conv_real - corr_imag, cross_real])
    back_imag = jnp.stack([conv_imag + corr_real, cross_imag])
    time_real, time_imag = transform(back_real, back_imag, 1.0)
    inverse_scale = 1.0 / (2 * length)
    conv_part = time_real[0, :, :length] * inverse_scale
    corr_part = time_imag[0, :, :length] * inverse_scale
    cross_part = time_real[1, :, :length] * inverse_scale
    gain_column = local_gain[:, None]
    long_out = (conv_part + gain_column * mixed_wide).astype(jnp.bfloat16)
    mixed_grad = (corr_part + gain_column * gated_wide).astype(jnp.bfloat16)
    return (long_out, mixed_grad, cross_part.astype(jnp.bfloat16))


def featurize(history, weights, margin, span_count):
    running = weights[:, :, 0:1] * history[:, :, margin : margin + span_count]
    for offset in range(1, margin + 1):
        running = (
            running
            + weights[:, :, offset : offset + 1]
            * history[:, :, margin - offset : margin - offset + span_count]
        )
    return running


def unfeaturize(padded_grad, weights, span_count):
    running = weights[:, :, 0:1] * padded_grad[:, :, 0:span_count]
    for offset in range(1, weights.shape[2]):
        running = (
            running
            + weights[:, :, offset : offset + 1] * padded_grad[:, :, offset : offset + span_count]
        )
    return running


def tap_grads(primed_grad, history, margin, span_count):
    columns = []
    for offset in range(margin + 1):
        columns.append(
            jnp.sum(
                primed_grad * history[:, :, margin - offset : margin - offset + span_count], axis=-1
            )
        )
    return jnp.stack(columns, axis=-1)


def packed_tables(length):
    half, quarter = length // 2, length // 4
    steps = np.arange(half)
    bins = np.arange(length).reshape(quarter, 4).T.reshape(-1)
    phase = (steps[:, None] * bins[None, :]) % (2 * length)
    angles = np.pi / length * phase
    sines = np.sin(angles)
    sines[:, 0] = 1.0 - 2.0 * (steps % 2)
    table = np.concatenate([np.cos(angles), sines], 1)
    weights = np.full(2 * length, 1.0 / length)
    weights[0] = weights[length] = 0.5 / length
    split = []
    for exact in (table.T, table * weights):
        exact = exact.astype(np.float32)
        high = exact.astype(jnp.bfloat16)
        low = (exact - high.astype(np.float32)).astype(jnp.bfloat16)
        split.append((high, low))
    return np.concatenate(split[0], 1), np.stack(split[1])


def fused_kernel(
    sizes,
    feat_hbm,
    cot_hbm,
    filt_hbm,
    short_hbm,
    gain_hbm,
    fwd_hbm,
    back_hbm,
    gated_out,
    grad_out,
    long_out,
    chip_sums,
    late_sums,
    raw,
    short,
    gain_line,
    fwd,
    back,
    hist,
    cot,
    primed,
    moving,
    halo_out,
    halo_in,
    edge_out,
    edge_in,
    gate_out,
    mix_out,
    filt_in,
    gate_in,
    mix_in,
    tokens,
    freq,
    pair,
    res_grad,
    res_out,
    res_long,
    got_grad,
    got_out,
    own_sums,
    mate_sums,
    load_sem,
    send_sem,
    recv_sem,
):
    groups, rows, span, length, taps = sizes
    me = lax.axis_index("seq")
    peers = range(1, groups)
    edge = 16
    FILT, GATE, MIX, GRAD, OUT, LONG, MATE, CHIP, LATE, HALO, EDGE = range(11)
    half, quarter = length // 2, length // 4
    half_groups, twins = groups // 2, groups // 2
    mate = me + 1 - 2 * lax.rem(me, 2)

    def near(step):
        return lax.rem(me + step, groups)

    def block(index, extent, count=1):
        return pl.ds(pl.multiple_of(index * extent, extent), extent * count)

    def lanes(step):
        return block(near(step), rows)

    barrier = pltpu.get_barrier_semaphore()
    for step in peers:
        pl.semaphore_signal(
            barrier,
            inc=1,
            device_id={"seq": near(step)},
            device_id_type=pl.DeviceIdType.MESH,
        )
    pairs = [
        (feat_hbm, raw.at[0:3]),
        (cot_hbm, raw.at[3]),
        (short_hbm, short),
        (gain_hbm, gain_line),
        (filt_hbm.at[lanes(0), :], filt_in.at[0]),
        (fwd_hbm, fwd),
        (back_hbm, back),
    ]
    loads = [
        pltpu.make_async_copy(source, target, load_sem.at[index])
        for index, (source, target) in enumerate(pairs)
    ]
    for index in (2, 0, 1):
        loads[index].start()

    def remote(source, target, kind, peer):
        return pltpu.make_async_remote_copy(
            src_ref=source,
            dst_ref=target,
            send_sem=send_sem.at[kind],
            recv_sem=recv_sem.at[kind],
            device_id={"seq": peer},
            device_id_type=pl.DeviceIdType.MESH,
        )

    def push(kind, source_of, target_of):
        for step in peers:
            remote(source_of(step), target_of(groups - step), kind, near(step)).start()

    def push_rows(kind, source, target, first, count):
        picked = pl.ds(first, count)
        push(
            kind,
            lambda step: source.at[step, picked, :],
            lambda slot: target.at[slot, picked, :],
        )

    def whole(kind, target):
        landed = target.at[1:groups]
        return remote(landed, landed, kind, near(1))

    loads[2].wait()
    loads[0].wait()

    halo_out[...] = jnp.zeros_like(halo_out)
    edge_out[...] = jnp.zeros_like(edge_out)
    for step in range(groups):
        for stream in range(3):
            wide = raw[stream, lanes(step), :].T.astype(jnp.float32)
            hist[step, stream, 8:, :] = wide
            halo_out[near(step), 2 * stream : 2 * stream + 2, :] = wide[span - 2 :, :]

    right, left = near(1), near(groups - 1)

    pl.semaphore_wait(barrier, groups - 1)
    @pl.when(me < groups - 1)
    def _():
        remote(halo_out, halo_in, HALO, right).start()

    push(FILT, lambda step: filt_hbm.at[lanes(step), :], lambda slot: filt_in.at[slot])
    for index in (3, 4, 5, 6):
        loads[index].start()

    loads[1].wait()
    for step in range(groups):
        cot[step, :span, :] = raw[3, lanes(step), :].T.astype(jnp.float32)

    def coef(stream, offset, step):
        return short[stream, offset : offset + 1, lanes(step)]

    def featurize(step, stream, first, count):
        running = coef(stream, 0, step) * hist[step, stream, 8 + first : 8 + first + count, :]
        for offset in range(1, taps):
            start = 8 + first - offset
            running = (
                running
                + coef(stream, offset, step) * hist[step, stream, start : start + count, :]
            )
        primed[step, stream, first : first + count, :] = running
        return running

    def gate(step, first, count):
        value = featurize(step, 0, first, count) * cot[step, first : first + count, :]
        gate_out[step, first : first + count, :] = value.astype(jnp.bfloat16)

    def mix(step, first, count):
        value = featurize(step, 1, first, count) * featurize(step, 2, first, count)
        mix_out[step, first : first + count, :] = value.astype(jnp.bfloat16)

    for step in range(groups):
        gate(step, edge, span - edge)
    push_rows(GATE, gate_out, gate_in, edge, span - edge)
    for step in range(groups):
        mix(step, edge, span - edge)

    @pl.when(me > 0)
    def _():
        remote(halo_in, halo_in, HALO, left).wait_recv()

    @pl.when(me == 0)
    def _():
        halo_in[...] = jnp.zeros_like(halo_in)

    for step in range(groups):
        for stream in range(3):
            hist[step, stream, 6:8, :] = halo_in[near(step), 2 * stream : 2 * stream + 2, :]
        gate(step, 0, edge)
    push_rows(GATE, gate_out, gate_in, 0, edge)
    for step in range(groups):
        mix(step, 0, edge)
    whole(GATE, gate_in).wait_send()
    push_rows(MIX, mix_out, mix_in, 0, span)
    for step in range(groups):
        edge_out[near(step), 0:2, :] = primed[step, 1, 0:2, :]
        edge_out[near(step), 2:4, :] = primed[step, 2, 0:2, :]
        edge_out[near(step), 4:6, :] = cot[step, 0:2, :]

    @pl.when(me > 0)
    def _():
        remote(edge_out, edge_in, EDGE, left).start()

    gate_in[0] = gate_out[0]
    mix_in[0] = mix_out[0]
    res_grad[length:, :] = jnp.zeros((edge, rows), jnp.bfloat16)
    res_out[length:, :] = jnp.zeros((edge, rows), jnp.bfloat16)
    own_sums[...] = jnp.zeros_like(own_sums)
    late_sums[0] = jnp.zeros(late_sums.shape[1:], jnp.float32)
    for step in range(groups):
        local = gate_out[step].astype(jnp.float32) * mix_out[step].astype(jnp.float32)
        own_sums[near(step), 2 * taps : 2 * taps + 1, :] = jnp.sum(local, axis=0, keepdims=True)

    def place(kind, step, value):
        position = near(step)
        column = pl.ds(pl.multiple_of(position // half_groups * rows, rows), rows)
        for copy in range(2):
            start = copy * half + lax.rem(position, half_groups) * span
            tokens[kind, pl.ds(pl.multiple_of(start, span), span), column] = value

    def forward(kind):
        both = jnp.dot(fwd[...], tokens[kind], preferred_element_type=jnp.float32)
        for turn in range(4):
            even_rows = slice(turn * quarter, (turn + 1) * quarter)
            odd_rows = slice(length + turn * quarter, length + (turn + 1) * quarter)
            even, odd = both[even_rows, :rows], both[odd_rows, :rows]
            even_late, odd_late = both[even_rows, rows:], both[odd_rows, rows:]
            if turn == 0:
                even, odd = even + even_late, odd + odd_late
            elif turn == 1:
                even, odd = even - odd_late, odd + even_late
            elif turn == 2:
                even, odd = even - even_late, odd - odd_late
            else:
                even, odd = even + odd_late, odd - even_late
            freq[kind, even_rows, :] = even
            freq[kind, odd_rows, :] = odd

    def product(left_kind, right_kind, sign):
        for turn in range(4):
            even_rows = slice(turn * quarter, (turn + 1) * quarter)
            odd_rows = slice(length + turn * quarter, length + (turn + 1) * quarter)
            left_c, left_s = freq[left_kind, even_rows, :], freq[left_kind, odd_rows, :]
            right_c, right_s = freq[right_kind, even_rows, :], freq[right_kind, odd_rows, :]
            both = left_s * right_s
            cross = left_s * right_c - sign * (left_c * right_s)
            if turn == 0:
                first = lax.broadcasted_iota(jnp.int32, (quarter, rows), 0) == 0
                even = left_c * right_c + sign * jnp.where(first, 0.0, both)
                odd = jnp.where(first, both, cross)
            else:
                even = left_c * right_c + sign * both
                odd = cross
            for part in range(2):
                narrow_even = even.astype(jnp.bfloat16)
                narrow_odd = odd.astype(jnp.bfloat16)
                if part == 0:
                    even = even - narrow_even.astype(jnp.float32)
                    odd = odd - narrow_odd.astype(jnp.float32)
                pair[part, even_rows, :rows] = narrow_even
                pair[part, odd_rows, :rows] = narrow_odd
                late_even, late_odd = (
                    (narrow_even, narrow_odd),
                    (narrow_odd, -narrow_even),
                    (-narrow_even, -narrow_odd),
                    (-narrow_odd, narrow_even),
                )[turn]
                pair[part, even_rows, rows:] = late_even
                pair[part, odd_rows, rows:] = late_odd

    def inverse():
        total = jnp.dot(back[0], pair[0], preferred_element_type=jnp.float32)
        total += jnp.dot(back[0], pair[1], preferred_element_type=jnp.float32)
        total += jnp.dot(back[1], pair[0], preferred_element_type=jnp.float32)
        return total

    def finish(kind, result):
        total = inverse()
        if kind is not None:
            total = total + wide_gain * tokens[kind, :half, :].astype(jnp.float32)
        total = total.astype(jnp.bfloat16)
        result[:half, :] = total[:, :rows]
        result[half:length, :] = total[:, rows:]

    gates, mixes, kernels = range(3)

    loads[3].wait()
    loads[4].wait()
    loads[5].wait()
    gain = gain_line[:, lanes(0)]
    wide_gain = jnp.concatenate([gain, gain], 1)

    whole(FILT, filt_in).wait_recv()
    for step in range(groups):
        place(kernels, step, filt_in[step].T)
    forward(kernels)

    whole(GATE, gate_in).wait_recv()
    for step in range(groups):
        place(gates, step, gate_in[step])
    forward(gates)
    product(gates, kernels, 1.0)
    loads[6].wait()
    finish(gates, res_grad)

    def spread(kind, result, target, extent):
        def taken(step):
            return pl.ds(pl.multiple_of(near(step) * span, span), extent)

        push(kind, lambda step: result.at[taken(step), :], lambda slot: target.at[slot])
        target[0] = result[taken(0), :]

    spread(GRAD, res_grad, got_grad, span + edge)

    whole(MIX, mix_in).wait_recv()
    for step in range(groups):
        place(mixes, step, mix_in[step])
    forward(mixes)
    product(mixes, kernels, -1.0)
    finish(mixes, res_out)
    spread(OUT, res_out, got_out, span + edge)

    product(gates, mixes, 1.0)
    finish(None, res_long)
    @pl.when(me < groups - 1)
    def _():
        remote(edge_in, edge_in, EDGE, right).wait_recv()

    @pl.when(me == groups - 1)
    def _():
        edge_in[...] = jnp.zeros_like(edge_in)

    for step in range(groups):
        primed[step, 1, span : span + 2, :] = edge_in[near(step), 0:2, :]
        primed[step, 2, span : span + 2, :] = edge_in[near(step), 2:4, :]
        cot[step, span : span + 2, :] = edge_in[near(step), 4:6, :]

    def settle_stream(step, stream, value, sums, row):
        moving[...] = value
        running = coef(stream, 0, step) * moving[0:span, :]
        for offset in range(1, taps):
            running = running + coef(stream, offset, step) * moving[offset : offset + span, :]
        grad_out[stream, step] = running.astype(jnp.bfloat16)
        for offset in range(taps):
            start = 8 - offset
            total = jnp.sum(
                moving[0:span, :] * hist[step, stream, start : start + span, :],
                axis=0,
                keepdims=True,
            )
            sums[near(step), row + offset : row + offset + 1, :] = total

    reach = span + 8
    whole(GRAD, got_grad).wait_recv()
    for step in range(groups):
        mixed_back = got_grad[step].astype(jnp.float32)[:reach, :]
        settle_stream(step, 1, mixed_back * primed[step, 2, :, :], own_sums, 0)
        settle_stream(step, 2, mixed_back * primed[step, 1, :, :], own_sums, taps)
    remote(own_sums, mate_sums, MATE, mate).start()
    whole(OUT, got_out).wait_send()
    spread(LONG, res_long, long_out, span)
    remote(own_sums, mate_sums, MATE, mate).wait_recv()
    chip_sums[0] = own_sums[...] + mate_sums[...]
    for twin in range(1, twins):
        remote(chip_sums.at[0], chip_sums.at[twins - twin], CHIP, near(2 * twin)).start()

    whole(OUT, got_out).wait_recv()
    for step in range(groups):
        long_wide = got_out[step].astype(jnp.float32)[:reach, :]
        settle_stream(step, 0, long_wide * cot[step], late_sums.at[0], 0)
    push(LATE, lambda step: late_sums.at[0], lambda slot: late_sums.at[slot])
    for step in range(groups):
        gated_out[step] = (
            primed[step, 0, :span, :] * got_out[step, :span, :].astype(jnp.float32)
        ).astype(jnp.bfloat16)

    whole(LONG, long_out).wait_recv()
    others = chip_sums.at[1:twins]
    remote(others, others, CHIP, near(2)).wait_recv()
    whole(LATE, late_sums).wait_recv()
    remote(own_sums, mate_sums, MATE, mate).wait_send()
    remote(others, others, CHIP, near(2)).wait_send()

    @pl.when(me < groups - 1)
    def _():
        remote(halo_out, halo_in, HALO, right).wait_send()

    @pl.when(me > 0)
    def _():
        remote(edge_out, edge_in, EDGE, left).wait_send()

    for kind, target in (
        (FILT, filt_in),
        (MIX, mix_in),
        (GRAD, got_grad),
        (LONG, long_out),
        (LATE, late_sums),
    ):
        whole(kind, target).wait_send()


def settle_kernel(
    sizes, gated, grad, long, chip_sums, late_sums, gated_hbm, grad_hbm, long_hbm, taps_hbm, skip_hbm,
    wide, taps_line, skip_line, done,
):
    groups, rows, span, taps = sizes
    twins = groups // 2
    me = lax.axis_index("seq")
    copies = []

    def start(source, target):
        copy = pltpu.make_async_copy(source, target, done.at[len(copies)])
        copy.start()
        copies.append(copy)

    def turn(slot, source):
        for step in range(groups):
            owner = lax.rem(me + step, groups)
            picked = pl.ds(pl.multiple_of(owner * rows, rows), rows)
            wide[slot, picked, :] = source[step].T

    for stream in range(3):
        turn(stream, grad.at[stream])
    start(wide.at[0:3], grad_hbm)
    turn(3, gated)
    start(wide.at[3], gated_hbm)
    turn(4, long)
    start(wide.at[4], long_hbm)
    for group in range(groups):
        picked = slice(group * rows, (group + 1) * rows)
        early = late = None
        for source in range(groups):
            value = late_sums[lax.rem(source + groups - me, groups), group]
            late = value if late is None else late + value
        for source in range(twins):
            value = chip_sums[lax.rem(source + twins - me // 2, twins), group]
            early = value if early is None else early + value
        taps_line[0, :, picked] = late[:taps]
        taps_line[1, :, picked] = early[:taps]
        taps_line[2, :, picked] = early[taps : 2 * taps]
        skip_line[:, picked] = early[2 * taps : 2 * taps + 1]
    start(taps_line, taps_hbm)
    start(skip_line, skip_hbm)
    for copy in copies:
        copy.wait()


def fused(features, cotangent, long_filter, short_filters, skip_gain, groups):
    channels, span = cotangent.shape
    rows = channels // groups
    length = span * groups
    taps = short_filters.shape[2]
    hbm = pl.BlockSpec(memory_space=pltpu.HBM)
    vmem = pl.BlockSpec(memory_space=pltpu.VMEM)
    dma = pltpu.SemaphoreType.DMA
    narrow, wide = jnp.bfloat16, jnp.float32
    kinds = 11
    forward_table, back_table = packed_tables(length)
    middle = pl.pallas_call(
        functools.partial(fused_kernel, (groups, rows, span, length, taps)),
        out_shape=(
            pltpu.VMEM((groups, span, rows), narrow),
            pltpu.VMEM((3, groups, span, rows), narrow),
            pltpu.VMEM((groups, span, rows), narrow),
            pltpu.VMEM((groups // 2, groups, 8, rows), wide),
            pltpu.VMEM((groups, groups, 4, rows), wide),
        ),
        in_specs=[hbm] * 7,
        out_specs=(vmem,) * 5,
        scratch_shapes=[
            pltpu.VMEM((4, channels, span), narrow),
            pltpu.VMEM((3, taps, channels), wide),
            pltpu.VMEM((1, channels), wide),
            pltpu.VMEM((2 * length, length), narrow),
            pltpu.VMEM((2, length // 2, 2 * length), narrow),
            pltpu.VMEM((groups, 3, span + 8, rows), wide),
            pltpu.VMEM((groups, span + 8, rows), wide),
            pltpu.VMEM((groups, 3, span + 8, rows), wide),
            pltpu.VMEM((span + 8, rows), wide),
            pltpu.VMEM((groups, 8, rows), wide),
            pltpu.VMEM((groups, 8, rows), wide),
            pltpu.VMEM((groups, 8, rows), wide),
            pltpu.VMEM((groups, 8, rows), wide),
            pltpu.VMEM((groups, span, rows), narrow),
            pltpu.VMEM((groups, span, rows), narrow),
            pltpu.VMEM((groups, rows, span), narrow),
            pltpu.VMEM((groups, span, rows), narrow),
            pltpu.VMEM((groups, span, rows), narrow),
            pltpu.VMEM((3, length, 2 * rows), narrow),
            pltpu.VMEM((3, 2 * length, rows), wide),
            pltpu.VMEM((2, 2 * length, 2 * rows), narrow),
            pltpu.VMEM((length + 16, rows), narrow),
            pltpu.VMEM((length + 16, rows), narrow),
            pltpu.VMEM((length, rows), narrow),
            pltpu.VMEM((groups, span + 16, rows), narrow),
            pltpu.VMEM((groups, span + 16, rows), narrow),
            pltpu.VMEM((groups, 8, rows), wide),
            pltpu.VMEM((groups, 8, rows), wide),
            dma((7,)),
            dma((kinds,)),
            dma((kinds,)),
        ],
        compiler_params=pltpu.CompilerParams(
            collective_id=0, has_side_effects=True, vmem_limit_bytes=40 * 2**20
        ),
    )(
        *[
            pltpu.with_memory_space_constraint(value, pltpu.HBM)
            for value in (
                features,
                cotangent,
                long_filter,
                jnp.swapaxes(short_filters, 1, 2),
                skip_gain[None],
                jnp.asarray(forward_table),
                jnp.asarray(back_table),
            )
        ]
    )
    gated_out, feature_grad, long_grad, taps_grad, gain_grad = pl.pallas_call(
        functools.partial(settle_kernel, (groups, rows, span, taps)),
        out_shape=(
            jax.ShapeDtypeStruct((channels, span), narrow),
            jax.ShapeDtypeStruct((3, channels, span), narrow),
            jax.ShapeDtypeStruct((channels, span), narrow),
            jax.ShapeDtypeStruct((3, taps, channels), wide),
            jax.ShapeDtypeStruct((1, channels), wide),
        ),
        in_specs=[vmem] * 5,
        out_specs=(hbm,) * 5,
        scratch_shapes=[
            pltpu.VMEM((5, channels, span), narrow),
            pltpu.VMEM((3, taps, channels), wide),
            pltpu.VMEM((1, channels), wide),
            dma((5,)),
        ],
    )(*[pltpu.with_memory_space_constraint(value, pltpu.VMEM) for value in middle])
    return gated_out, feature_grad, long_grad, jnp.swapaxes(taps_grad, 1, 2), gain_grad[0]


def dense_fits(features, short_filters, groups):
    channels, span = features.shape[1:]
    rows, length = channels // groups, span * groups
    return (
        channels % groups == 0
        and groups % 2 == 0
        and groups > 2
        and rows == 128
        and span == 128
        and length % 512 == 0
        and length <= 1024
        and 2 <= short_filters.shape[2] <= 3
    )


def shards(features, cotangent, long_filter, short_filters, skip_gain):
    groups = lax.axis_size("seq")
    if dense_fits(features, short_filters, groups):
        return fused(features, cotangent, long_filter, short_filters, skip_gain, groups)
    seq_index = lax.axis_index("seq")
    channels = features.shape[1]
    per_group = channels // groups
    margin = short_filters.shape[2] - 1
    local_gain = lax.dynamic_slice_in_dim(skip_gain, seq_index * per_group, per_group, 0)
    stacked = jnp.concatenate([features, cotangent[None], long_filter[None]], 0)
    columns = lax.all_to_all(stacked, "seq", split_axis=1, concat_axis=2, tiled=True)
    weights = lax.dynamic_slice_in_dim(short_filters, seq_index * per_group, per_group, 1)
    length = columns.shape[2]
    history = jnp.pad(columns[:3].astype(jnp.float32), ((0, 0), (0, 0), (margin, 0)))
    primed = featurize(history, weights, margin, length)
    mixed_term = (primed[1] * primed[2]).astype(jnp.bfloat16)
    cot_wide = columns[3].astype(jnp.float32)
    gated_grad = (cot_wide * primed[0]).astype(jnp.bfloat16)
    long_out, mixed_grad, kernel_grad = spectral(mixed_term, gated_grad, columns[4], local_gain)
    long_wide = long_out.astype(jnp.float32)
    mixed_back = mixed_grad.astype(jnp.float32)
    gated_out = (primed[0] * long_wide).astype(jnp.bfloat16)
    primed_grad = jnp.stack([cot_wide * long_wide, mixed_back * primed[2], mixed_back * primed[1]])
    padded_grad = jnp.pad(primed_grad, ((0, 0), (0, 0), (0, margin)))
    feature_grad = unfeaturize(padded_grad, weights, length).astype(jnp.bfloat16)
    taps_grad = tap_grads(primed_grad, history, margin, length)
    gain_grad = jnp.sum(gated_grad.astype(jnp.float32) * mixed_term.astype(jnp.float32), axis=-1)
    results = jnp.concatenate([gated_out[None], feature_grad, kernel_grad[None]], 0)
    row_blocks = lax.all_to_all(results, "seq", split_axis=2, concat_axis=1, tiled=True)
    short_grad, skip_grad = (
        lax.all_gather(taps_grad, "seq", axis=1, tiled=True),
        lax.all_gather(gain_grad, "seq", axis=0, tiled=True),
    )
    return (row_blocks[0], row_blocks[1:4], row_blocks[4], short_grad, skip_grad)


def solution(mesh):
    placed = (
        P(None, "chan", "seq"),
        P("chan", "seq"),
        P("chan", "seq"),
        P(None, "chan", None),
        P("chan"),
    )
    return jax.shard_map(
        shards,
        mesh=mesh,
        in_specs=placed,
        out_specs=(
            P("chan", "seq"),
            P(None, "chan", "seq"),
            P("chan", "seq"),
            P(None, "chan", None),
            P("chan"),
        ),
        check_vma=False,
    )
```

```python
import functools
import math

import jax
import jax.numpy as jnp
import numpy as np
from jax import lax
from jax.experimental import pallas as pl
from jax.experimental.pallas import tpu as pltpu
from jax.sharding import PartitionSpec as P

inner_length = 128
radix_width = 8


def phase_tables(row_count, col_count, length, direction):
    phase_index = (
        lax.iota(jnp.int32, row_count)[:, None] * lax.iota(jnp.int32, col_count)[None, :] % length
    )
    angles = direction * 2.0 * math.pi / length * phase_index.astype(jnp.float32)
    return (jnp.cos(angles), jnp.sin(angles))


def last_axis(operand, matrix):
    return jnp.einsum("...n,nk->...k", operand, matrix, precision=lax.Precision.HIGH)


def first_axis(operand, matrix):
    return jnp.einsum("...ab,ak->...kb", operand, matrix, precision=lax.Precision.HIGH)


def transform(real_part, imag_part, direction):
    length = real_part.shape[-1]
    if length <= inner_length or length % radix_width != 0:
        cos_table, sin_table = phase_tables(length, length, length, direction)
        return (
            last_axis(real_part, cos_table) - last_axis(imag_part, sin_table),
            last_axis(real_part, sin_table) + last_axis(imag_part, cos_table),
        )
    rest_length = length // radix_width
    grid_shape = real_part.shape[:-1] + (radix_width, rest_length)
    real_grid = real_part.reshape(grid_shape)
    imag_grid = imag_part.reshape(grid_shape)
    cos_table, sin_table = phase_tables(radix_width, radix_width, radix_width, direction)
    section_real = first_axis(real_grid, cos_table) - first_axis(imag_grid, sin_table)
    section_imag = first_axis(real_grid, sin_table) + first_axis(imag_grid, cos_table)
    twist_cos, twist_sin = phase_tables(radix_width, rest_length, length, direction)
    turned_real = section_real * twist_cos - section_imag * twist_sin
    turned_imag = section_real * twist_sin + section_imag * twist_cos
    inner_real, inner_imag = transform(turned_real, turned_imag, direction)
    return (
        jnp.swapaxes(inner_real, -1, -2).reshape(real_part.shape),
        jnp.swapaxes(inner_imag, -1, -2).reshape(real_part.shape),
    )


def spectral(mixed_term, gated_grad, kernel, local_gain):
    length = mixed_term.shape[-1]
    mixed_wide = mixed_term.astype(jnp.float32)
    gated_wide = gated_grad.astype(jnp.float32)
    kernel_wide = kernel.astype(jnp.float32)
    extend = ((0, 0), (0, length))
    real_in = jnp.stack([jnp.pad(mixed_wide, extend), jnp.pad(kernel_wide, extend)])
    imag_in = jnp.stack(
        [jnp.pad(gated_wide, extend), jnp.zeros((kernel_wide.shape[0], 2 * length), jnp.float32)]
    )
    freq_real, freq_imag = transform(real_in, imag_in, -1.0)
    packed_real = freq_real[0]
    packed_imag = freq_imag[0]
    mirror_real = jnp.roll(jnp.flip(packed_real, -1), 1, -1)
    mirror_imag = jnp.roll(jnp.flip(packed_imag, -1), 1, -1)
    mix_real = 0.5 * (packed_real + mirror_real)
    mix_imag = 0.5 * (packed_imag - mirror_imag)
    grad_real = 0.5 * (packed_imag + mirror_imag)
    grad_imag = 0.5 * (mirror_real - packed_real)
    kern_real = freq_real[1]
    kern_imag = freq_imag[1]
    conv_real = mix_real * kern_real - mix_imag * kern_imag
    conv_imag = mix_real * kern_imag + mix_imag * kern_real
    corr_real = grad_real * kern_real + grad_imag * kern_imag
    corr_imag = grad_imag * kern_real - grad_real * kern_imag
    cross_real = grad_real * mix_real + grad_imag * mix_imag
    cross_imag = grad_imag * mix_real - grad_real * mix_imag
    back_real = jnp.stack([conv_real - corr_imag, cross_real])
    back_imag = jnp.stack([conv_imag + corr_real, cross_imag])
    time_real, time_imag = transform(back_real, back_imag, 1.0)
    inverse_scale = 1.0 / (2 * length)
    conv_part = time_real[0, :, :length] * inverse_scale
    corr_part = time_imag[0, :, :length] * inverse_scale
    cross_part = time_real[1, :, :length] * inverse_scale
    gain_column = local_gain[:, None]
    long_out = (conv_part + gain_column * mixed_wide).astype(jnp.bfloat16)
    mixed_grad = (corr_part + gain_column * gated_wide).astype(jnp.bfloat16)
    return (long_out, mixed_grad, cross_part.astype(jnp.bfloat16))


def featurize(history, weights, margin, span_count):
    running = weights[:, :, 0:1] * history[:, :, margin : margin + span_count]
    for offset in range(1, margin + 1):
        running = (
            running
            + weights[:, :, offset : offset + 1]
            * history[:, :, margin - offset : margin - offset + span_count]
        )
    return running


def unfeaturize(padded_grad, weights, span_count):
    running = weights[:, :, 0:1] * padded_grad[:, :, 0:span_count]
    for offset in range(1, weights.shape[2]):
        running = (
            running
            + weights[:, :, offset : offset + 1] * padded_grad[:, :, offset : offset + span_count]
        )
    return running


def tap_grads(primed_grad, history, margin, span_count):
    columns = []
    for offset in range(margin + 1):
        columns.append(
            jnp.sum(
                primed_grad * history[:, :, margin - offset : margin - offset + span_count], axis=-1
            )
        )
    return jnp.stack(columns, axis=-1)


def packed_tables(length):
    half, quarter = length // 2, length // 4
    steps = np.arange(half)
    bins = np.arange(length).reshape(quarter, 4).T.reshape(-1)
    phase = (steps[:, None] * bins[None, :]) % (2 * length)
    angles = np.pi / length * phase
    sines = np.sin(angles)
    sines[:, 0] = 1.0 - 2.0 * (steps % 2)
    table = np.concatenate([np.cos(angles), sines], 1)
    weights = np.full(2 * length, 1.0 / length)
    weights[0] = weights[length] = 0.5 / length
    forward = table.T.astype(np.float32)
    high = forward.astype(jnp.bfloat16)
    low = (forward - high.astype(np.float32)).astype(jnp.bfloat16)
    return np.concatenate([high, low], 1), (table * weights).astype(np.float32).astype(jnp.bfloat16)


def fused_kernel(
    sizes,
    feat_hbm,
    cot_hbm,
    filt_hbm,
    short_hbm,
    gain_hbm,
    fwd_hbm,
    back_hbm,
    gated_out,
    grad_out,
    long_out,
    chip_sums,
    late_sums,
    raw,
    short,
    gain_line,
    fwd,
    back,
    hist,
    cot,
    primed,
    moving,
    halo_out,
    halo_in,
    edge_out,
    edge_in,
    last_out,
    last_in,
    gate_out,
    mix_out,
    filt_in,
    gate_in,
    mix_in,
    tokens,
    freq,
    pair,
    res_grad,
    res_out,
    res_long,
    got_grad,
    got_out,
    own_sums,
    mate_sums,
    load_sem,
    send_sem,
    recv_sem,
):
    groups, rows, span, length, taps = sizes
    me = lax.axis_index("seq")
    peers = range(1, groups)
    edge = 16
    FILT, GATE, MIX, GRAD, OUT, LONG, MATE, CHIP, LATE, HALO, EDGE, LAST = range(12)
    half, quarter = length // 2, length // 4
    half_groups, twins = groups // 2, groups // 2
    mate = me + 1 - 2 * lax.rem(me, 2)

    def near(step):
        return lax.rem(me + step, groups)

    def block(index, extent, count=1):
        return pl.ds(pl.multiple_of(index * extent, extent), extent * count)

    def lanes(step):
        return block(near(step), rows)

    barrier = pltpu.get_barrier_semaphore()
    for step in peers:
        pl.semaphore_signal(
            barrier,
            inc=1,
            device_id={"seq": near(step)},
            device_id_type=pl.DeviceIdType.MESH,
        )
    pairs = [
        (feat_hbm, raw.at[0:3]),
        (cot_hbm, raw.at[3]),
        (short_hbm, short),
        (gain_hbm, gain_line),
        (filt_hbm.at[lanes(0), :], filt_in.at[0]),
        (fwd_hbm, fwd),
        (back_hbm, back),
    ]
    loads = [
        pltpu.make_async_copy(source, target, load_sem.at[index])
        for index, (source, target) in enumerate(pairs)
    ]
    for index in (2, 0, 1):
        loads[index].start()

    def remote(source, target, kind, peer):
        return pltpu.make_async_remote_copy(
            src_ref=source,
            dst_ref=target,
            send_sem=send_sem.at[kind],
            recv_sem=recv_sem.at[kind],
            device_id={"seq": peer},
            device_id_type=pl.DeviceIdType.MESH,
        )

    def push(kind, source_of, target_of):
        for step in peers:
            remote(source_of(step), target_of(groups - step), kind, near(step)).start()

    def push_rows(kind, source, target, first, count):
        picked = pl.ds(first, count)
        push(
            kind,
            lambda step: source.at[step, picked, :],
            lambda slot: target.at[slot, picked, :],
        )

    def whole(kind, target):
        landed = target.at[1:groups]
        return remote(landed, landed, kind, near(1))

    loads[2].wait()
    loads[0].wait()

    halo_out[...] = jnp.zeros_like(halo_out)
    last_out[...] = jnp.zeros_like(last_out)
    moving[...] = jnp.zeros_like(moving)
    for step in range(groups):
        for stream in range(3):
            wide = raw[stream, lanes(step), :].T.astype(jnp.float32)
            hist[step, stream, 8:, :] = wide
            halo_out[near(step), 2 * stream : 2 * stream + 2, :] = wide[span - 2 :, :]

    right, left = near(1), near(groups - 1)

    pl.semaphore_wait(barrier, groups - 1)
    @pl.when(me < groups - 1)
    def _():
        remote(halo_out, halo_in, HALO, right).start()

    push(FILT, lambda step: filt_hbm.at[lanes(step), :], lambda slot: filt_in.at[slot])
    for index in (3, 4, 5, 6):
        loads[index].start()

    loads[1].wait()
    for step in range(groups):
        cot[step] = raw[3, lanes(step), :].T.astype(jnp.float32)

    def coef(stream, offset, step):
        return short[stream, offset : offset + 1, lanes(step)]

    def featurize(step, stream, first, count):
        running = coef(stream, 0, step) * hist[step, stream, 8 + first : 8 + first + count, :]
        for offset in range(1, taps):
            start = 8 + first - offset
            running = (
                running
                + coef(stream, offset, step) * hist[step, stream, start : start + count, :]
            )
        primed[step, stream, first : first + count, :] = running
        return running

    def gate(step, first, count):
        value = featurize(step, 0, first, count) * cot[step, first : first + count, :]
        gate_out[step, first : first + count, :] = value.astype(jnp.bfloat16)

    def mix(step, first, count):
        value = featurize(step, 1, first, count) * featurize(step, 2, first, count)
        mix_out[step, first : first + count, :] = value.astype(jnp.bfloat16)

    for step in range(groups):
        gate(step, edge, span - edge)
    push_rows(GATE, gate_out, gate_in, edge, span - edge)
    for step in range(groups):
        mix(step, edge, span - edge)

    @pl.when(me > 0)
    def _():
        remote(halo_in, halo_in, HALO, left).wait_recv()

    @pl.when(me == 0)
    def _():
        halo_in[...] = jnp.zeros_like(halo_in)

    for step in range(groups):
        for stream in range(3):
            hist[step, stream, 6:8, :] = halo_in[near(step), 2 * stream : 2 * stream + 2, :]
        gate(step, 0, edge)
    push_rows(GATE, gate_out, gate_in, 0, edge)
    for step in range(groups):
        mix(step, 0, edge)
    whole(GATE, gate_in).wait_send()
    push_rows(MIX, mix_out, mix_in, 0, span)
    gate_in[0] = gate_out[0]
    mix_in[0] = mix_out[0]
    own_sums[...] = jnp.zeros_like(own_sums)
    late_sums[0] = jnp.zeros(late_sums.shape[1:], jnp.float32)
    for step in range(groups):
        local = gate_out[step].astype(jnp.float32) * mix_out[step].astype(jnp.float32)
        own_sums[near(step), 2 * taps : 2 * taps + 1, :] = jnp.sum(local, axis=0, keepdims=True)

    def place(kind, step, value):
        position = near(step)
        column = pl.ds(pl.multiple_of(position // half_groups * rows, rows), rows)
        for copy in range(2):
            start = copy * half + lax.rem(position, half_groups) * span
            tokens[kind, pl.ds(pl.multiple_of(start, span), span), column] = value

    def forward(kind):
        both = jnp.dot(fwd[...], tokens[kind], preferred_element_type=jnp.float32)
        for turn in range(4):
            even_rows = slice(turn * quarter, (turn + 1) * quarter)
            odd_rows = slice(length + turn * quarter, length + (turn + 1) * quarter)
            even, odd = both[even_rows, :rows], both[odd_rows, :rows]
            even_late, odd_late = both[even_rows, rows:], both[odd_rows, rows:]
            if turn == 0:
                even, odd = even + even_late, odd + odd_late
            elif turn == 1:
                even, odd = even - odd_late, odd + even_late
            elif turn == 2:
                even, odd = even - even_late, odd - odd_late
            else:
                even, odd = even + odd_late, odd - even_late
            freq[kind, even_rows, :] = even
            freq[kind, odd_rows, :] = odd

    def product(left_kind, right_kind, sign):
        for turn in range(4):
            even_rows = slice(turn * quarter, (turn + 1) * quarter)
            odd_rows = slice(length + turn * quarter, length + (turn + 1) * quarter)
            left_c, left_s = freq[left_kind, even_rows, :], freq[left_kind, odd_rows, :]
            right_c, right_s = freq[right_kind, even_rows, :], freq[right_kind, odd_rows, :]
            both = left_s * right_s
            cross = left_s * right_c - sign * (left_c * right_s)
            if turn == 0:
                first = lax.broadcasted_iota(jnp.int32, (quarter, rows), 0) == 0
                even = left_c * right_c + sign * jnp.where(first, 0.0, both)
                odd = jnp.where(first, both, cross)
            else:
                even = left_c * right_c + sign * both
                odd = cross
            even = even.astype(jnp.bfloat16)
            odd = odd.astype(jnp.bfloat16)
            pair[even_rows, :rows] = even
            pair[odd_rows, :rows] = odd
            late_even, late_odd = ((even, odd), (odd, -even), (-even, -odd), (-odd, even))[turn]
            pair[even_rows, rows:] = late_even
            pair[odd_rows, rows:] = late_odd

    def finish(kind, result):
        total = jnp.dot(back[...], pair[...], preferred_element_type=jnp.float32)
        if kind is not None:
            total = total + wide_gain * tokens[kind, :half, :].astype(jnp.float32)
        total = total.astype(jnp.bfloat16)
        result[:half, :] = total[:, :rows]
        result[half:, :] = total[:, rows:]

    gates, mixes, kernels = range(3)

    loads[3].wait()
    loads[4].wait()
    loads[5].wait()
    gain = gain_line[:, lanes(0)]
    wide_gain = jnp.concatenate([gain, gain], 1)

    whole(FILT, filt_in).wait_recv()
    for step in range(groups):
        place(kernels, step, filt_in[step].T)
    forward(kernels)

    whole(GATE, gate_in).wait_recv()
    for step in range(groups):
        place(gates, step, gate_in[step])
    forward(gates)
    product(gates, kernels, 1.0)
    loads[6].wait()
    finish(gates, res_grad)

    def spread(kind, result, target):
        def taken(step):
            return block(near(step), span)

        push(kind, lambda step: result.at[taken(step), :], lambda slot: target.at[slot])
        target[0] = result[taken(0), :]

    spread(GRAD, res_grad, got_grad)

    whole(MIX, mix_in).wait_recv()
    for step in range(groups):
        place(mixes, step, mix_in[step])
    forward(mixes)
    product(mixes, kernels, -1.0)
    finish(mixes, res_out)
    spread(OUT, res_out, got_out)

    product(gates, mixes, 1.0)
    finish(None, res_long)
    def tally(step, stream, sums, row):
        for offset in range(taps):
            start = 8 - offset
            total = jnp.sum(
                moving[stream, step, 0:span, :] * hist[step, stream, start : start + span, :],
                axis=0,
                keepdims=True,
            )
            sums[near(step), row + offset : row + offset + 1, :] = total

    def spend(step, stream, first, count):
        running = coef(stream, 0, step) * moving[stream, step, first : first + count, :]
        for offset in range(1, taps):
            start = first + offset
            running = (
                running
                + coef(stream, offset, step) * moving[stream, step, start : start + count, :]
            )
        grad_out[stream, step, first : first + count, :] = running.astype(jnp.bfloat16)

    def hand_left(kind, source, target):
        @pl.when(me > 0)
        def _():
            remote(source, target, kind, left).start()

    def complete(kind, source, target, streams):
        @pl.when(me < groups - 1)
        def _():
            remote(target, target, kind, right).wait_recv()
            for step in range(groups):
                for place_of, stream in enumerate(streams):
                    taken = target[near(step), 2 * place_of : 2 * place_of + 2, :]
                    moving[stream, step, span : span + 2, :] = taken

        for step in range(groups):
            for stream in streams:
                spend(step, stream, span - edge, edge)

        @pl.when(me > 0)
        def _():
            remote(source, target, kind, left).wait_send()

    whole(OUT, got_out).wait_send()
    spread(LONG, res_long, long_out)

    whole(GRAD, got_grad).wait_recv()
    for step in range(groups):
        mixed_back = got_grad[step].astype(jnp.float32)
        moving[1, step, 0:span, :] = mixed_back * primed[step, 2, :, :]
        moving[2, step, 0:span, :] = mixed_back * primed[step, 1, :, :]
        edge_out[near(step), 0:2, :] = moving[1, step, 0:2, :]
        edge_out[near(step), 2:4, :] = moving[2, step, 0:2, :]
        tally(step, 1, own_sums, 0)
        tally(step, 2, own_sums, taps)
    remote(own_sums, mate_sums, MATE, mate).start()
    hand_left(EDGE, edge_out, edge_in)
    for step in range(groups):
        spend(step, 1, 0, span - edge)
        spend(step, 2, 0, span - edge)
    remote(own_sums, mate_sums, MATE, mate).wait_recv()
    chip_sums[0] = own_sums[...] + mate_sums[...]
    for twin in range(1, twins):
        remote(chip_sums.at[0], chip_sums.at[twins - twin], CHIP, near(2 * twin)).start()

    whole(OUT, got_out).wait_recv()
    for step in range(groups):
        moving[0, step, 0:span, :] = got_out[step].astype(jnp.float32) * cot[step]
        last_out[near(step), 0:2, :] = moving[0, step, 0:2, :]
        tally(step, 0, late_sums.at[0], 0)
    push(LATE, lambda step: late_sums.at[0], lambda slot: late_sums.at[slot])
    hand_left(LAST, last_out, last_in)
    for step in range(groups):
        gated_out[step] = (
            primed[step, 0, :, :] * got_out[step].astype(jnp.float32)
        ).astype(jnp.bfloat16)
        spend(step, 0, 0, span - edge)

    complete(EDGE, edge_out, edge_in, (1, 2))
    complete(LAST, last_out, last_in, (0,))
    whole(LONG, long_out).wait_recv()
    others = chip_sums.at[1:twins]
    remote(others, others, CHIP, near(2)).wait_recv()
    whole(LATE, late_sums).wait_recv()
    remote(own_sums, mate_sums, MATE, mate).wait_send()
    remote(others, others, CHIP, near(2)).wait_send()

    @pl.when(me < groups - 1)
    def _():
        remote(halo_out, halo_in, HALO, right).wait_send()

    for kind, target in (
        (FILT, filt_in),
        (MIX, mix_in),
        (GRAD, got_grad),
        (LONG, long_out),
        (LATE, late_sums),
    ):
        whole(kind, target).wait_send()


def settle_kernel(
    sizes, gated, grad, long, chip_sums, late_sums, gated_hbm, grad_hbm, long_hbm, taps_hbm, skip_hbm,
    wide, taps_line, skip_line, done,
):
    groups, rows, span, taps = sizes
    twins = groups // 2
    me = lax.axis_index("seq")
    copies = []

    def start(source, target):
        copy = pltpu.make_async_copy(source, target, done.at[len(copies)])
        copy.start()
        copies.append(copy)

    def turn(slot, source):
        for step in range(groups):
            owner = lax.rem(me + step, groups)
            picked = pl.ds(pl.multiple_of(owner * rows, rows), rows)
            wide[slot, picked, :] = source[step].T

    for stream in range(3):
        turn(stream, grad.at[stream])
    start(wide.at[0:3], grad_hbm)
    turn(3, gated)
    start(wide.at[3], gated_hbm)
    turn(4, long)
    start(wide.at[4], long_hbm)
    for group in range(groups):
        picked = slice(group * rows, (group + 1) * rows)
        early = late = None
        for source in range(groups):
            value = late_sums[lax.rem(source + groups - me, groups), group]
            late = value if late is None else late + value
        for source in range(twins):
            value = chip_sums[lax.rem(source + twins - me // 2, twins), group]
            early = value if early is None else early + value
        taps_line[0, :, picked] = late[:taps]
        taps_line[1, :, picked] = early[:taps]
        taps_line[2, :, picked] = early[taps : 2 * taps]
        skip_line[:, picked] = early[2 * taps : 2 * taps + 1]
    start(taps_line, taps_hbm)
    start(skip_line, skip_hbm)
    for copy in copies:
        copy.wait()


def fused(features, cotangent, long_filter, short_filters, skip_gain, groups):
    channels, span = cotangent.shape
    rows = channels // groups
    length = span * groups
    taps = short_filters.shape[2]
    hbm = pl.BlockSpec(memory_space=pltpu.HBM)
    vmem = pl.BlockSpec(memory_space=pltpu.VMEM)
    dma = pltpu.SemaphoreType.DMA
    narrow, wide = jnp.bfloat16, jnp.float32
    kinds = 12
    forward_table, back_table = packed_tables(length)
    middle = pl.pallas_call(
        functools.partial(fused_kernel, (groups, rows, span, length, taps)),
        out_shape=(
            pltpu.VMEM((groups, span, rows), narrow),
            pltpu.VMEM((3, groups, span, rows), narrow),
            pltpu.VMEM((groups, span, rows), narrow),
            pltpu.VMEM((groups // 2, groups, 8, rows), wide),
            pltpu.VMEM((groups, groups, 4, rows), wide),
        ),
        in_specs=[hbm] * 7,
        out_specs=(vmem,) * 5,
        scratch_shapes=[
            pltpu.VMEM((4, channels, span), narrow),
            pltpu.VMEM((3, taps, channels), wide),
            pltpu.VMEM((1, channels), wide),
            pltpu.VMEM((2 * length, length), narrow),
            pltpu.VMEM((length // 2, 2 * length), narrow),
            pltpu.VMEM((groups, 3, span + 8, rows), wide),
            pltpu.VMEM((groups, span, rows), wide),
            pltpu.VMEM((groups, 3, span, rows), wide),
            pltpu.VMEM((3, groups, span + 8, rows), wide),
            pltpu.VMEM((groups, 8, rows), wide),
            pltpu.VMEM((groups, 8, rows), wide),
            pltpu.VMEM((groups, 4, rows), wide),
            pltpu.VMEM((groups, 4, rows), wide),
            pltpu.VMEM((groups, 4, rows), wide),
            pltpu.VMEM((groups, 4, rows), wide),
            pltpu.VMEM((groups, span, rows), narrow),
            pltpu.VMEM((groups, span, rows), narrow),
            pltpu.VMEM((groups, rows, span), narrow),
            pltpu.VMEM((groups, span, rows), narrow),
            pltpu.VMEM((groups, span, rows), narrow),
            pltpu.VMEM((3, length, 2 * rows), narrow),
            pltpu.VMEM((3, 2 * length, rows), wide),
            pltpu.VMEM((2 * length, 2 * rows), narrow),
            pltpu.VMEM((length, rows), narrow),
            pltpu.VMEM((length, rows), narrow),
            pltpu.VMEM((length, rows), narrow),
            pltpu.VMEM((groups, span, rows), narrow),
            pltpu.VMEM((groups, span, rows), narrow),
            pltpu.VMEM((groups, 8, rows), wide),
            pltpu.VMEM((groups, 8, rows), wide),
            dma((7,)),
            dma((kinds,)),
            dma((kinds,)),
        ],
        compiler_params=pltpu.CompilerParams(
            collective_id=0, has_side_effects=True, vmem_limit_bytes=40 * 2**20
        ),
    )(
        *[
            pltpu.with_memory_space_constraint(value, pltpu.HBM)
            for value in (
                features,
                cotangent,
                long_filter,
                jnp.swapaxes(short_filters, 1, 2),
                skip_gain[None],
                jnp.asarray(forward_table),
                jnp.asarray(back_table),
            )
        ]
    )
    gated_out, feature_grad, long_grad, taps_grad, gain_grad = pl.pallas_call(
        functools.partial(settle_kernel, (groups, rows, span, taps)),
        out_shape=(
            jax.ShapeDtypeStruct((channels, span), narrow),
            jax.ShapeDtypeStruct((3, channels, span), narrow),
            jax.ShapeDtypeStruct((channels, span), narrow),
            jax.ShapeDtypeStruct((3, taps, channels), wide),
            jax.ShapeDtypeStruct((1, channels), wide),
        ),
        in_specs=[vmem] * 5,
        out_specs=(hbm,) * 5,
        scratch_shapes=[
            pltpu.VMEM((5, channels, span), narrow),
            pltpu.VMEM((3, taps, channels), wide),
            pltpu.VMEM((1, channels), wide),
            dma((5,)),
        ],
    )(*[pltpu.with_memory_space_constraint(value, pltpu.VMEM) for value in middle])
    return gated_out, feature_grad, long_grad, jnp.swapaxes(taps_grad, 1, 2), gain_grad[0]


def dense_fits(features, short_filters, groups):
    channels, span = features.shape[1:]
    rows, length = channels // groups, span * groups
    return (
        channels % groups == 0
        and groups % 2 == 0
        and groups > 2
        and rows == 128
        and span == 128
        and length % 512 == 0
        and length <= 1024
        and 2 <= short_filters.shape[2] <= 3
    )


def shards(features, cotangent, long_filter, short_filters, skip_gain):
    groups = lax.axis_size("seq")
    if dense_fits(features, short_filters, groups):
        return fused(features, cotangent, long_filter, short_filters, skip_gain, groups)
    seq_index = lax.axis_index("seq")
    channels = features.shape[1]
    per_group = channels // groups
    margin = short_filters.shape[2] - 1
    local_gain = lax.dynamic_slice_in_dim(skip_gain, seq_index * per_group, per_group, 0)
    stacked = jnp.concatenate([features, cotangent[None], long_filter[None]], 0)
    columns = lax.all_to_all(stacked, "seq", split_axis=1, concat_axis=2, tiled=True)
    weights = lax.dynamic_slice_in_dim(short_filters, seq_index * per_group, per_group, 1)
    length = columns.shape[2]
    history = jnp.pad(columns[:3].astype(jnp.float32), ((0, 0), (0, 0), (margin, 0)))
    primed = featurize(history, weights, margin, length)
    mixed_term = (primed[1] * primed[2]).astype(jnp.bfloat16)
    cot_wide = columns[3].astype(jnp.float32)
    gated_grad = (cot_wide * primed[0]).astype(jnp.bfloat16)
    long_out, mixed_grad, kernel_grad = spectral(mixed_term, gated_grad, columns[4], local_gain)
    long_wide = long_out.astype(jnp.float32)
    mixed_back = mixed_grad.astype(jnp.float32)
    gated_out = (primed[0] * long_wide).astype(jnp.bfloat16)
    primed_grad = jnp.stack([cot_wide * long_wide, mixed_back * primed[2], mixed_back * primed[1]])
    padded_grad = jnp.pad(primed_grad, ((0, 0), (0, 0), (0, margin)))
    feature_grad = unfeaturize(padded_grad, weights, length).astype(jnp.bfloat16)
    taps_grad = tap_grads(primed_grad, history, margin, length)
    gain_grad = jnp.sum(gated_grad.astype(jnp.float32) * mixed_term.astype(jnp.float32), axis=-1)
    results = jnp.concatenate([gated_out[None], feature_grad, kernel_grad[None]], 0)
    row_blocks = lax.all_to_all(results, "seq", split_axis=2, concat_axis=1, tiled=True)
    short_grad, skip_grad = (
        lax.all_gather(taps_grad, "seq", axis=1, tiled=True),
        lax.all_gather(gain_grad, "seq", axis=0, tiled=True),
    )
    return (row_blocks[0], row_blocks[1:4], row_blocks[4], short_grad, skip_grad)


def solution(mesh):
    placed = (
        P(None, "chan", "seq"),
        P("chan", "seq"),
        P("chan", "seq"),
        P(None, "chan", None),
        P("chan"),
    )
    return jax.shard_map(
        shards,
        mesh=mesh,
        in_specs=placed,
        out_specs=(
            P("chan", "seq"),
            P(None, "chan", "seq"),
            P("chan", "seq"),
            P(None, "chan", None),
            P("chan"),
        ),
        check_vma=False,
    )
```

```python
import functools
import math

import jax
import jax.numpy as jnp
import numpy as np
from jax import lax
from jax.experimental import pallas as pl
from jax.experimental.pallas import tpu as pltpu
from jax.sharding import PartitionSpec as P

inner_length = 128
radix_width = 8


def phase_tables(row_count, col_count, length, direction):
    phase_index = (
        lax.iota(jnp.int32, row_count)[:, None] * lax.iota(jnp.int32, col_count)[None, :] % length
    )
    angles = direction * 2.0 * math.pi / length * phase_index.astype(jnp.float32)
    return (jnp.cos(angles), jnp.sin(angles))


def last_axis(operand, matrix):
    return jnp.einsum("...n,nk->...k", operand, matrix, precision=lax.Precision.HIGH)


def first_axis(operand, matrix):
    return jnp.einsum("...ab,ak->...kb", operand, matrix, precision=lax.Precision.HIGH)


def transform(real_part, imag_part, direction):
    length = real_part.shape[-1]
    if length <= inner_length or length % radix_width != 0:
        cos_table, sin_table = phase_tables(length, length, length, direction)
        return (
            last_axis(real_part, cos_table) - last_axis(imag_part, sin_table),
            last_axis(real_part, sin_table) + last_axis(imag_part, cos_table),
        )
    rest_length = length // radix_width
    grid_shape = real_part.shape[:-1] + (radix_width, rest_length)
    real_grid = real_part.reshape(grid_shape)
    imag_grid = imag_part.reshape(grid_shape)
    cos_table, sin_table = phase_tables(radix_width, radix_width, radix_width, direction)
    section_real = first_axis(real_grid, cos_table) - first_axis(imag_grid, sin_table)
    section_imag = first_axis(real_grid, sin_table) + first_axis(imag_grid, cos_table)
    twist_cos, twist_sin = phase_tables(radix_width, rest_length, length, direction)
    turned_real = section_real * twist_cos - section_imag * twist_sin
    turned_imag = section_real * twist_sin + section_imag * twist_cos
    inner_real, inner_imag = transform(turned_real, turned_imag, direction)
    return (
        jnp.swapaxes(inner_real, -1, -2).reshape(real_part.shape),
        jnp.swapaxes(inner_imag, -1, -2).reshape(real_part.shape),
    )


def spectral(mixed_term, gated_grad, kernel, local_gain):
    length = mixed_term.shape[-1]
    mixed_wide = mixed_term.astype(jnp.float32)
    gated_wide = gated_grad.astype(jnp.float32)
    kernel_wide = kernel.astype(jnp.float32)
    extend = ((0, 0), (0, length))
    real_in = jnp.stack([jnp.pad(mixed_wide, extend), jnp.pad(kernel_wide, extend)])
    imag_in = jnp.stack(
        [jnp.pad(gated_wide, extend), jnp.zeros((kernel_wide.shape[0], 2 * length), jnp.float32)]
    )
    freq_real, freq_imag = transform(real_in, imag_in, -1.0)
    packed_real = freq_real[0]
    packed_imag = freq_imag[0]
    mirror_real = jnp.roll(jnp.flip(packed_real, -1), 1, -1)
    mirror_imag = jnp.roll(jnp.flip(packed_imag, -1), 1, -1)
    mix_real = 0.5 * (packed_real + mirror_real)
    mix_imag = 0.5 * (packed_imag - mirror_imag)
    grad_real = 0.5 * (packed_imag + mirror_imag)
    grad_imag = 0.5 * (mirror_real - packed_real)
    kern_real = freq_real[1]
    kern_imag = freq_imag[1]
    conv_real = mix_real * kern_real - mix_imag * kern_imag
    conv_imag = mix_real * kern_imag + mix_imag * kern_real
    corr_real = grad_real * kern_real + grad_imag * kern_imag
    corr_imag = grad_imag * kern_real - grad_real * kern_imag
    cross_real = grad_real * mix_real + grad_imag * mix_imag
    cross_imag = grad_imag * mix_real - grad_real * mix_imag
    back_real = jnp.stack([conv_real - corr_imag, cross_real])
    back_imag = jnp.stack([conv_imag + corr_real, cross_imag])
    time_real, time_imag = transform(back_real, back_imag, 1.0)
    inverse_scale = 1.0 / (2 * length)
    conv_part = time_real[0, :, :length] * inverse_scale
    corr_part = time_imag[0, :, :length] * inverse_scale
    cross_part = time_real[1, :, :length] * inverse_scale
    gain_column = local_gain[:, None]
    long_out = (conv_part + gain_column * mixed_wide).astype(jnp.bfloat16)
    mixed_grad = (corr_part + gain_column * gated_wide).astype(jnp.bfloat16)
    return (long_out, mixed_grad, cross_part.astype(jnp.bfloat16))


def featurize(history, weights, margin, span_count):
    running = weights[:, :, 0:1] * history[:, :, margin : margin + span_count]
    for offset in range(1, margin + 1):
        running = (
            running
            + weights[:, :, offset : offset + 1]
            * history[:, :, margin - offset : margin - offset + span_count]
        )
    return running


def unfeaturize(padded_grad, weights, span_count):
    running = weights[:, :, 0:1] * padded_grad[:, :, 0:span_count]
    for offset in range(1, weights.shape[2]):
        running = (
            running
            + weights[:, :, offset : offset + 1] * padded_grad[:, :, offset : offset + span_count]
        )
    return running


def tap_grads(primed_grad, history, margin, span_count):
    columns = []
    for offset in range(margin + 1):
        columns.append(
            jnp.sum(
                primed_grad * history[:, :, margin - offset : margin - offset + span_count], axis=-1
            )
        )
    return jnp.stack(columns, axis=-1)


def packed_tables(length):
    half, quarter = length // 2, length // 4
    steps = np.arange(half)
    bins = np.arange(length).reshape(quarter, 4).T.reshape(-1)
    phase = (steps[:, None] * bins[None, :]) % (2 * length)
    angles = np.pi / length * phase
    sines = np.sin(angles)
    sines[:, 0] = 1.0 - 2.0 * (steps % 2)
    table = np.concatenate([np.cos(angles), sines], 1)
    weights = np.full(2 * length, 1.0 / length)
    weights[0] = weights[length] = 0.5 / length
    forward = table.T.astype(np.float32)
    high = forward.astype(jnp.bfloat16)
    low = (forward - high.astype(np.float32)).astype(jnp.bfloat16)
    return np.concatenate([high, low], 1), (table * weights).astype(np.float32).astype(jnp.bfloat16)


def fused_kernel(
    sizes,
    feat_hbm,
    cot_hbm,
    filt_hbm,
    short_hbm,
    gain_hbm,
    fwd_hbm,
    back_hbm,
    gated_out,
    grad_out,
    long_out,
    chip_sums,
    late_sums,
    long_in,
    spent,
    raw,
    short,
    gain_line,
    fwd,
    back,
    hist,
    cot,
    primed,
    moving,
    halo_out,
    halo_in,
    edge_out,
    edge_in,
    last_out,
    last_in,
    gate_out,
    mix_out,
    filt_in,
    gate_in,
    mix_in,
    tokens,
    freq,
    pair,
    res_grad,
    res_out,
    res_long,
    got_grad,
    got_out,
    own_sums,
    mate_sums,
    load_sem,
    send_sem,
    recv_sem,
):
    groups, rows, span, length, taps = sizes
    me = lax.axis_index("seq")
    peers = range(1, groups)
    edge = 16
    FILT, GATE, MIX, GRAD, OUT, LONG, MATE, CHIP, LATE, HALO, EDGE, LAST = range(12)
    half, quarter = length // 2, length // 4
    half_groups, twins = groups // 2, groups // 2
    mate = me + 1 - 2 * lax.rem(me, 2)

    def near(step):
        return lax.rem(me + step, groups)

    def block(index, extent, count=1):
        return pl.ds(pl.multiple_of(index * extent, extent), extent * count)

    def lanes(step):
        return block(near(step), rows)

    barrier = pltpu.get_barrier_semaphore()
    for step in peers:
        pl.semaphore_signal(
            barrier,
            inc=1,
            device_id={"seq": near(step)},
            device_id_type=pl.DeviceIdType.MESH,
        )
    pairs = [
        (feat_hbm, raw.at[0:3]),
        (cot_hbm, raw.at[3]),
        (short_hbm, short),
        (gain_hbm, gain_line),
        (filt_hbm.at[lanes(0), :], filt_in.at[0]),
        (fwd_hbm, fwd),
        (back_hbm, back),
    ]
    loads = [
        pltpu.make_async_copy(source, target, load_sem.at[index])
        for index, (source, target) in enumerate(pairs)
    ]
    for index in (2, 0, 1):
        loads[index].start()

    def remote(source, target, kind, peer):
        return pltpu.make_async_remote_copy(
            src_ref=source,
            dst_ref=target,
            send_sem=send_sem.at[kind],
            recv_sem=recv_sem.at[kind],
            device_id={"seq": peer},
            device_id_type=pl.DeviceIdType.MESH,
        )

    def push(kind, source_of, target_of):
        for step in peers:
            remote(source_of(step), target_of(groups - step), kind, near(step)).start()

    def push_rows(kind, source, target, first, count):
        picked = pl.ds(first, count)
        push(
            kind,
            lambda step: source.at[step, picked, :],
            lambda slot: target.at[slot, picked, :],
        )

    def whole(kind, target):
        landed = target.at[1:groups]
        return remote(landed, landed, kind, near(1))

    loads[2].wait()
    loads[0].wait()

    halo_out[...] = jnp.zeros_like(halo_out)
    for step in range(groups):
        for stream in range(3):
            wide = raw[stream, lanes(step), :].T.astype(jnp.float32)
            hist[step, stream, 8:, :] = wide
            halo_out[near(step), 2 * stream : 2 * stream + 2, :] = wide[span - 2 :, :]

    right, left = near(1), near(groups - 1)

    pl.semaphore_wait(barrier, groups - 1)
    @pl.when(me < groups - 1)
    def _():
        remote(halo_out, halo_in, HALO, right).start()

    push(FILT, lambda step: filt_hbm.at[lanes(step), :], lambda slot: filt_in.at[slot])
    for index in (3, 4, 5, 6):
        loads[index].start()

    loads[1].wait()
    for step in range(groups):
        cot[step] = raw[3, lanes(step), :].T.astype(jnp.float32)

    def coef(stream, offset, step):
        return short[stream, offset : offset + 1, lanes(step)]

    def featurize(step, stream, first, count):
        running = coef(stream, 0, step) * hist[step, stream, 8 + first : 8 + first + count, :]
        for offset in range(1, taps):
            start = 8 + first - offset
            running = (
                running
                + coef(stream, offset, step) * hist[step, stream, start : start + count, :]
            )
        primed[step, stream, first : first + count, :] = running
        return running

    def gate(step, first, count):
        value = featurize(step, 0, first, count) * cot[step, first : first + count, :]
        gate_out[step, first : first + count, :] = value.astype(jnp.bfloat16)

    def mix(step, first, count):
        value = featurize(step, 1, first, count) * featurize(step, 2, first, count)
        mix_out[step, first : first + count, :] = value.astype(jnp.bfloat16)

    for step in range(groups):
        gate(step, edge, span - edge)
    push_rows(GATE, gate_out, gate_in, edge, span - edge)
    for step in range(groups):
        mix(step, edge, span - edge)

    @pl.when(me > 0)
    def _():
        remote(halo_in, halo_in, HALO, left).wait_recv()

    @pl.when(me == 0)
    def _():
        halo_in[...] = jnp.zeros_like(halo_in)

    for step in range(groups):
        for stream in range(3):
            hist[step, stream, 6:8, :] = halo_in[near(step), 2 * stream : 2 * stream + 2, :]
        gate(step, 0, edge)
    push_rows(GATE, gate_out, gate_in, 0, edge)
    for step in range(groups):
        mix(step, 0, edge)
    whole(GATE, gate_in).wait_send()
    push_rows(MIX, mix_out, mix_in, 0, span)
    last_out[...] = jnp.zeros_like(last_out)
    moving[:, :, span:, :] = jnp.zeros((3, groups, 8, rows), jnp.float32)
    gate_in[0] = gate_out[0]
    mix_in[0] = mix_out[0]
    own_sums[...] = jnp.zeros_like(own_sums)
    late_sums[0] = jnp.zeros(late_sums.shape[1:], jnp.float32)
    for step in range(groups):
        local = gate_out[step].astype(jnp.float32) * mix_out[step].astype(jnp.float32)
        own_sums[near(step), 2 * taps : 2 * taps + 1, :] = jnp.sum(local, axis=0, keepdims=True)

    def place(kind, step, value):
        position = near(step)
        column = pl.ds(pl.multiple_of(position // half_groups * rows, rows), rows)
        for copy in range(2):
            start = copy * half + lax.rem(position, half_groups) * span
            tokens[kind, pl.ds(pl.multiple_of(start, span), span), column] = value

    def forward(kind):
        for turn in range(4):
            even_rows = slice(turn * quarter, (turn + 1) * quarter)
            odd_rows = slice(length + turn * quarter, length + (turn + 1) * quarter)
            cosines = jnp.dot(fwd[even_rows, :], tokens[kind], preferred_element_type=jnp.float32)
            sines = jnp.dot(fwd[odd_rows, :], tokens[kind], preferred_element_type=jnp.float32)
            even, odd = cosines[:, :rows], sines[:, :rows]
            even_late, odd_late = cosines[:, rows:], sines[:, rows:]
            if turn == 0:
                even, odd = even + even_late, odd + odd_late
            elif turn == 1:
                even, odd = even - odd_late, odd + even_late
            elif turn == 2:
                even, odd = even - even_late, odd - odd_late
            else:
                even, odd = even + odd_late, odd - even_late
            freq[kind, even_rows, :] = even
            freq[kind, odd_rows, :] = odd

    def product(left_kind, right_kind, sign):
        for turn in range(4):
            even_rows = slice(turn * quarter, (turn + 1) * quarter)
            odd_rows = slice(length + turn * quarter, length + (turn + 1) * quarter)
            left_c, left_s = freq[left_kind, even_rows, :], freq[left_kind, odd_rows, :]
            right_c, right_s = freq[right_kind, even_rows, :], freq[right_kind, odd_rows, :]
            both = left_s * right_s
            cross = left_s * right_c - sign * (left_c * right_s)
            if turn == 0:
                first = lax.broadcasted_iota(jnp.int32, (quarter, rows), 0) == 0
                even = left_c * right_c + sign * jnp.where(first, 0.0, both)
                odd = jnp.where(first, both, cross)
            else:
                even = left_c * right_c + sign * both
                odd = cross
            even = even.astype(jnp.bfloat16)
            odd = odd.astype(jnp.bfloat16)
            pair[even_rows, :rows] = even
            pair[odd_rows, :rows] = odd
            late_even, late_odd = ((even, odd), (odd, -even), (-even, -odd), (-odd, even))[turn]
            pair[even_rows, rows:] = late_even
            pair[odd_rows, rows:] = late_odd

    def finish(kind, result):
        total = jnp.dot(back[...], pair[...], preferred_element_type=jnp.float32)
        if kind is not None:
            total = total + wide_gain * tokens[kind, :half, :].astype(jnp.float32)
        total = total.astype(jnp.bfloat16)
        result[:half, :] = total[:, :rows]
        result[half:, :] = total[:, rows:]

    gates, mixes, kernels = range(3)

    loads[3].wait()
    loads[4].wait()
    loads[5].wait()
    gain = gain_line[:, lanes(0)]
    wide_gain = jnp.concatenate([gain, gain], 1)

    whole(FILT, filt_in).wait_recv()
    for step in range(groups):
        place(kernels, step, filt_in[step].T)
    forward(kernels)

    whole(GATE, gate_in).wait_recv()
    for step in range(groups):
        place(gates, step, gate_in[step])
    forward(gates)
    product(gates, kernels, 1.0)
    loads[6].wait()
    finish(gates, res_grad)

    def spread(kind, result, target):
        def taken(step):
            return block(near(step), span)

        push(kind, lambda step: result.at[taken(step), :], lambda slot: target.at[slot])
        target[0] = result[taken(0), :]

    spread(GRAD, res_grad, got_grad)

    whole(MIX, mix_in).wait_recv()
    for step in range(groups):
        place(mixes, step, mix_in[step])
    forward(mixes)
    product(mixes, kernels, -1.0)
    finish(mixes, res_out)
    spread(OUT, res_out, got_out)

    product(gates, mixes, 1.0)
    finish(None, res_long)
    def tally(step, stream, sums, row):
        for offset in range(taps):
            start = 8 - offset
            total = jnp.sum(
                moving[stream, step, 0:span, :] * hist[step, stream, start : start + span, :],
                axis=0,
                keepdims=True,
            )
            sums[near(step), row + offset : row + offset + 1, :] = total

    def spend(step, stream, first, count):
        running = coef(stream, 0, step) * moving[stream, step, first : first + count, :]
        for offset in range(1, taps):
            start = first + offset
            running = (
                running
                + coef(stream, offset, step) * moving[stream, step, start : start + count, :]
            )
        spent[stream, step, first : first + count, :] = running.astype(jnp.bfloat16)

    def hand_left(kind, source, target):
        @pl.when(me > 0)
        def _():
            remote(source, target, kind, left).start()

    def complete(kind, source, target, streams):
        @pl.when(me < groups - 1)
        def _():
            remote(target, target, kind, right).wait_recv()
            for step in range(groups):
                for place_of, stream in enumerate(streams):
                    taken = target[near(step), 2 * place_of : 2 * place_of + 2, :]
                    moving[stream, step, span : span + 2, :] = taken

        for step in range(groups):
            for stream in streams:
                spend(step, stream, span - edge, edge)
                grad_out[stream, lanes(step), :] = spent[stream, step].T

        @pl.when(me > 0)
        def _():
            remote(source, target, kind, left).wait_send()

    whole(GRAD, got_grad).wait_recv()
    for step in range(groups):
        mixed_back = got_grad[step].astype(jnp.float32)
        moving[1, step, 0:span, :] = mixed_back * primed[step, 2, :, :]
        moving[2, step, 0:span, :] = mixed_back * primed[step, 1, :, :]
        edge_out[near(step), 0:2, :] = moving[1, step, 0:2, :]
        edge_out[near(step), 2:4, :] = moving[2, step, 0:2, :]
        tally(step, 1, own_sums, 0)
        tally(step, 2, own_sums, taps)
    remote(own_sums, mate_sums, MATE, mate).start()
    spread(LONG, res_long, long_in)
    hand_left(EDGE, edge_out, edge_in)
    for step in range(groups):
        spend(step, 1, 0, span - edge)
        spend(step, 2, 0, span - edge)
    remote(own_sums, mate_sums, MATE, mate).wait_recv()
    chip_sums[0] = own_sums[...] + mate_sums[...]
    for twin in range(1, twins):
        remote(chip_sums.at[0], chip_sums.at[twins - twin], CHIP, near(2 * twin)).start()

    whole(OUT, got_out).wait_recv()
    for step in range(groups):
        moving[0, step, 0:span, :] = got_out[step].astype(jnp.float32) * cot[step]
        last_out[near(step), 0:2, :] = moving[0, step, 0:2, :]
        tally(step, 0, late_sums.at[0], 0)
    push(LATE, lambda step: late_sums.at[0], lambda slot: late_sums.at[slot])
    hand_left(LAST, last_out, last_in)
    for step in range(groups):
        gated = primed[step, 0, :, :] * got_out[step].astype(jnp.float32)
        gated_out[lanes(step), :] = gated.astype(jnp.bfloat16).T
        spend(step, 0, 0, span - edge)

    complete(EDGE, edge_out, edge_in, (1, 2))
    complete(LAST, last_out, last_in, (0,))
    whole(LONG, long_in).wait_recv()
    for step in range(groups):
        long_out[lanes(step), :] = long_in[step].T
    others = chip_sums.at[1:twins]
    remote(others, others, CHIP, near(2)).wait_recv()
    whole(LATE, late_sums).wait_recv()
    remote(own_sums, mate_sums, MATE, mate).wait_send()
    remote(others, others, CHIP, near(2)).wait_send()

    @pl.when(me < groups - 1)
    def _():
        remote(halo_out, halo_in, HALO, right).wait_send()

    for kind, target in (
        (FILT, filt_in),
        (MIX, mix_in),
        (GRAD, got_grad),
        (OUT, got_out),
        (LONG, long_in),
        (LATE, late_sums),
    ):
        whole(kind, target).wait_send()


def settle_kernel(
    sizes, gated, grad, long, chip_sums, late_sums, gated_hbm, grad_hbm, long_hbm, taps_hbm, skip_hbm,
    taps_line, skip_line, done,
):
    groups, rows, span, taps = sizes
    twins = groups // 2
    me = lax.axis_index("seq")
    copies = []

    def start(source, target):
        copy = pltpu.make_async_copy(source, target, done.at[len(copies)])
        copy.start()
        copies.append(copy)

    start(grad, grad_hbm)
    start(gated, gated_hbm)
    start(long, long_hbm)
    for group in range(groups):
        picked = slice(group * rows, (group + 1) * rows)
        early = late = None
        for source in range(groups):
            value = late_sums[lax.rem(source + groups - me, groups), group]
            late = value if late is None else late + value
        for source in range(twins):
            value = chip_sums[lax.rem(source + twins - me // 2, twins), group]
            early = value if early is None else early + value
        taps_line[0, :, picked] = late[:taps]
        taps_line[1, :, picked] = early[:taps]
        taps_line[2, :, picked] = early[taps : 2 * taps]
        skip_line[:, picked] = early[2 * taps : 2 * taps + 1]
    start(taps_line, taps_hbm)
    start(skip_line, skip_hbm)
    for copy in copies:
        copy.wait()


def fused(features, cotangent, long_filter, short_filters, skip_gain, groups):
    channels, span = cotangent.shape
    rows = channels // groups
    length = span * groups
    taps = short_filters.shape[2]
    hbm = pl.BlockSpec(memory_space=pltpu.HBM)
    vmem = pl.BlockSpec(memory_space=pltpu.VMEM)
    dma = pltpu.SemaphoreType.DMA
    narrow, wide = jnp.bfloat16, jnp.float32
    kinds = 12
    forward_table, back_table = packed_tables(length)
    middle = pl.pallas_call(
        functools.partial(fused_kernel, (groups, rows, span, length, taps)),
        out_shape=(
            pltpu.VMEM((channels, span), narrow),
            pltpu.VMEM((3, channels, span), narrow),
            pltpu.VMEM((channels, span), narrow),
            pltpu.VMEM((groups // 2, groups, 8, rows), wide),
            pltpu.VMEM((groups, groups, 4, rows), wide),
        ),
        in_specs=[hbm] * 7,
        out_specs=(vmem,) * 5,
        scratch_shapes=[
            pltpu.VMEM((groups, span, rows), narrow),
            pltpu.VMEM((3, groups, span, rows), narrow),
            pltpu.VMEM((4, channels, span), narrow),
            pltpu.VMEM((3, taps, channels), wide),
            pltpu.VMEM((1, channels), wide),
            pltpu.VMEM((2 * length, length), narrow),
            pltpu.VMEM((length // 2, 2 * length), narrow),
            pltpu.VMEM((groups, 3, span + 8, rows), wide),
            pltpu.VMEM((groups, span, rows), wide),
            pltpu.VMEM((groups, 3, span, rows), wide),
            pltpu.VMEM((3, groups, span + 8, rows), wide),
            pltpu.VMEM((groups, 8, rows), wide),
            pltpu.VMEM((groups, 8, rows), wide),
            pltpu.VMEM((groups, 4, rows), wide),
            pltpu.VMEM((groups, 4, rows), wide),
            pltpu.VMEM((groups, 4, rows), wide),
            pltpu.VMEM((groups, 4, rows), wide),
            pltpu.VMEM((groups, span, rows), narrow),
            pltpu.VMEM((groups, span, rows), narrow),
            pltpu.VMEM((groups, rows, span), narrow),
            pltpu.VMEM((groups, span, rows), narrow),
            pltpu.VMEM((groups, span, rows), narrow),
            pltpu.VMEM((3, length, 2 * rows), narrow),
            pltpu.VMEM((3, 2 * length, rows), wide),
            pltpu.VMEM((2 * length, 2 * rows), narrow),
            pltpu.VMEM((length, rows), narrow),
            pltpu.VMEM((length, rows), narrow),
            pltpu.VMEM((length, rows), narrow),
            pltpu.VMEM((groups, span, rows), narrow),
            pltpu.VMEM((groups, span, rows), narrow),
            pltpu.VMEM((groups, 8, rows), wide),
            pltpu.VMEM((groups, 8, rows), wide),
            dma((7,)),
            dma((kinds,)),
            dma((kinds,)),
        ],
        compiler_params=pltpu.CompilerParams(
            collective_id=0, has_side_effects=True, vmem_limit_bytes=40 * 2**20
        ),
    )(
        *[
            pltpu.with_memory_space_constraint(value, pltpu.HBM)
            for value in (
                features,
                cotangent,
                long_filter,
                jnp.swapaxes(short_filters, 1, 2),
                skip_gain[None],
                jnp.asarray(forward_table),
                jnp.asarray(back_table),
            )
        ]
    )
    gated_out, feature_grad, long_grad, taps_grad, gain_grad = pl.pallas_call(
        functools.partial(settle_kernel, (groups, rows, span, taps)),
        out_shape=(
            jax.ShapeDtypeStruct((channels, span), narrow),
            jax.ShapeDtypeStruct((3, channels, span), narrow),
            jax.ShapeDtypeStruct((channels, span), narrow),
            jax.ShapeDtypeStruct((3, taps, channels), wide),
            jax.ShapeDtypeStruct((1, channels), wide),
        ),
        in_specs=[vmem] * 5,
        out_specs=(hbm,) * 5,
        scratch_shapes=[
            pltpu.VMEM((3, taps, channels), wide),
            pltpu.VMEM((1, channels), wide),
            dma((5,)),
        ],
    )(*[pltpu.with_memory_space_constraint(value, pltpu.VMEM) for value in middle])
    return gated_out, feature_grad, long_grad, jnp.swapaxes(taps_grad, 1, 2), gain_grad[0]


def dense_fits(features, short_filters, groups):
    channels, span = features.shape[1:]
    rows, length = channels // groups, span * groups
    return (
        channels % groups == 0
        and groups % 2 == 0
        and groups > 2
        and rows == 128
        and span == 128
        and length % 512 == 0
        and length <= 1024
        and 2 <= short_filters.shape[2] <= 3
    )


def shards(features, cotangent, long_filter, short_filters, skip_gain):
    groups = lax.axis_size("seq")
    if dense_fits(features, short_filters, groups):
        return fused(features, cotangent, long_filter, short_filters, skip_gain, groups)
    seq_index = lax.axis_index("seq")
    channels = features.shape[1]
    per_group = channels // groups
    margin = short_filters.shape[2] - 1
    local_gain = lax.dynamic_slice_in_dim(skip_gain, seq_index * per_group, per_group, 0)
    stacked = jnp.concatenate([features, cotangent[None], long_filter[None]], 0)
    columns = lax.all_to_all(stacked, "seq", split_axis=1, concat_axis=2, tiled=True)
    weights = lax.dynamic_slice_in_dim(short_filters, seq_index * per_group, per_group, 1)
    length = columns.shape[2]
    history = jnp.pad(columns[:3].astype(jnp.float32), ((0, 0), (0, 0), (margin, 0)))
    primed = featurize(history, weights, margin, length)
    mixed_term = (primed[1] * primed[2]).astype(jnp.bfloat16)
    cot_wide = columns[3].astype(jnp.float32)
    gated_grad = (cot_wide * primed[0]).astype(jnp.bfloat16)
    long_out, mixed_grad, kernel_grad = spectral(mixed_term, gated_grad, columns[4], local_gain)
    long_wide = long_out.astype(jnp.float32)
    mixed_back = mixed_grad.astype(jnp.float32)
    gated_out = (primed[0] * long_wide).astype(jnp.bfloat16)
    primed_grad = jnp.stack([cot_wide * long_wide, mixed_back * primed[2], mixed_back * primed[1]])
    padded_grad = jnp.pad(primed_grad, ((0, 0), (0, 0), (0, margin)))
    feature_grad = unfeaturize(padded_grad, weights, length).astype(jnp.bfloat16)
    taps_grad = tap_grads(primed_grad, history, margin, length)
    gain_grad = jnp.sum(gated_grad.astype(jnp.float32) * mixed_term.astype(jnp.float32), axis=-1)
    results = jnp.concatenate([gated_out[None], feature_grad, kernel_grad[None]], 0)
    row_blocks = lax.all_to_all(results, "seq", split_axis=2, concat_axis=1, tiled=True)
    short_grad, skip_grad = (
        lax.all_gather(taps_grad, "seq", axis=1, tiled=True),
        lax.all_gather(gain_grad, "seq", axis=0, tiled=True),
    )
    return (row_blocks[0], row_blocks[1:4], row_blocks[4], short_grad, skip_grad)


def solution(mesh):
    placed = (
        P(None, "chan", "seq"),
        P("chan", "seq"),
        P("chan", "seq"),
        P(None, "chan", None),
        P("chan"),
    )
    return jax.shard_map(
        shards,
        mesh=mesh,
        in_specs=placed,
        out_specs=(
            P("chan", "seq"),
            P(None, "chan", "seq"),
            P("chan", "seq"),
            P(None, "chan", None),
            P("chan"),
        ),
        check_vma=False,
    )
```

```python
import functools
import math

import jax
import jax.numpy as jnp
import numpy as np
from jax import lax
from jax.experimental import pallas as pl
from jax.experimental.pallas import tpu as pltpu
from jax.sharding import PartitionSpec as P

inner_length = 128
radix_width = 8


def phase_tables(row_count, col_count, length, direction):
    phase_index = (
        lax.iota(jnp.int32, row_count)[:, None] * lax.iota(jnp.int32, col_count)[None, :] % length
    )
    angles = direction * 2.0 * math.pi / length * phase_index.astype(jnp.float32)
    return (jnp.cos(angles), jnp.sin(angles))


def last_axis(operand, matrix):
    return jnp.einsum("...n,nk->...k", operand, matrix, precision=lax.Precision.HIGH)


def first_axis(operand, matrix):
    return jnp.einsum("...ab,ak->...kb", operand, matrix, precision=lax.Precision.HIGH)


def transform(real_part, imag_part, direction):
    length = real_part.shape[-1]
    if length <= inner_length or length % radix_width != 0:
        cos_table, sin_table = phase_tables(length, length, length, direction)
        return (
            last_axis(real_part, cos_table) - last_axis(imag_part, sin_table),
            last_axis(real_part, sin_table) + last_axis(imag_part, cos_table),
        )
    rest_length = length // radix_width
    grid_shape = real_part.shape[:-1] + (radix_width, rest_length)
    real_grid = real_part.reshape(grid_shape)
    imag_grid = imag_part.reshape(grid_shape)
    cos_table, sin_table = phase_tables(radix_width, radix_width, radix_width, direction)
    section_real = first_axis(real_grid, cos_table) - first_axis(imag_grid, sin_table)
    section_imag = first_axis(real_grid, sin_table) + first_axis(imag_grid, cos_table)
    twist_cos, twist_sin = phase_tables(radix_width, rest_length, length, direction)
    turned_real = section_real * twist_cos - section_imag * twist_sin
    turned_imag = section_real * twist_sin + section_imag * twist_cos
    inner_real, inner_imag = transform(turned_real, turned_imag, direction)
    return (
        jnp.swapaxes(inner_real, -1, -2).reshape(real_part.shape),
        jnp.swapaxes(inner_imag, -1, -2).reshape(real_part.shape),
    )


def spectral(mixed_term, gated_grad, kernel, local_gain):
    length = mixed_term.shape[-1]
    mixed_wide = mixed_term.astype(jnp.float32)
    gated_wide = gated_grad.astype(jnp.float32)
    kernel_wide = kernel.astype(jnp.float32)
    extend = ((0, 0), (0, length))
    real_in = jnp.stack([jnp.pad(mixed_wide, extend), jnp.pad(kernel_wide, extend)])
    imag_in = jnp.stack(
        [jnp.pad(gated_wide, extend), jnp.zeros((kernel_wide.shape[0], 2 * length), jnp.float32)]
    )
    freq_real, freq_imag = transform(real_in, imag_in, -1.0)
    packed_real = freq_real[0]
    packed_imag = freq_imag[0]
    mirror_real = jnp.roll(jnp.flip(packed_real, -1), 1, -1)
    mirror_imag = jnp.roll(jnp.flip(packed_imag, -1), 1, -1)
    mix_real = 0.5 * (packed_real + mirror_real)
    mix_imag = 0.5 * (packed_imag - mirror_imag)
    grad_real = 0.5 * (packed_imag + mirror_imag)
    grad_imag = 0.5 * (mirror_real - packed_real)
    kern_real = freq_real[1]
    kern_imag = freq_imag[1]
    conv_real = mix_real * kern_real - mix_imag * kern_imag
    conv_imag = mix_real * kern_imag + mix_imag * kern_real
    corr_real = grad_real * kern_real + grad_imag * kern_imag
    corr_imag = grad_imag * kern_real - grad_real * kern_imag
    cross_real = grad_real * mix_real + grad_imag * mix_imag
    cross_imag = grad_imag * mix_real - grad_real * mix_imag
    back_real = jnp.stack([conv_real - corr_imag, cross_real])
    back_imag = jnp.stack([conv_imag + corr_real, cross_imag])
    time_real, time_imag = transform(back_real, back_imag, 1.0)
    inverse_scale = 1.0 / (2 * length)
    conv_part = time_real[0, :, :length] * inverse_scale
    corr_part = time_imag[0, :, :length] * inverse_scale
    cross_part = time_real[1, :, :length] * inverse_scale
    gain_column = local_gain[:, None]
    long_out = (conv_part + gain_column * mixed_wide).astype(jnp.bfloat16)
    mixed_grad = (corr_part + gain_column * gated_wide).astype(jnp.bfloat16)
    return (long_out, mixed_grad, cross_part.astype(jnp.bfloat16))


def featurize(history, weights, margin, span_count):
    running = weights[:, :, 0:1] * history[:, :, margin : margin + span_count]
    for offset in range(1, margin + 1):
        running = (
            running
            + weights[:, :, offset : offset + 1]
            * history[:, :, margin - offset : margin - offset + span_count]
        )
    return running


def unfeaturize(padded_grad, weights, span_count):
    running = weights[:, :, 0:1] * padded_grad[:, :, 0:span_count]
    for offset in range(1, weights.shape[2]):
        running = (
            running
            + weights[:, :, offset : offset + 1] * padded_grad[:, :, offset : offset + span_count]
        )
    return running


def tap_grads(primed_grad, history, margin, span_count):
    columns = []
    for offset in range(margin + 1):
        columns.append(
            jnp.sum(
                primed_grad * history[:, :, margin - offset : margin - offset + span_count], axis=-1
            )
        )
    return jnp.stack(columns, axis=-1)


def packed_tables(length):
    half, quarter = length // 2, length // 4
    steps = np.arange(half)
    bins = np.arange(length).reshape(quarter, 4).T.reshape(-1)
    phase = (steps[:, None] * bins[None, :]) % (2 * length)
    angles = np.pi / length * phase
    sines = np.sin(angles)
    sines[:, 0] = 1.0 - 2.0 * (steps % 2)
    table = np.concatenate([np.cos(angles), sines], 1)
    weights = np.full(2 * length, 1.0 / length)
    weights[0] = weights[length] = 0.5 / length
    forward = table.T.astype(np.float32)
    high = forward.astype(jnp.bfloat16)
    low = (forward - high.astype(np.float32)).astype(jnp.bfloat16)
    return np.concatenate([high, low], 1), (table * weights).astype(np.float32).astype(jnp.bfloat16)


def fused_kernel(
    sizes,
    feat_hbm,
    cot_hbm,
    filt_hbm,
    short_hbm,
    gain_hbm,
    fwd_hbm,
    back_hbm,
    gated_out,
    grad_out,
    long_out,
    chip_sums,
    late_sums,
    long_in,
    spent,
    filt_raw,
    raw,
    short,
    gain_line,
    fwd,
    back,
    hist,
    cot,
    primed,
    moving,
    halo_out,
    halo_in,
    edge_out,
    edge_in,
    last_out,
    last_in,
    gate_out,
    mix_out,
    filt_in,
    gate_in,
    mix_in,
    tokens,
    freq,
    pair,
    res_grad,
    res_out,
    res_long,
    got_grad,
    got_out,
    own_sums,
    mate_sums,
    load_sem,
    send_sem,
    recv_sem,
):
    groups, rows, span, length, taps = sizes
    me = lax.axis_index("seq")
    peers = (2, 1, *range(3, groups))
    edge = 16
    FILT, GATE, MIX, GRAD, OUT, LONG, MATE, CHIP, LATE, HALO, EDGE, LAST = range(12)
    half, quarter = length // 2, length // 4
    half_groups, twins = groups // 2, groups // 2
    mate = me + 1 - 2 * lax.rem(me, 2)

    def near(step):
        return lax.rem(me + step, groups)

    def block(index, extent, count=1):
        return pl.ds(pl.multiple_of(index * extent, extent), extent * count)

    def lanes(step):
        return block(near(step), rows)

    barrier = pltpu.get_barrier_semaphore()
    for step in peers:
        pl.semaphore_signal(
            barrier,
            inc=1,
            device_id={"seq": near(step)},
            device_id_type=pl.DeviceIdType.MESH,
        )
    pairs = [
        (feat_hbm, raw.at[0:3]),
        (cot_hbm, raw.at[3]),
        (short_hbm, short),
        (gain_hbm, gain_line),
        (filt_hbm, filt_raw),
        (fwd_hbm, fwd),
        (back_hbm, back),
    ]
    loads = [
        pltpu.make_async_copy(source, target, load_sem.at[index])
        for index, (source, target) in enumerate(pairs)
    ]
    for index in (2, 0, 4, 1, 3, 5, 6):
        loads[index].start()

    def remote(source, target, kind, peer):
        return pltpu.make_async_remote_copy(
            src_ref=source,
            dst_ref=target,
            send_sem=send_sem.at[kind],
            recv_sem=recv_sem.at[kind],
            device_id={"seq": peer},
            device_id_type=pl.DeviceIdType.MESH,
        )

    def push(kind, source_of, target_of):
        for step in peers:
            remote(source_of(step), target_of(groups - step), kind, near(step)).start()

    def push_rows(kind, source, target, first, count):
        picked = pl.ds(first, count)
        push(
            kind,
            lambda step: source.at[step, picked, :],
            lambda slot: target.at[slot, picked, :],
        )

    def whole(kind, target):
        landed = target.at[1:groups]
        return remote(landed, landed, kind, near(1))

    loads[2].wait()
    loads[0].wait()

    halo_out[...] = jnp.zeros_like(halo_out)
    for step in range(groups):
        for stream in range(3):
            wide = raw[stream, lanes(step), :].T.astype(jnp.float32)
            hist[step, stream, 8:, :] = wide
            halo_out[near(step), 2 * stream : 2 * stream + 2, :] = wide[span - 2 :, :]

    right, left = near(1), near(groups - 1)

    pl.semaphore_wait(barrier, groups - 1)
    @pl.when(me < groups - 1)
    def _():
        remote(halo_out, halo_in, HALO, right).start()

    loads[4].wait()
    push(FILT, lambda step: filt_raw.at[lanes(step), :], lambda slot: filt_in.at[slot])

    loads[1].wait()
    for step in range(groups):
        cot[step] = raw[3, lanes(step), :].T.astype(jnp.float32)

    def coef(stream, offset, step):
        return short[stream, offset : offset + 1, lanes(step)]

    def featurize(step, stream, first, count):
        running = coef(stream, 0, step) * hist[step, stream, 8 + first : 8 + first + count, :]
        for offset in range(1, taps):
            start = 8 + first - offset
            running = (
                running
                + coef(stream, offset, step) * hist[step, stream, start : start + count, :]
            )
        primed[step, stream, first : first + count, :] = running
        return running

    def gate(step, first, count):
        value = featurize(step, 0, first, count) * cot[step, first : first + count, :]
        gate_out[step, first : first + count, :] = value.astype(jnp.bfloat16)

    def mix(step, first, count):
        value = featurize(step, 1, first, count) * featurize(step, 2, first, count)
        mix_out[step, first : first + count, :] = value.astype(jnp.bfloat16)

    for step in range(groups):
        gate(step, edge, span - edge)
    push_rows(GATE, gate_out, gate_in, edge, span - edge)
    for step in range(groups):
        mix(step, edge, span - edge)

    @pl.when(me > 0)
    def _():
        remote(halo_in, halo_in, HALO, left).wait_recv()

    @pl.when(me == 0)
    def _():
        halo_in[...] = jnp.zeros_like(halo_in)

    for step in range(groups):
        for stream in range(3):
            hist[step, stream, 6:8, :] = halo_in[near(step), 2 * stream : 2 * stream + 2, :]
        gate(step, 0, edge)
    push_rows(GATE, gate_out, gate_in, 0, edge)
    for step in range(groups):
        mix(step, 0, edge)
    whole(GATE, gate_in).wait_send()
    push_rows(MIX, mix_out, mix_in, 0, span)
    last_out[...] = jnp.zeros_like(last_out)
    moving[:, :, span:, :] = jnp.zeros((3, groups, 8, rows), jnp.float32)
    gate_in[0] = gate_out[0]
    mix_in[0] = mix_out[0]
    own_sums[...] = jnp.zeros_like(own_sums)
    late_sums[0] = jnp.zeros(late_sums.shape[1:], jnp.float32)
    for step in range(groups):
        local = gate_out[step].astype(jnp.float32) * mix_out[step].astype(jnp.float32)
        own_sums[near(step), 2 * taps : 2 * taps + 1, :] = jnp.sum(local, axis=0, keepdims=True)

    def place(kind, step, value):
        position = near(step)
        column = pl.ds(pl.multiple_of(position // half_groups * rows, rows), rows)
        for copy in range(2):
            start = copy * half + lax.rem(position, half_groups) * span
            tokens[kind, pl.ds(pl.multiple_of(start, span), span), column] = value

    def forward(kind):
        for turn in range(4):
            even_rows = slice(turn * quarter, (turn + 1) * quarter)
            odd_rows = slice(length + turn * quarter, length + (turn + 1) * quarter)
            cosines = jnp.dot(fwd[even_rows, :], tokens[kind], preferred_element_type=jnp.float32)
            sines = jnp.dot(fwd[odd_rows, :], tokens[kind], preferred_element_type=jnp.float32)
            even, odd = cosines[:, :rows], sines[:, :rows]
            even_late, odd_late = cosines[:, rows:], sines[:, rows:]
            if turn == 0:
                even, odd = even + even_late, odd + odd_late
            elif turn == 1:
                even, odd = even - odd_late, odd + even_late
            elif turn == 2:
                even, odd = even - even_late, odd - odd_late
            else:
                even, odd = even + odd_late, odd - even_late
            freq[kind, even_rows, :] = even
            freq[kind, odd_rows, :] = odd

    def product(left_kind, right_kind, sign):
        for turn in range(4):
            even_rows = slice(turn * quarter, (turn + 1) * quarter)
            odd_rows = slice(length + turn * quarter, length + (turn + 1) * quarter)
            left_c, left_s = freq[left_kind, even_rows, :], freq[left_kind, odd_rows, :]
            right_c, right_s = freq[right_kind, even_rows, :], freq[right_kind, odd_rows, :]
            both = left_s * right_s
            cross = left_s * right_c - sign * (left_c * right_s)
            if turn == 0:
                first = lax.broadcasted_iota(jnp.int32, (quarter, rows), 0) == 0
                even = left_c * right_c + sign * jnp.where(first, 0.0, both)
                odd = jnp.where(first, both, cross)
            else:
                even = left_c * right_c + sign * both
                odd = cross
            even = even.astype(jnp.bfloat16)
            odd = odd.astype(jnp.bfloat16)
            pair[even_rows, :rows] = even
            pair[odd_rows, :rows] = odd
            late_even, late_odd = ((even, odd), (odd, -even), (-even, -odd), (-odd, even))[turn]
            pair[even_rows, rows:] = late_even
            pair[odd_rows, rows:] = late_odd

    def finish(kind, result):
        total = jnp.dot(back[...], pair[...], preferred_element_type=jnp.float32)
        if kind is not None:
            total = total + wide_gain * tokens[kind, :half, :].astype(jnp.float32)
        total = total.astype(jnp.bfloat16)
        result[:half, :] = total[:, :rows]
        result[half:, :] = total[:, rows:]

    gates, mixes, kernels = range(3)

    loads[3].wait()
    filt_in[0] = filt_raw[lanes(0), :]
    loads[5].wait()
    gain = gain_line[:, lanes(0)]
    wide_gain = jnp.concatenate([gain, gain], 1)

    whole(FILT, filt_in).wait_recv()
    for step in range(groups):
        place(kernels, step, filt_in[step].T)
    forward(kernels)

    whole(GATE, gate_in).wait_recv()
    for step in range(groups):
        place(gates, step, gate_in[step])
    forward(gates)
    product(gates, kernels, 1.0)
    loads[6].wait()
    finish(gates, res_grad)

    def spread(kind, result, target):
        def taken(step):
            return block(near(step), span)

        push(kind, lambda step: result.at[taken(step), :], lambda slot: target.at[slot])
        target[0] = result[taken(0), :]

    spread(GRAD, res_grad, got_grad)

    whole(MIX, mix_in).wait_recv()
    for step in range(groups):
        place(mixes, step, mix_in[step])
    forward(mixes)
    product(mixes, kernels, -1.0)
    finish(mixes, res_out)
    spread(OUT, res_out, got_out)

    product(gates, mixes, 1.0)
    finish(None, res_long)
    def tally(step, stream, sums, row):
        for offset in range(taps):
            start = 8 - offset
            total = jnp.sum(
                moving[stream, step, 0:span, :] * hist[step, stream, start : start + span, :],
                axis=0,
                keepdims=True,
            )
            sums[near(step), row + offset : row + offset + 1, :] = total

    def spend(step, stream, first, count):
        running = coef(stream, 0, step) * moving[stream, step, first : first + count, :]
        for offset in range(1, taps):
            start = first + offset
            running = (
                running
                + coef(stream, offset, step) * moving[stream, step, start : start + count, :]
            )
        spent[stream, step, first : first + count, :] = running.astype(jnp.bfloat16)

    def hand_left(kind, source, target):
        @pl.when(me > 0)
        def _():
            remote(source, target, kind, left).start()

    def complete(kind, source, target, streams):
        @pl.when(me < groups - 1)
        def _():
            remote(target, target, kind, right).wait_recv()
            for step in range(groups):
                for place_of, stream in enumerate(streams):
                    taken = target[near(step), 2 * place_of : 2 * place_of + 2, :]
                    moving[stream, step, span : span + 2, :] = taken

        for step in range(groups):
            for stream in streams:
                spend(step, stream, span - edge, edge)
                grad_out[stream, lanes(step), :] = spent[stream, step].T

        @pl.when(me > 0)
        def _():
            remote(source, target, kind, left).wait_send()

    whole(GRAD, got_grad).wait_recv()
    for step in range(groups):
        mixed_back = got_grad[step].astype(jnp.float32)
        moving[1, step, 0:span, :] = mixed_back * primed[step, 2, :, :]
        moving[2, step, 0:span, :] = mixed_back * primed[step, 1, :, :]
        edge_out[near(step), 0:2, :] = moving[1, step, 0:2, :]
        edge_out[near(step), 2:4, :] = moving[2, step, 0:2, :]
        tally(step, 1, own_sums, 0)
        tally(step, 2, own_sums, taps)
    remote(own_sums, mate_sums, MATE, mate).start()
    spread(LONG, res_long, long_in)
    hand_left(EDGE, edge_out, edge_in)
    for step in range(groups):
        spend(step, 1, 0, span - edge)
        spend(step, 2, 0, span - edge)
    remote(own_sums, mate_sums, MATE, mate).wait_recv()
    chip_sums[0] = own_sums[...] + mate_sums[...]
    for twin in range(1, twins):
        remote(chip_sums.at[0], chip_sums.at[twins - twin], CHIP, near(2 * twin)).start()

    whole(OUT, got_out).wait_recv()
    for step in range(groups):
        moving[0, step, 0:span, :] = got_out[step].astype(jnp.float32) * cot[step]
        last_out[near(step), 0:2, :] = moving[0, step, 0:2, :]
        tally(step, 0, late_sums.at[0], 0)
    push(LATE, lambda step: late_sums.at[0], lambda slot: late_sums.at[slot])
    hand_left(LAST, last_out, last_in)
    for step in range(groups):
        gated = primed[step, 0, :, :] * got_out[step].astype(jnp.float32)
        gated_out[lanes(step), :] = gated.astype(jnp.bfloat16).T
        spend(step, 0, 0, span - edge)

    complete(EDGE, edge_out, edge_in, (1, 2))
    complete(LAST, last_out, last_in, (0,))
    whole(LONG, long_in).wait_recv()
    for step in range(groups):
        long_out[lanes(step), :] = long_in[step].T
    others = chip_sums.at[1:twins]
    remote(others, others, CHIP, near(2)).wait_recv()
    whole(LATE, late_sums).wait_recv()
    remote(own_sums, mate_sums, MATE, mate).wait_send()
    remote(others, others, CHIP, near(2)).wait_send()

    @pl.when(me < groups - 1)
    def _():
        remote(halo_out, halo_in, HALO, right).wait_send()

    for kind, target in (
        (FILT, filt_in),
        (MIX, mix_in),
        (GRAD, got_grad),
        (OUT, got_out),
        (LONG, long_in),
        (LATE, late_sums),
    ):
        whole(kind, target).wait_send()


def settle_kernel(
    sizes, gated, grad, long, chip_sums, late_sums, gated_hbm, grad_hbm, long_hbm, taps_hbm, skip_hbm,
    taps_line, skip_line, done,
):
    groups, rows, span, taps = sizes
    twins = groups // 2
    me = lax.axis_index("seq")
    copies = []

    def start(source, target):
        copy = pltpu.make_async_copy(source, target, done.at[len(copies)])
        copy.start()
        copies.append(copy)

    start(grad, grad_hbm)
    start(gated, gated_hbm)
    start(long, long_hbm)
    for group in range(groups):
        picked = slice(group * rows, (group + 1) * rows)
        early = late = None
        for source in range(groups):
            value = late_sums[lax.rem(source + groups - me, groups), group]
            late = value if late is None else late + value
        for source in range(twins):
            value = chip_sums[lax.rem(source + twins - me // 2, twins), group]
            early = value if early is None else early + value
        taps_line[0, :, picked] = late[:taps]
        taps_line[1, :, picked] = early[:taps]
        taps_line[2, :, picked] = early[taps : 2 * taps]
        skip_line[:, picked] = early[2 * taps : 2 * taps + 1]
    start(taps_line, taps_hbm)
    start(skip_line, skip_hbm)
    for copy in copies:
        copy.wait()


def fused(features, cotangent, long_filter, short_filters, skip_gain, groups):
    channels, span = cotangent.shape
    rows = channels // groups
    length = span * groups
    taps = short_filters.shape[2]
    hbm = pl.BlockSpec(memory_space=pltpu.HBM)
    vmem = pl.BlockSpec(memory_space=pltpu.VMEM)
    dma = pltpu.SemaphoreType.DMA
    narrow, wide = jnp.bfloat16, jnp.float32
    kinds = 12
    forward_table, back_table = packed_tables(length)
    middle = pl.pallas_call(
        functools.partial(fused_kernel, (groups, rows, span, length, taps)),
        out_shape=(
            pltpu.VMEM((channels, span), narrow),
            pltpu.VMEM((3, channels, span), narrow),
            pltpu.VMEM((channels, span), narrow),
            pltpu.VMEM((groups // 2, groups, 8, rows), wide),
            pltpu.VMEM((groups, groups, 4, rows), wide),
        ),
        in_specs=[hbm] * 7,
        out_specs=(vmem,) * 5,
        scratch_shapes=[
            pltpu.VMEM((groups, span, rows), narrow),
            pltpu.VMEM((3, groups, span, rows), narrow),
            pltpu.VMEM((channels, span), narrow),
            pltpu.VMEM((4, channels, span), narrow),
            pltpu.VMEM((3, taps, channels), wide),
            pltpu.VMEM((1, channels), wide),
            pltpu.VMEM((2 * length, length), narrow),
            pltpu.VMEM((length // 2, 2 * length), narrow),
            pltpu.VMEM((groups, 3, span + 8, rows), wide),
            pltpu.VMEM((groups, span, rows), wide),
            pltpu.VMEM((groups, 3, span, rows), wide),
            pltpu.VMEM((3, groups, span + 8, rows), wide),
            pltpu.VMEM((groups, 8, rows), wide),
            pltpu.VMEM((groups, 8, rows), wide),
            pltpu.VMEM((groups, 4, rows), wide),
            pltpu.VMEM((groups, 4, rows), wide),
            pltpu.VMEM((groups, 4, rows), wide),
            pltpu.VMEM((groups, 4, rows), wide),
            pltpu.VMEM((groups, span, rows), narrow),
            pltpu.VMEM((groups, span, rows), narrow),
            pltpu.VMEM((groups, rows, span), narrow),
            pltpu.VMEM((groups, span, rows), narrow),
            pltpu.VMEM((groups, span, rows), narrow),
            pltpu.VMEM((3, length, 2 * rows), narrow),
            pltpu.VMEM((3, 2 * length, rows), wide),
            pltpu.VMEM((2 * length, 2 * rows), narrow),
            pltpu.VMEM((length, rows), narrow),
            pltpu.VMEM((length, rows), narrow),
            pltpu.VMEM((length, rows), narrow),
            pltpu.VMEM((groups, span, rows), narrow),
            pltpu.VMEM((groups, span, rows), narrow),
            pltpu.VMEM((groups, 8, rows), wide),
            pltpu.VMEM((groups, 8, rows), wide),
            dma((7,)),
            dma((kinds,)),
            dma((kinds,)),
        ],
        compiler_params=pltpu.CompilerParams(
            collective_id=0, has_side_effects=True, vmem_limit_bytes=40 * 2**20
        ),
    )(
        *[
            pltpu.with_memory_space_constraint(value, pltpu.HBM)
            for value in (
                features,
                cotangent,
                long_filter,
                jnp.swapaxes(short_filters, 1, 2),
                skip_gain[None],
                jnp.asarray(forward_table),
                jnp.asarray(back_table),
            )
        ]
    )
    gated_out, feature_grad, long_grad, taps_grad, gain_grad = pl.pallas_call(
        functools.partial(settle_kernel, (groups, rows, span, taps)),
        out_shape=(
            jax.ShapeDtypeStruct((channels, span), narrow),
            jax.ShapeDtypeStruct((3, channels, span), narrow),
            jax.ShapeDtypeStruct((channels, span), narrow),
            jax.ShapeDtypeStruct((3, taps, channels), wide),
            jax.ShapeDtypeStruct((1, channels), wide),
        ),
        in_specs=[vmem] * 5,
        out_specs=(hbm,) * 5,
        scratch_shapes=[
            pltpu.VMEM((3, taps, channels), wide),
            pltpu.VMEM((1, channels), wide),
            dma((5,)),
        ],
    )(*[pltpu.with_memory_space_constraint(value, pltpu.VMEM) for value in middle])
    return gated_out, feature_grad, long_grad, jnp.swapaxes(taps_grad, 1, 2), gain_grad[0]


def dense_fits(features, short_filters, groups):
    channels, span = features.shape[1:]
    rows, length = channels // groups, span * groups
    return (
        channels % groups == 0
        and groups % 2 == 0
        and groups > 2
        and rows == 128
        and span == 128
        and length % 512 == 0
        and length <= 1024
        and 2 <= short_filters.shape[2] <= 3
    )


def shards(features, cotangent, long_filter, short_filters, skip_gain):
    groups = lax.axis_size("seq")
    if dense_fits(features, short_filters, groups):
        return fused(features, cotangent, long_filter, short_filters, skip_gain, groups)
    seq_index = lax.axis_index("seq")
    channels = features.shape[1]
    per_group = channels // groups
    margin = short_filters.shape[2] - 1
    local_gain = lax.dynamic_slice_in_dim(skip_gain, seq_index * per_group, per_group, 0)
    stacked = jnp.concatenate([features, cotangent[None], long_filter[None]], 0)
    columns = lax.all_to_all(stacked, "seq", split_axis=1, concat_axis=2, tiled=True)
    weights = lax.dynamic_slice_in_dim(short_filters, seq_index * per_group, per_group, 1)
    length = columns.shape[2]
    history = jnp.pad(columns[:3].astype(jnp.float32), ((0, 0), (0, 0), (margin, 0)))
    primed = featurize(history, weights, margin, length)
    mixed_term = (primed[1] * primed[2]).astype(jnp.bfloat16)
    cot_wide = columns[3].astype(jnp.float32)
    gated_grad = (cot_wide * primed[0]).astype(jnp.bfloat16)
    long_out, mixed_grad, kernel_grad = spectral(mixed_term, gated_grad, columns[4], local_gain)
    long_wide = long_out.astype(jnp.float32)
    mixed_back = mixed_grad.astype(jnp.float32)
    gated_out = (primed[0] * long_wide).astype(jnp.bfloat16)
    primed_grad = jnp.stack([cot_wide * long_wide, mixed_back * primed[2], mixed_back * primed[1]])
    padded_grad = jnp.pad(primed_grad, ((0, 0), (0, 0), (0, margin)))
    feature_grad = unfeaturize(padded_grad, weights, length).astype(jnp.bfloat16)
    taps_grad = tap_grads(primed_grad, history, margin, length)
    gain_grad = jnp.sum(gated_grad.astype(jnp.float32) * mixed_term.astype(jnp.float32), axis=-1)
    results = jnp.concatenate([gated_out[None], feature_grad, kernel_grad[None]], 0)
    row_blocks = lax.all_to_all(results, "seq", split_axis=2, concat_axis=1, tiled=True)
    short_grad, skip_grad = (
        lax.all_gather(taps_grad, "seq", axis=1, tiled=True),
        lax.all_gather(gain_grad, "seq", axis=0, tiled=True),
    )
    return (row_blocks[0], row_blocks[1:4], row_blocks[4], short_grad, skip_grad)


def solution(mesh):
    placed = (
        P(None, "chan", "seq"),
        P("chan", "seq"),
        P("chan", "seq"),
        P(None, "chan", None),
        P("chan"),
    )
    return jax.shard_map(
        shards,
        mesh=mesh,
        in_specs=placed,
        out_specs=(
            P("chan", "seq"),
            P(None, "chan", "seq"),
            P("chan", "seq"),
            P(None, "chan", None),
            P("chan"),
        ),
        check_vma=False,
    )
```

```python
import functools
import math

import jax
import jax.numpy as jnp
import numpy as np
from jax import lax
from jax.experimental import pallas as pl
from jax.experimental.pallas import tpu as pltpu
from jax.sharding import PartitionSpec as P

inner_length = 128
radix_width = 8


def phase_tables(row_count, col_count, length, direction):
    phase_index = (
        lax.iota(jnp.int32, row_count)[:, None] * lax.iota(jnp.int32, col_count)[None, :] % length
    )
    angles = direction * 2.0 * math.pi / length * phase_index.astype(jnp.float32)
    return (jnp.cos(angles), jnp.sin(angles))


def last_axis(operand, matrix):
    return jnp.einsum("...n,nk->...k", operand, matrix, precision=lax.Precision.HIGH)


def first_axis(operand, matrix):
    return jnp.einsum("...ab,ak->...kb", operand, matrix, precision=lax.Precision.HIGH)


def transform(real_part, imag_part, direction):
    length = real_part.shape[-1]
    if length <= inner_length or length % radix_width != 0:
        cos_table, sin_table = phase_tables(length, length, length, direction)
        return (
            last_axis(real_part, cos_table) - last_axis(imag_part, sin_table),
            last_axis(real_part, sin_table) + last_axis(imag_part, cos_table),
        )
    rest_length = length // radix_width
    grid_shape = real_part.shape[:-1] + (radix_width, rest_length)
    real_grid = real_part.reshape(grid_shape)
    imag_grid = imag_part.reshape(grid_shape)
    cos_table, sin_table = phase_tables(radix_width, radix_width, radix_width, direction)
    section_real = first_axis(real_grid, cos_table) - first_axis(imag_grid, sin_table)
    section_imag = first_axis(real_grid, sin_table) + first_axis(imag_grid, cos_table)
    twist_cos, twist_sin = phase_tables(radix_width, rest_length, length, direction)
    turned_real = section_real * twist_cos - section_imag * twist_sin
    turned_imag = section_real * twist_sin + section_imag * twist_cos
    inner_real, inner_imag = transform(turned_real, turned_imag, direction)
    return (
        jnp.swapaxes(inner_real, -1, -2).reshape(real_part.shape),
        jnp.swapaxes(inner_imag, -1, -2).reshape(real_part.shape),
    )


def spectral(mixed_term, gated_grad, kernel, local_gain):
    length = mixed_term.shape[-1]
    mixed_wide = mixed_term.astype(jnp.float32)
    gated_wide = gated_grad.astype(jnp.float32)
    kernel_wide = kernel.astype(jnp.float32)
    extend = ((0, 0), (0, length))
    real_in = jnp.stack([jnp.pad(mixed_wide, extend), jnp.pad(kernel_wide, extend)])
    imag_in = jnp.stack(
        [jnp.pad(gated_wide, extend), jnp.zeros((kernel_wide.shape[0], 2 * length), jnp.float32)]
    )
    freq_real, freq_imag = transform(real_in, imag_in, -1.0)
    packed_real = freq_real[0]
    packed_imag = freq_imag[0]
    mirror_real = jnp.roll(jnp.flip(packed_real, -1), 1, -1)
    mirror_imag = jnp.roll(jnp.flip(packed_imag, -1), 1, -1)
    mix_real = 0.5 * (packed_real + mirror_real)
    mix_imag = 0.5 * (packed_imag - mirror_imag)
    grad_real = 0.5 * (packed_imag + mirror_imag)
    grad_imag = 0.5 * (mirror_real - packed_real)
    kern_real = freq_real[1]
    kern_imag = freq_imag[1]
    conv_real = mix_real * kern_real - mix_imag * kern_imag
    conv_imag = mix_real * kern_imag + mix_imag * kern_real
    corr_real = grad_real * kern_real + grad_imag * kern_imag
    corr_imag = grad_imag * kern_real - grad_real * kern_imag
    cross_real = grad_real * mix_real + grad_imag * mix_imag
    cross_imag = grad_imag * mix_real - grad_real * mix_imag
    back_real = jnp.stack([conv_real - corr_imag, cross_real])
    back_imag = jnp.stack([conv_imag + corr_real, cross_imag])
    time_real, time_imag = transform(back_real, back_imag, 1.0)
    inverse_scale = 1.0 / (2 * length)
    conv_part = time_real[0, :, :length] * inverse_scale
    corr_part = time_imag[0, :, :length] * inverse_scale
    cross_part = time_real[1, :, :length] * inverse_scale
    gain_column = local_gain[:, None]
    long_out = (conv_part + gain_column * mixed_wide).astype(jnp.bfloat16)
    mixed_grad = (corr_part + gain_column * gated_wide).astype(jnp.bfloat16)
    return (long_out, mixed_grad, cross_part.astype(jnp.bfloat16))


def featurize(history, weights, margin, span_count):
    running = weights[:, :, 0:1] * history[:, :, margin : margin + span_count]
    for offset in range(1, margin + 1):
        running = (
            running
            + weights[:, :, offset : offset + 1]
            * history[:, :, margin - offset : margin - offset + span_count]
        )
    return running


def unfeaturize(padded_grad, weights, span_count):
    running = weights[:, :, 0:1] * padded_grad[:, :, 0:span_count]
    for offset in range(1, weights.shape[2]):
        running = (
            running
            + weights[:, :, offset : offset + 1] * padded_grad[:, :, offset : offset + span_count]
        )
    return running


def tap_grads(primed_grad, history, margin, span_count):
    columns = []
    for offset in range(margin + 1):
        columns.append(
            jnp.sum(
                primed_grad * history[:, :, margin - offset : margin - offset + span_count], axis=-1
            )
        )
    return jnp.stack(columns, axis=-1)


def packed_tables(length):
    half, quarter = length // 2, length // 4
    steps = np.arange(half)
    bins = np.arange(length).reshape(quarter, 4).T.reshape(-1)
    phase = (steps[:, None] * bins[None, :]) % (2 * length)
    angles = np.pi / length * phase
    sines = np.sin(angles)
    sines[:, 0] = 1.0 - 2.0 * (steps % 2)
    table = np.concatenate([np.cos(angles), sines], 1)
    weights = np.full(2 * length, 1.0 / length)
    weights[0] = weights[length] = 0.5 / length
    forward = table.T.astype(np.float32)
    high = forward.astype(jnp.bfloat16)
    low = (forward - high.astype(np.float32)).astype(jnp.bfloat16)
    return np.concatenate([high, low], 1), (table * weights).astype(np.float32).astype(jnp.bfloat16)


def fused_kernel(
    sizes,
    feat_hbm,
    cot_hbm,
    filt_hbm,
    short_hbm,
    gain_hbm,
    fwd_hbm,
    back_hbm,
    gated_out,
    grad_out,
    long_out,
    chip_sums,
    late_sums,
    long_in,
    spent,
    filt_raw,
    raw,
    short,
    gain_line,
    fwd,
    back,
    hist,
    cot,
    primed,
    moving,
    halo_out,
    halo_in,
    edge_out,
    edge_in,
    last_out,
    last_in,
    gate_out,
    mix_out,
    filt_in,
    gate_in,
    mix_in,
    tokens,
    freq,
    pair,
    res_grad,
    res_out,
    res_long,
    got_grad,
    got_out,
    own_sums,
    mate_sums,
    load_sem,
    send_sem,
    recv_sem,
):
    groups, rows, span, length, taps = sizes
    me = lax.axis_index("seq")
    peers = (2, 1, *range(3, groups))
    edge = 16
    FILT, GATE, MIX, GRAD, OUT, LONG, MATE, CHIP, LATE, HALO, EDGE, LAST = range(12)
    half, quarter = length // 2, length // 4
    half_groups, twins = groups // 2, groups // 2
    mate = me + 1 - 2 * lax.rem(me, 2)

    def near(step):
        return lax.rem(me + step, groups)

    def block(index, extent, count=1):
        return pl.ds(pl.multiple_of(index * extent, extent), extent * count)

    def lanes(step):
        return block(near(step), rows)

    barrier = pltpu.get_barrier_semaphore()
    for step in peers:
        pl.semaphore_signal(
            barrier,
            inc=1,
            device_id={"seq": near(step)},
            device_id_type=pl.DeviceIdType.MESH,
        )
    pairs = [
        (feat_hbm, raw.at[0:3]),
        (cot_hbm, raw.at[3]),
        (short_hbm, short),
        (gain_hbm, gain_line),
        (filt_hbm, filt_raw),
        (fwd_hbm, fwd),
        (back_hbm, back),
    ]
    loads = [
        pltpu.make_async_copy(source, target, load_sem.at[index])
        for index, (source, target) in enumerate(pairs)
    ]
    for index in (2, 0, 4, 1, 3, 5, 6):
        loads[index].start()

    def remote(source, target, kind, peer):
        return pltpu.make_async_remote_copy(
            src_ref=source,
            dst_ref=target,
            send_sem=send_sem.at[kind],
            recv_sem=recv_sem.at[kind],
            device_id={"seq": peer},
            device_id_type=pl.DeviceIdType.MESH,
        )

    def push(kind, source_of, target_of):
        for step in peers:
            remote(source_of(step), target_of(groups - step), kind, near(step)).start()

    def push_rows(kind, source, target, first, count):
        picked = pl.ds(first, count)
        push(
            kind,
            lambda step: source.at[step, picked, :],
            lambda slot: target.at[slot, picked, :],
        )

    def whole(kind, target):
        landed = target.at[1:groups]
        return remote(landed, landed, kind, near(1))

    loads[2].wait()
    loads[0].wait()

    halo_out[...] = jnp.zeros_like(halo_out)
    for step in range(groups):
        for stream in range(3):
            wide = raw[stream, lanes(step), :].T.astype(jnp.float32)
            hist[step, stream, 8:, :] = wide
            halo_out[near(step), 2 * stream : 2 * stream + 2, :] = wide[span - 2 :, :]

    right, left = near(1), near(groups - 1)

    pl.semaphore_wait(barrier, groups - 1)
    @pl.when(me < groups - 1)
    def _():
        remote(halo_out, halo_in, HALO, right).start()

    loads[4].wait()
    push(FILT, lambda step: filt_raw.at[lanes(step), :], lambda slot: filt_in.at[slot])

    loads[1].wait()
    for step in range(groups):
        cot[step] = raw[3, lanes(step), :].T.astype(jnp.float32)

    def coef(stream, offset, step):
        return short[stream, offset : offset + 1, lanes(step)]

    def featurize(step, stream, first, count):
        running = coef(stream, 0, step) * hist[step, stream, 8 + first : 8 + first + count, :]
        for offset in range(1, taps):
            start = 8 + first - offset
            running = (
                running
                + coef(stream, offset, step) * hist[step, stream, start : start + count, :]
            )
        primed[step, stream, first : first + count, :] = running
        return running

    def gate(step, first, count):
        value = featurize(step, 0, first, count) * cot[step, first : first + count, :]
        gate_out[step, first : first + count, :] = value.astype(jnp.bfloat16)

    def mix(step, first, count):
        value = featurize(step, 1, first, count) * featurize(step, 2, first, count)
        mix_out[step, first : first + count, :] = value.astype(jnp.bfloat16)

    for step in range(groups):
        gate(step, edge, span - edge)
    push_rows(GATE, gate_out, gate_in, edge, span - edge)
    for step in range(groups):
        mix(step, edge, span - edge)

    @pl.when(me > 0)
    def _():
        remote(halo_in, halo_in, HALO, left).wait_recv()

    @pl.when(me == 0)
    def _():
        halo_in[...] = jnp.zeros_like(halo_in)

    for step in range(groups):
        for stream in range(3):
            hist[step, stream, 6:8, :] = halo_in[near(step), 2 * stream : 2 * stream + 2, :]
        gate(step, 0, edge)
    push_rows(GATE, gate_out, gate_in, 0, edge)
    for step in range(groups):
        mix(step, 0, edge)
    whole(GATE, gate_in).wait_send()
    push_rows(MIX, mix_out, mix_in, 0, span)
    last_out[...] = jnp.zeros_like(last_out)
    moving[:, :, span:, :] = jnp.zeros((3, groups, 8, rows), jnp.float32)
    gate_in[0] = gate_out[0]
    mix_in[0] = mix_out[0]
    own_sums[...] = jnp.zeros_like(own_sums)
    late_sums[0] = jnp.zeros(late_sums.shape[1:], jnp.float32)
    for step in range(groups):
        local = gate_out[step].astype(jnp.float32) * mix_out[step].astype(jnp.float32)
        own_sums[near(step), 2 * taps : 2 * taps + 1, :] = jnp.sum(local, axis=0, keepdims=True)

    def place(kind, step, value):
        position = near(step)
        column = pl.ds(pl.multiple_of(position // half_groups * rows, rows), rows)
        for copy in range(2):
            start = copy * half + lax.rem(position, half_groups) * span
            tokens[kind, pl.ds(pl.multiple_of(start, span), span), column] = value

    def forward(kind):
        for turn in range(4):
            even_rows = slice(turn * quarter, (turn + 1) * quarter)
            odd_rows = slice(length + turn * quarter, length + (turn + 1) * quarter)
            cosines = jnp.dot(fwd[even_rows, :], tokens[kind], preferred_element_type=jnp.float32)
            sines = jnp.dot(fwd[odd_rows, :], tokens[kind], preferred_element_type=jnp.float32)
            even, odd = cosines[:, :rows], sines[:, :rows]
            even_late, odd_late = cosines[:, rows:], sines[:, rows:]
            if turn == 0:
                even, odd = even + even_late, odd + odd_late
            elif turn == 1:
                even, odd = even - odd_late, odd + even_late
            elif turn == 2:
                even, odd = even - even_late, odd - odd_late
            else:
                even, odd = even + odd_late, odd - even_late
            freq[kind, even_rows, :] = even
            freq[kind, odd_rows, :] = odd

    def product(left_kind, right_kind, sign):
        for turn in range(4):
            even_rows = slice(turn * quarter, (turn + 1) * quarter)
            odd_rows = slice(length + turn * quarter, length + (turn + 1) * quarter)
            left_c, left_s = freq[left_kind, even_rows, :], freq[left_kind, odd_rows, :]
            right_c, right_s = freq[right_kind, even_rows, :], freq[right_kind, odd_rows, :]
            both = left_s * right_s
            cross = left_s * right_c - sign * (left_c * right_s)
            if turn == 0:
                first = lax.broadcasted_iota(jnp.int32, (quarter, rows), 0) == 0
                even = left_c * right_c + sign * jnp.where(first, 0.0, both)
                odd = jnp.where(first, both, cross)
            else:
                even = left_c * right_c + sign * both
                odd = cross
            even = even.astype(jnp.bfloat16)
            odd = odd.astype(jnp.bfloat16)
            pair[even_rows, :rows] = even
            pair[odd_rows, :rows] = odd
            late_even, late_odd = ((even, odd), (odd, -even), (-even, -odd), (-odd, even))[turn]
            pair[even_rows, rows:] = late_even
            pair[odd_rows, rows:] = late_odd

    def finish(kind, result):
        total = jnp.dot(back[...], pair[...], preferred_element_type=jnp.float32)
        if kind is not None:
            total = total + wide_gain * tokens[kind, :half, :].astype(jnp.float32)
        total = total.astype(jnp.bfloat16)
        result[:half, :] = total[:, :rows]
        result[half:, :] = total[:, rows:]

    gates, mixes, kernels = range(3)

    loads[3].wait()
    filt_in[0] = filt_raw[lanes(0), :]
    loads[5].wait()
    gain = gain_line[:, lanes(0)]
    wide_gain = jnp.concatenate([gain, gain], 1)

    whole(FILT, filt_in).wait_recv()
    for step in range(groups):
        place(kernels, step, filt_in[step].T)
    forward(kernels)

    whole(GATE, gate_in).wait_recv()
    for step in range(groups):
        place(gates, step, gate_in[step])
    forward(gates)
    product(gates, kernels, 1.0)
    loads[6].wait()
    finish(gates, res_grad)

    def spread(kind, result, target):
        def taken(step):
            return block(near(step), span)

        push(kind, lambda step: result.at[taken(step), :], lambda slot: target.at[slot])
        target[0] = result[taken(0), :]

    spread(GRAD, res_grad, got_grad)

    whole(MIX, mix_in).wait_recv()
    for step in range(groups):
        place(mixes, step, mix_in[step])
    forward(mixes)
    product(mixes, kernels, -1.0)
    finish(mixes, res_out)
    spread(OUT, res_out, got_out)

    product(gates, mixes, 1.0)
    finish(None, res_long)
    def tally(step, stream, sums, row):
        for offset in range(taps):
            start = 8 - offset
            total = jnp.sum(
                moving[stream, step, 0:span, :] * hist[step, stream, start : start + span, :],
                axis=0,
                keepdims=True,
            )
            sums[near(step), row + offset : row + offset + 1, :] = total

    def spend(step, stream, first, count):
        running = coef(stream, 0, step) * moving[stream, step, first : first + count, :]
        for offset in range(1, taps):
            start = first + offset
            running = (
                running
                + coef(stream, offset, step) * moving[stream, step, start : start + count, :]
            )
        spent[stream, step, first : first + count, :] = running.astype(jnp.bfloat16)

    def hand_left(kind, source, target):
        @pl.when(me > 0)
        def _():
            remote(source, target, kind, left).start()

    def complete(kind, source, target, streams):
        @pl.when(me < groups - 1)
        def _():
            remote(target, target, kind, right).wait_recv()
            for step in range(groups):
                for place_of, stream in enumerate(streams):
                    taken = target[near(step), 2 * place_of : 2 * place_of + 2, :]
                    moving[stream, step, span : span + 2, :] = taken

        for step in range(groups):
            for stream in streams:
                spend(step, stream, span - edge, edge)
                grad_out[stream, lanes(step), :] = spent[stream, step].T

        @pl.when(me > 0)
        def _():
            remote(source, target, kind, left).wait_send()

    whole(GRAD, got_grad).wait_recv()
    spread(LONG, res_long, long_in)
    for step in range(groups):
        mixed_back = got_grad[step].astype(jnp.float32)
        moving[1, step, 0:span, :] = mixed_back * primed[step, 2, :, :]
        moving[2, step, 0:span, :] = mixed_back * primed[step, 1, :, :]
        edge_out[near(step), 0:2, :] = moving[1, step, 0:2, :]
        edge_out[near(step), 2:4, :] = moving[2, step, 0:2, :]
        tally(step, 1, own_sums, 0)
        tally(step, 2, own_sums, taps)
    remote(own_sums, mate_sums, MATE, mate).start()
    hand_left(EDGE, edge_out, edge_in)
    for step in range(groups):
        spend(step, 1, 0, span - edge)
        spend(step, 2, 0, span - edge)
    remote(own_sums, mate_sums, MATE, mate).wait_recv()
    chip_sums[0] = own_sums[...] + mate_sums[...]
    for twin in range(1, twins):
        remote(chip_sums.at[0], chip_sums.at[twins - twin], CHIP, near(2 * twin)).start()

    whole(OUT, got_out).wait_recv()
    for step in range(groups):
        moving[0, step, 0:span, :] = got_out[step].astype(jnp.float32) * cot[step]
        last_out[near(step), 0:2, :] = moving[0, step, 0:2, :]
        tally(step, 0, late_sums.at[0], 0)
    push(LATE, lambda step: late_sums.at[0], lambda slot: late_sums.at[slot])
    hand_left(LAST, last_out, last_in)
    for step in range(groups):
        gated = primed[step, 0, :, :] * got_out[step].astype(jnp.float32)
        gated_out[lanes(step), :] = gated.astype(jnp.bfloat16).T
        spend(step, 0, 0, span - edge)

    complete(EDGE, edge_out, edge_in, (1, 2))
    complete(LAST, last_out, last_in, (0,))
    whole(LONG, long_in).wait_recv()
    for step in range(groups):
        long_out[lanes(step), :] = long_in[step].T
    others = chip_sums.at[1:twins]
    remote(others, others, CHIP, near(2)).wait_recv()
    whole(LATE, late_sums).wait_recv()
    remote(own_sums, mate_sums, MATE, mate).wait_send()
    remote(others, others, CHIP, near(2)).wait_send()

    @pl.when(me < groups - 1)
    def _():
        remote(halo_out, halo_in, HALO, right).wait_send()

    for kind, target in (
        (FILT, filt_in),
        (MIX, mix_in),
        (GRAD, got_grad),
        (OUT, got_out),
        (LONG, long_in),
        (LATE, late_sums),
    ):
        whole(kind, target).wait_send()


def settle_kernel(
    sizes, gated, grad, long, chip_sums, late_sums, gated_hbm, grad_hbm, long_hbm, taps_hbm, skip_hbm,
    taps_line, skip_line, done,
):
    groups, rows, span, taps = sizes
    twins = groups // 2
    me = lax.axis_index("seq")
    copies = []

    def start(source, target):
        copy = pltpu.make_async_copy(source, target, done.at[len(copies)])
        copy.start()
        copies.append(copy)

    start(grad, grad_hbm)
    start(gated, gated_hbm)
    start(long, long_hbm)
    for group in range(groups):
        picked = slice(group * rows, (group + 1) * rows)
        early = late = None
        for source in range(groups):
            value = late_sums[lax.rem(source + groups - me, groups), group]
            late = value if late is None else late + value
        for source in range(twins):
            value = chip_sums[lax.rem(source + twins - me // 2, twins), group]
            early = value if early is None else early + value
        taps_line[0, :, picked] = late[:taps]
        taps_line[1, :, picked] = early[:taps]
        taps_line[2, :, picked] = early[taps : 2 * taps]
        skip_line[:, picked] = early[2 * taps : 2 * taps + 1]
    start(taps_line, taps_hbm)
    start(skip_line, skip_hbm)
    for copy in copies:
        copy.wait()


def fused(features, cotangent, long_filter, short_filters, skip_gain, groups):
    channels, span = cotangent.shape
    rows = channels // groups
    length = span * groups
    taps = short_filters.shape[2]
    hbm = pl.BlockSpec(memory_space=pltpu.HBM)
    vmem = pl.BlockSpec(memory_space=pltpu.VMEM)
    dma = pltpu.SemaphoreType.DMA
    narrow, wide = jnp.bfloat16, jnp.float32
    kinds = 12
    forward_table, back_table = packed_tables(length)
    middle = pl.pallas_call(
        functools.partial(fused_kernel, (groups, rows, span, length, taps)),
        out_shape=(
            pltpu.VMEM((channels, span), narrow),
            pltpu.VMEM((3, channels, span), narrow),
            pltpu.VMEM((channels, span), narrow),
            pltpu.VMEM((groups // 2, groups, 8, rows), wide),
            pltpu.VMEM((groups, groups, 4, rows), wide),
        ),
        in_specs=[hbm] * 7,
        out_specs=(vmem,) * 5,
        scratch_shapes=[
            pltpu.VMEM((groups, span, rows), narrow),
            pltpu.VMEM((3, groups, span, rows), narrow),
            pltpu.VMEM((channels, span), narrow),
            pltpu.VMEM((4, channels, span), narrow),
            pltpu.VMEM((3, taps, channels), wide),
            pltpu.VMEM((1, channels), wide),
            pltpu.VMEM((2 * length, length), narrow),
            pltpu.VMEM((length // 2, 2 * length), narrow),
            pltpu.VMEM((groups, 3, span + 8, rows), wide),
            pltpu.VMEM((groups, span, rows), wide),
            pltpu.VMEM((groups, 3, span, rows), wide),
            pltpu.VMEM((3, groups, span + 8, rows), wide),
            pltpu.VMEM((groups, 8, rows), wide),
            pltpu.VMEM((groups, 8, rows), wide),
            pltpu.VMEM((groups, 4, rows), wide),
            pltpu.VMEM((groups, 4, rows), wide),
            pltpu.VMEM((groups, 4, rows), wide),
            pltpu.VMEM((groups, 4, rows), wide),
            pltpu.VMEM((groups, span, rows), narrow),
            pltpu.VMEM((groups, span, rows), narrow),
            pltpu.VMEM((groups, rows, span), narrow),
            pltpu.VMEM((groups, span, rows), narrow),
            pltpu.VMEM((groups, span, rows), narrow),
            pltpu.VMEM((3, length, 2 * rows), narrow),
            pltpu.VMEM((3, 2 * length, rows), wide),
            pltpu.VMEM((2 * length, 2 * rows), narrow),
            pltpu.VMEM((length, rows), narrow),
            pltpu.VMEM((length, rows), narrow),
            pltpu.VMEM((length, rows), narrow),
            pltpu.VMEM((groups, span, rows), narrow),
            pltpu.VMEM((groups, span, rows), narrow),
            pltpu.VMEM((groups, 8, rows), wide),
            pltpu.VMEM((groups, 8, rows), wide),
            dma((7,)),
            dma((kinds,)),
            dma((kinds,)),
        ],
        compiler_params=pltpu.CompilerParams(
            collective_id=0, has_side_effects=True, vmem_limit_bytes=40 * 2**20
        ),
    )(
        *[
            pltpu.with_memory_space_constraint(value, pltpu.HBM)
            for value in (
                features,
                cotangent,
                long_filter,
                jnp.swapaxes(short_filters, 1, 2),
                skip_gain[None],
                jnp.asarray(forward_table),
                jnp.asarray(back_table),
            )
        ]
    )
    gated_out, feature_grad, long_grad, taps_grad, gain_grad = pl.pallas_call(
        functools.partial(settle_kernel, (groups, rows, span, taps)),
        out_shape=(
            jax.ShapeDtypeStruct((channels, span), narrow),
            jax.ShapeDtypeStruct((3, channels, span), narrow),
            jax.ShapeDtypeStruct((channels, span), narrow),
            jax.ShapeDtypeStruct((3, taps, channels), wide),
            jax.ShapeDtypeStruct((1, channels), wide),
        ),
        in_specs=[vmem] * 5,
        out_specs=(hbm,) * 5,
        scratch_shapes=[
            pltpu.VMEM((3, taps, channels), wide),
            pltpu.VMEM((1, channels), wide),
            dma((5,)),
        ],
    )(*[pltpu.with_memory_space_constraint(value, pltpu.VMEM) for value in middle])
    return gated_out, feature_grad, long_grad, jnp.swapaxes(taps_grad, 1, 2), gain_grad[0]


def dense_fits(features, short_filters, groups):
    channels, span = features.shape[1:]
    rows, length = channels // groups, span * groups
    return (
        channels % groups == 0
        and groups % 2 == 0
        and groups > 2
        and rows == 128
        and span == 128
        and length % 512 == 0
        and length <= 1024
        and 2 <= short_filters.shape[2] <= 3
    )


def shards(features, cotangent, long_filter, short_filters, skip_gain):
    groups = lax.axis_size("seq")
    if dense_fits(features, short_filters, groups):
        return fused(features, cotangent, long_filter, short_filters, skip_gain, groups)
    seq_index = lax.axis_index("seq")
    channels = features.shape[1]
    per_group = channels // groups
    margin = short_filters.shape[2] - 1
    local_gain = lax.dynamic_slice_in_dim(skip_gain, seq_index * per_group, per_group, 0)
    stacked = jnp.concatenate([features, cotangent[None], long_filter[None]], 0)
    columns = lax.all_to_all(stacked, "seq", split_axis=1, concat_axis=2, tiled=True)
    weights = lax.dynamic_slice_in_dim(short_filters, seq_index * per_group, per_group, 1)
    length = columns.shape[2]
    history = jnp.pad(columns[:3].astype(jnp.float32), ((0, 0), (0, 0), (margin, 0)))
    primed = featurize(history, weights, margin, length)
    mixed_term = (primed[1] * primed[2]).astype(jnp.bfloat16)
    cot_wide = columns[3].astype(jnp.float32)
    gated_grad = (cot_wide * primed[0]).astype(jnp.bfloat16)
    long_out, mixed_grad, kernel_grad = spectral(mixed_term, gated_grad, columns[4], local_gain)
    long_wide = long_out.astype(jnp.float32)
    mixed_back = mixed_grad.astype(jnp.float32)
    gated_out = (primed[0] * long_wide).astype(jnp.bfloat16)
    primed_grad = jnp.stack([cot_wide * long_wide, mixed_back * primed[2], mixed_back * primed[1]])
    padded_grad = jnp.pad(primed_grad, ((0, 0), (0, 0), (0, margin)))
    feature_grad = unfeaturize(padded_grad, weights, length).astype(jnp.bfloat16)
    taps_grad = tap_grads(primed_grad, history, margin, length)
    gain_grad = jnp.sum(gated_grad.astype(jnp.float32) * mixed_term.astype(jnp.float32), axis=-1)
    results = jnp.concatenate([gated_out[None], feature_grad, kernel_grad[None]], 0)
    row_blocks = lax.all_to_all(results, "seq", split_axis=2, concat_axis=1, tiled=True)
    short_grad, skip_grad = (
        lax.all_gather(taps_grad, "seq", axis=1, tiled=True),
        lax.all_gather(gain_grad, "seq", axis=0, tiled=True),
    )
    return (row_blocks[0], row_blocks[1:4], row_blocks[4], short_grad, skip_grad)


def solution(mesh):
    placed = (
        P(None, "chan", "seq"),
        P("chan", "seq"),
        P("chan", "seq"),
        P(None, "chan", None),
        P("chan"),
    )
    return jax.shard_map(
        shards,
        mesh=mesh,
        in_specs=placed,
        out_specs=(
            P("chan", "seq"),
            P(None, "chan", "seq"),
            P("chan", "seq"),
            P(None, "chan", None),
            P("chan"),
        ),
        check_vma=False,
    )
```

```python
import functools
import math

import jax
import jax.numpy as jnp
import numpy as np
from jax import lax
from jax.experimental import pallas as pl
from jax.experimental.pallas import tpu as pltpu
from jax.sharding import PartitionSpec as P

inner_length = 128
radix_width = 8


def phase_tables(row_count, col_count, length, direction):
    phase_index = (
        lax.iota(jnp.int32, row_count)[:, None] * lax.iota(jnp.int32, col_count)[None, :] % length
    )
    angles = direction * 2.0 * math.pi / length * phase_index.astype(jnp.float32)
    return (jnp.cos(angles), jnp.sin(angles))


def last_axis(operand, matrix):
    return jnp.einsum("...n,nk->...k", operand, matrix, precision=lax.Precision.HIGH)


def first_axis(operand, matrix):
    return jnp.einsum("...ab,ak->...kb", operand, matrix, precision=lax.Precision.HIGH)


def transform(real_part, imag_part, direction):
    length = real_part.shape[-1]
    if length <= inner_length or length % radix_width != 0:
        cos_table, sin_table = phase_tables(length, length, length, direction)
        return (
            last_axis(real_part, cos_table) - last_axis(imag_part, sin_table),
            last_axis(real_part, sin_table) + last_axis(imag_part, cos_table),
        )
    rest_length = length // radix_width
    grid_shape = real_part.shape[:-1] + (radix_width, rest_length)
    real_grid = real_part.reshape(grid_shape)
    imag_grid = imag_part.reshape(grid_shape)
    cos_table, sin_table = phase_tables(radix_width, radix_width, radix_width, direction)
    section_real = first_axis(real_grid, cos_table) - first_axis(imag_grid, sin_table)
    section_imag = first_axis(real_grid, sin_table) + first_axis(imag_grid, cos_table)
    twist_cos, twist_sin = phase_tables(radix_width, rest_length, length, direction)
    turned_real = section_real * twist_cos - section_imag * twist_sin
    turned_imag = section_real * twist_sin + section_imag * twist_cos
    inner_real, inner_imag = transform(turned_real, turned_imag, direction)
    return (
        jnp.swapaxes(inner_real, -1, -2).reshape(real_part.shape),
        jnp.swapaxes(inner_imag, -1, -2).reshape(real_part.shape),
    )


def spectral(mixed_term, gated_grad, kernel, local_gain):
    length = mixed_term.shape[-1]
    mixed_wide = mixed_term.astype(jnp.float32)
    gated_wide = gated_grad.astype(jnp.float32)
    kernel_wide = kernel.astype(jnp.float32)
    extend = ((0, 0), (0, length))
    real_in = jnp.stack([jnp.pad(mixed_wide, extend), jnp.pad(kernel_wide, extend)])
    imag_in = jnp.stack(
        [jnp.pad(gated_wide, extend), jnp.zeros((kernel_wide.shape[0], 2 * length), jnp.float32)]
    )
    freq_real, freq_imag = transform(real_in, imag_in, -1.0)
    packed_real = freq_real[0]
    packed_imag = freq_imag[0]
    mirror_real = jnp.roll(jnp.flip(packed_real, -1), 1, -1)
    mirror_imag = jnp.roll(jnp.flip(packed_imag, -1), 1, -1)
    mix_real = 0.5 * (packed_real + mirror_real)
    mix_imag = 0.5 * (packed_imag - mirror_imag)
    grad_real = 0.5 * (packed_imag + mirror_imag)
    grad_imag = 0.5 * (mirror_real - packed_real)
    kern_real = freq_real[1]
    kern_imag = freq_imag[1]
    conv_real = mix_real * kern_real - mix_imag * kern_imag
    conv_imag = mix_real * kern_imag + mix_imag * kern_real
    corr_real = grad_real * kern_real + grad_imag * kern_imag
    corr_imag = grad_imag * kern_real - grad_real * kern_imag
    cross_real = grad_real * mix_real + grad_imag * mix_imag
    cross_imag = grad_imag * mix_real - grad_real * mix_imag
    back_real = jnp.stack([conv_real - corr_imag, cross_real])
    back_imag = jnp.stack([conv_imag + corr_real, cross_imag])
    time_real, time_imag = transform(back_real, back_imag, 1.0)
    inverse_scale = 1.0 / (2 * length)
    conv_part = time_real[0, :, :length] * inverse_scale
    corr_part = time_imag[0, :, :length] * inverse_scale
    cross_part = time_real[1, :, :length] * inverse_scale
    gain_column = local_gain[:, None]
    long_out = (conv_part + gain_column * mixed_wide).astype(jnp.bfloat16)
    mixed_grad = (corr_part + gain_column * gated_wide).astype(jnp.bfloat16)
    return (long_out, mixed_grad, cross_part.astype(jnp.bfloat16))


def featurize(history, weights, margin, span_count):
    running = weights[:, :, 0:1] * history[:, :, margin : margin + span_count]
    for offset in range(1, margin + 1):
        running = (
            running
            + weights[:, :, offset : offset + 1]
            * history[:, :, margin - offset : margin - offset + span_count]
        )
    return running


def unfeaturize(padded_grad, weights, span_count):
    running = weights[:, :, 0:1] * padded_grad[:, :, 0:span_count]
    for offset in range(1, weights.shape[2]):
        running = (
            running
            + weights[:, :, offset : offset + 1] * padded_grad[:, :, offset : offset + span_count]
        )
    return running


def tap_grads(primed_grad, history, margin, span_count):
    columns = []
    for offset in range(margin + 1):
        columns.append(
            jnp.sum(
                primed_grad * history[:, :, margin - offset : margin - offset + span_count], axis=-1
            )
        )
    return jnp.stack(columns, axis=-1)


def packed_tables(length):
    half, quarter = length // 2, length // 4
    steps = np.arange(half)
    bins = np.arange(length).reshape(quarter, 4).T.reshape(-1)
    phase = (steps[:, None] * bins[None, :]) % (2 * length)
    angles = np.pi / length * phase
    sines = np.sin(angles)
    sines[:, 0] = 1.0 - 2.0 * (steps % 2)
    table = np.concatenate([np.cos(angles), sines], 1)
    weights = np.full(2 * length, 1.0 / length)
    weights[0] = weights[length] = 0.5 / length
    forward = table.T.astype(np.float32)
    high = forward.astype(jnp.bfloat16)
    low = (forward - high.astype(np.float32)).astype(jnp.bfloat16)
    return np.concatenate([high, low], 1), (table * weights).astype(np.float32).astype(jnp.bfloat16)


def fused_kernel(
    sizes,
    feat_hbm,
    cot_hbm,
    filt_hbm,
    short_hbm,
    gain_hbm,
    fwd_hbm,
    back_hbm,
    gated_out,
    grad_out,
    long_out,
    chip_sums,
    late_sums,
    long_in,
    spent,
    filt_raw,
    raw,
    short,
    gain_line,
    fwd,
    back,
    hist,
    cot,
    primed,
    moving,
    halo_out,
    halo_in,
    edge_out,
    edge_in,
    last_out,
    last_in,
    gate_out,
    mix_out,
    filt_in,
    gate_in,
    mix_in,
    tokens,
    freq,
    pair,
    res_grad,
    res_out,
    res_long,
    got_grad,
    got_out,
    own_sums,
    mate_sums,
    load_sem,
    send_sem,
    recv_sem,
):
    groups, rows, span, length, taps = sizes
    me = lax.axis_index("seq")
    peers = (2, 1, *range(3, groups))
    edge = 16
    FILT, GATE, MIX, GRAD, OUT, LONG, MATE, CHIP, LATE, HALO, EDGE, LAST = range(12)
    half, quarter = length // 2, length // 4
    half_groups, twins = groups // 2, groups // 2
    mate = me + 1 - 2 * lax.rem(me, 2)

    def near(step):
        return lax.rem(me + step, groups)

    def block(index, extent, count=1):
        return pl.ds(pl.multiple_of(index * extent, extent), extent * count)

    def lanes(step):
        return block(near(step), rows)

    barrier = pltpu.get_barrier_semaphore()
    for step in peers:
        pl.semaphore_signal(
            barrier,
            inc=1,
            device_id={"seq": near(step)},
            device_id_type=pl.DeviceIdType.MESH,
        )
    pairs = [
        (feat_hbm, raw.at[0:3]),
        (cot_hbm, raw.at[3]),
        (short_hbm, short),
        (gain_hbm, gain_line),
        (filt_hbm, filt_raw),
        (fwd_hbm, fwd),
        (back_hbm, back),
    ]
    loads = [
        pltpu.make_async_copy(source, target, load_sem.at[index])
        for index, (source, target) in enumerate(pairs)
    ]
    for index in (2, 0, 4, 1, 3, 5, 6):
        loads[index].start()

    def remote(source, target, kind, peer):
        return pltpu.make_async_remote_copy(
            src_ref=source,
            dst_ref=target,
            send_sem=send_sem.at[kind],
            recv_sem=recv_sem.at[kind],
            device_id={"seq": peer},
            device_id_type=pl.DeviceIdType.MESH,
        )

    def push(kind, source_of, target_of):
        for step in peers:
            remote(source_of(step), target_of(groups - step), kind, near(step)).start()

    def push_rows(kind, source, target, first, count):
        picked = pl.ds(first, count)
        push(
            kind,
            lambda step: source.at[step, picked, :],
            lambda slot: target.at[slot, picked, :],
        )

    def whole(kind, target):
        landed = target.at[1:groups]
        return remote(landed, landed, kind, near(1))

    loads[2].wait()
    loads[0].wait()

    halo_out[...] = jnp.zeros_like(halo_out)
    for step in range(groups):
        for stream in range(3):
            wide = raw[stream, lanes(step), :].T.astype(jnp.float32)
            hist[step, stream, 8:, :] = wide
            halo_out[near(step), 2 * stream : 2 * stream + 2, :] = wide[span - 2 :, :]

    right, left = near(1), near(groups - 1)

    pl.semaphore_wait(barrier, groups - 1)
    @pl.when(me < groups - 1)
    def _():
        remote(halo_out, halo_in, HALO, right).start()

    loads[4].wait()
    push(FILT, lambda step: filt_raw.at[lanes(step), :], lambda slot: filt_in.at[slot])

    loads[1].wait()
    for step in range(groups):
        cot[step] = raw[3, lanes(step), :].T.astype(jnp.float32)

    def coef(stream, offset, step):
        return short[stream, offset : offset + 1, lanes(step)]

    def featurize(step, stream, first, count):
        running = coef(stream, 0, step) * hist[step, stream, 8 + first : 8 + first + count, :]
        for offset in range(1, taps):
            start = 8 + first - offset
            running = (
                running
                + coef(stream, offset, step) * hist[step, stream, start : start + count, :]
            )
        primed[step, stream, first : first + count, :] = running
        return running

    def gate(step, first, count):
        value = featurize(step, 0, first, count) * cot[step, first : first + count, :]
        gate_out[step, first : first + count, :] = value.astype(jnp.bfloat16)

    def mix(step, first, count):
        value = featurize(step, 1, first, count) * featurize(step, 2, first, count)
        mix_out[step, first : first + count, :] = value.astype(jnp.bfloat16)

    for step in range(groups):
        gate(step, edge, span - edge)
    push_rows(GATE, gate_out, gate_in, edge, span - edge)
    for step in range(groups):
        mix(step, edge, span - edge)

    @pl.when(me > 0)
    def _():
        remote(halo_in, halo_in, HALO, left).wait_recv()

    @pl.when(me == 0)
    def _():
        halo_in[...] = jnp.zeros_like(halo_in)

    for step in range(groups):
        for stream in range(3):
            hist[step, stream, 6:8, :] = halo_in[near(step), 2 * stream : 2 * stream + 2, :]
        gate(step, 0, edge)
    push_rows(GATE, gate_out, gate_in, 0, edge)
    for step in range(groups):
        mix(step, 0, edge)
    whole(GATE, gate_in).wait_send()
    push_rows(MIX, mix_out, mix_in, 0, span)
    last_out[...] = jnp.zeros_like(last_out)
    moving[:, :, span:, :] = jnp.zeros((3, groups, 8, rows), jnp.float32)
    gate_in[0] = gate_out[0]
    mix_in[0] = mix_out[0]
    own_sums[...] = jnp.zeros_like(own_sums)
    late_sums[0] = jnp.zeros(late_sums.shape[1:], jnp.float32)
    for step in range(groups):
        local = gate_out[step].astype(jnp.float32) * mix_out[step].astype(jnp.float32)
        own_sums[near(step), 2 * taps : 2 * taps + 1, :] = jnp.sum(local, axis=0, keepdims=True)

    def place(kind, step, value):
        position = near(step)
        column = pl.ds(pl.multiple_of(position // half_groups * rows, rows), rows)
        for copy in range(2):
            start = copy * half + lax.rem(position, half_groups) * span
            tokens[kind, pl.ds(pl.multiple_of(start, span), span), column] = value

    def forward(kind):
        for turn in range(4):
            even_rows = slice(turn * quarter, (turn + 1) * quarter)
            odd_rows = slice(length + turn * quarter, length + (turn + 1) * quarter)
            cosines = jnp.dot(fwd[even_rows, :], tokens[kind], preferred_element_type=jnp.float32)
            sines = jnp.dot(fwd[odd_rows, :], tokens[kind], preferred_element_type=jnp.float32)
            even, odd = cosines[:, :rows], sines[:, :rows]
            even_late, odd_late = cosines[:, rows:], sines[:, rows:]
            if turn == 0:
                even, odd = even + even_late, odd + odd_late
            elif turn == 1:
                even, odd = even - odd_late, odd + even_late
            elif turn == 2:
                even, odd = even - even_late, odd - odd_late
            else:
                even, odd = even + odd_late, odd - even_late
            freq[kind, even_rows, :] = even
            freq[kind, odd_rows, :] = odd

    def product(left_kind, right_kind, sign):
        for turn in range(4):
            even_rows = slice(turn * quarter, (turn + 1) * quarter)
            odd_rows = slice(length + turn * quarter, length + (turn + 1) * quarter)
            left_c, left_s = freq[left_kind, even_rows, :], freq[left_kind, odd_rows, :]
            right_c, right_s = freq[right_kind, even_rows, :], freq[right_kind, odd_rows, :]
            both = left_s * right_s
            cross = left_s * right_c - sign * (left_c * right_s)
            if turn == 0:
                first = lax.broadcasted_iota(jnp.int32, (quarter, rows), 0) == 0
                even = left_c * right_c + sign * jnp.where(first, 0.0, both)
                odd = jnp.where(first, both, cross)
            else:
                even = left_c * right_c + sign * both
                odd = cross
            even = even.astype(jnp.bfloat16)
            odd = odd.astype(jnp.bfloat16)
            pair[even_rows, :rows] = even
            pair[odd_rows, :rows] = odd
            late_even, late_odd = ((even, odd), (odd, -even), (-even, -odd), (-odd, even))[turn]
            pair[even_rows, rows:] = late_even
            pair[odd_rows, rows:] = late_odd

    def finish(kind, result):
        total = jnp.dot(back[...], pair[...], preferred_element_type=jnp.float32)
        if kind is not None:
            total = total + wide_gain * tokens[kind, :half, :].astype(jnp.float32)
        total = total.astype(jnp.bfloat16)
        result[:half, :] = total[:, :rows]
        result[half:, :] = total[:, rows:]

    gates, mixes, kernels = range(3)

    loads[3].wait()
    filt_in[0] = filt_raw[lanes(0), :]
    loads[5].wait()
    gain = gain_line[:, lanes(0)]
    wide_gain = jnp.concatenate([gain, gain], 1)

    whole(FILT, filt_in).wait_recv()
    for step in range(groups):
        place(kernels, step, filt_in[step].T)
    forward(kernels)

    whole(GATE, gate_in).wait_recv()
    for step in range(groups):
        place(gates, step, gate_in[step])
    forward(gates)
    product(gates, kernels, 1.0)
    loads[6].wait()
    finish(gates, res_grad)

    def spread(kind, result, target):
        def taken(step):
            return block(near(step), span)

        push(kind, lambda step: result.at[taken(step), :], lambda slot: target.at[slot])
        target[0] = result[taken(0), :]

    spread(GRAD, res_grad, got_grad)

    whole(MIX, mix_in).wait_recv()
    for step in range(groups):
        place(mixes, step, mix_in[step])
    forward(mixes)
    product(mixes, kernels, -1.0)
    finish(mixes, res_out)
    spread(OUT, res_out, got_out)

    product(gates, mixes, 1.0)
    finish(None, res_long)
    def tally(step, stream, sums, row):
        for offset in range(taps):
            start = 8 - offset
            total = jnp.sum(
                moving[stream, step, 0:span, :] * hist[step, stream, start : start + span, :],
                axis=0,
                keepdims=True,
            )
            sums[near(step), row + offset : row + offset + 1, :] = total

    def spend(step, stream, first, count):
        running = coef(stream, 0, step) * moving[stream, step, first : first + count, :]
        for offset in range(1, taps):
            start = first + offset
            running = (
                running
                + coef(stream, offset, step) * moving[stream, step, start : start + count, :]
            )
        spent[stream, step, first : first + count, :] = running.astype(jnp.bfloat16)

    def hand_left(kind, source, target):
        @pl.when(me > 0)
        def _():
            remote(source, target, kind, left).start()

    def complete(kind, source, target, streams):
        @pl.when(me < groups - 1)
        def _():
            remote(target, target, kind, right).wait_recv()
            for step in range(groups):
                for place_of, stream in enumerate(streams):
                    taken = target[near(step), 2 * place_of : 2 * place_of + 2, :]
                    moving[stream, step, span : span + 2, :] = taken

        for step in range(groups):
            for stream in streams:
                spend(step, stream, span - edge, edge)
                grad_out[stream, lanes(step), :] = spent[stream, step].T

        @pl.when(me > 0)
        def _():
            remote(source, target, kind, left).wait_send()

    whole(GRAD, got_grad).wait_recv()
    spread(LONG, res_long, long_in)
    for step in range(groups):
        mixed_back = got_grad[step].astype(jnp.float32)
        moving[1, step, 0:span, :] = mixed_back * primed[step, 2, :, :]
        moving[2, step, 0:span, :] = mixed_back * primed[step, 1, :, :]
        edge_out[near(step), 0:2, :] = moving[1, step, 0:2, :]
        edge_out[near(step), 2:4, :] = moving[2, step, 0:2, :]
        tally(step, 1, own_sums, 0)
        tally(step, 2, own_sums, taps)
    remote(own_sums, mate_sums, MATE, mate).start()
    hand_left(EDGE, edge_out, edge_in)
    remote(own_sums, mate_sums, MATE, mate).wait_recv()
    chip_sums[0] = own_sums[...] + mate_sums[...]
    for twin in range(1, twins):
        remote(chip_sums.at[0], chip_sums.at[twins - twin], CHIP, near(2 * twin)).start()

    whole(OUT, got_out).wait_recv()
    for step in range(groups):
        moving[0, step, 0:span, :] = got_out[step].astype(jnp.float32) * cot[step]
        last_out[near(step), 0:2, :] = moving[0, step, 0:2, :]
        tally(step, 0, late_sums.at[0], 0)
    push(LATE, lambda step: late_sums.at[0], lambda slot: late_sums.at[slot])
    hand_left(LAST, last_out, last_in)
    for step in range(groups):
        spend(step, 1, 0, span - edge)
        spend(step, 2, 0, span - edge)
    for step in range(groups):
        gated = primed[step, 0, :, :] * got_out[step].astype(jnp.float32)
        gated_out[lanes(step), :] = gated.astype(jnp.bfloat16).T
        spend(step, 0, 0, span - edge)

    complete(EDGE, edge_out, edge_in, (1, 2))
    complete(LAST, last_out, last_in, (0,))
    whole(LONG, long_in).wait_recv()
    for step in range(groups):
        long_out[lanes(step), :] = long_in[step].T
    others = chip_sums.at[1:twins]
    remote(others, others, CHIP, near(2)).wait_recv()
    whole(LATE, late_sums).wait_recv()
    remote(own_sums, mate_sums, MATE, mate).wait_send()
    remote(others, others, CHIP, near(2)).wait_send()

    @pl.when(me < groups - 1)
    def _():
        remote(halo_out, halo_in, HALO, right).wait_send()

    for kind, target in (
        (FILT, filt_in),
        (MIX, mix_in),
        (GRAD, got_grad),
        (OUT, got_out),
        (LONG, long_in),
        (LATE, late_sums),
    ):
        whole(kind, target).wait_send()


def settle_kernel(
    sizes, gated, grad, long, chip_sums, late_sums, gated_hbm, grad_hbm, long_hbm, taps_hbm, skip_hbm,
    taps_line, skip_line, done,
):
    groups, rows, span, taps = sizes
    twins = groups // 2
    me = lax.axis_index("seq")
    copies = []

    def start(source, target):
        copy = pltpu.make_async_copy(source, target, done.at[len(copies)])
        copy.start()
        copies.append(copy)

    start(grad, grad_hbm)
    start(gated, gated_hbm)
    start(long, long_hbm)
    for group in range(groups):
        picked = slice(group * rows, (group + 1) * rows)
        early = late = None
        for source in range(groups):
            value = late_sums[lax.rem(source + groups - me, groups), group]
            late = value if late is None else late + value
        for source in range(twins):
            value = chip_sums[lax.rem(source + twins - me // 2, twins), group]
            early = value if early is None else early + value
        taps_line[0, :, picked] = late[:taps]
        taps_line[1, :, picked] = early[:taps]
        taps_line[2, :, picked] = early[taps : 2 * taps]
        skip_line[:, picked] = early[2 * taps : 2 * taps + 1]
    start(taps_line, taps_hbm)
    start(skip_line, skip_hbm)
    for copy in copies:
        copy.wait()


def fused(features, cotangent, long_filter, short_filters, skip_gain, groups):
    channels, span = cotangent.shape
    rows = channels // groups
    length = span * groups
    taps = short_filters.shape[2]
    hbm = pl.BlockSpec(memory_space=pltpu.HBM)
    vmem = pl.BlockSpec(memory_space=pltpu.VMEM)
    dma = pltpu.SemaphoreType.DMA
    narrow, wide = jnp.bfloat16, jnp.float32
    kinds = 12
    forward_table, back_table = packed_tables(length)
    middle = pl.pallas_call(
        functools.partial(fused_kernel, (groups, rows, span, length, taps)),
        out_shape=(
            pltpu.VMEM((channels, span), narrow),
            pltpu.VMEM((3, channels, span), narrow),
            pltpu.VMEM((channels, span), narrow),
            pltpu.VMEM((groups // 2, groups, 8, rows), wide),
            pltpu.VMEM((groups, groups, 4, rows), wide),
        ),
        in_specs=[hbm] * 7,
        out_specs=(vmem,) * 5,
        scratch_shapes=[
            pltpu.VMEM((groups, span, rows), narrow),
            pltpu.VMEM((3, groups, span, rows), narrow),
            pltpu.VMEM((channels, span), narrow),
            pltpu.VMEM((4, channels, span), narrow),
            pltpu.VMEM((3, taps, channels), wide),
            pltpu.VMEM((1, channels), wide),
            pltpu.VMEM((2 * length, length), narrow),
            pltpu.VMEM((length // 2, 2 * length), narrow),
            pltpu.VMEM((groups, 3, span + 8, rows), wide),
            pltpu.VMEM((groups, span, rows), wide),
            pltpu.VMEM((groups, 3, span, rows), wide),
            pltpu.VMEM((3, groups, span + 8, rows), wide),
            pltpu.VMEM((groups, 8, rows), wide),
            pltpu.VMEM((groups, 8, rows), wide),
            pltpu.VMEM((groups, 4, rows), wide),
            pltpu.VMEM((groups, 4, rows), wide),
            pltpu.VMEM((groups, 4, rows), wide),
            pltpu.VMEM((groups, 4, rows), wide),
            pltpu.VMEM((groups, span, rows), narrow),
            pltpu.VMEM((groups, span, rows), narrow),
            pltpu.VMEM((groups, rows, span), narrow),
            pltpu.VMEM((groups, span, rows), narrow),
            pltpu.VMEM((groups, span, rows), narrow),
            pltpu.VMEM((3, length, 2 * rows), narrow),
            pltpu.VMEM((3, 2 * length, rows), wide),
            pltpu.VMEM((2 * length, 2 * rows), narrow),
            pltpu.VMEM((length, rows), narrow),
            pltpu.VMEM((length, rows), narrow),
            pltpu.VMEM((length, rows), narrow),
            pltpu.VMEM((groups, span, rows), narrow),
            pltpu.VMEM((groups, span, rows), narrow),
            pltpu.VMEM((groups, 8, rows), wide),
            pltpu.VMEM((groups, 8, rows), wide),
            dma((7,)),
            dma((kinds,)),
            dma((kinds,)),
        ],
        compiler_params=pltpu.CompilerParams(
            collective_id=0, has_side_effects=True, vmem_limit_bytes=40 * 2**20
        ),
    )(
        *[
            pltpu.with_memory_space_constraint(value, pltpu.HBM)
            for value in (
                features,
                cotangent,
                long_filter,
                jnp.swapaxes(short_filters, 1, 2),
                skip_gain[None],
                jnp.asarray(forward_table),
                jnp.asarray(back_table),
            )
        ]
    )
    gated_out, feature_grad, long_grad, taps_grad, gain_grad = pl.pallas_call(
        functools.partial(settle_kernel, (groups, rows, span, taps)),
        out_shape=(
            jax.ShapeDtypeStruct((channels, span), narrow),
            jax.ShapeDtypeStruct((3, channels, span), narrow),
            jax.ShapeDtypeStruct((channels, span), narrow),
            jax.ShapeDtypeStruct((3, taps, channels), wide),
            jax.ShapeDtypeStruct((1, channels), wide),
        ),
        in_specs=[vmem] * 5,
        out_specs=(hbm,) * 5,
        scratch_shapes=[
            pltpu.VMEM((3, taps, channels), wide),
            pltpu.VMEM((1, channels), wide),
            dma((5,)),
        ],
    )(*[pltpu.with_memory_space_constraint(value, pltpu.VMEM) for value in middle])
    return gated_out, feature_grad, long_grad, jnp.swapaxes(taps_grad, 1, 2), gain_grad[0]


def dense_fits(features, short_filters, groups):
    channels, span = features.shape[1:]
    rows, length = channels // groups, span * groups
    return (
        channels % groups == 0
        and groups % 2 == 0
        and groups > 2
        and rows == 128
        and span == 128
        and length % 512 == 0
        and length <= 1024
        and 2 <= short_filters.shape[2] <= 3
    )


def shards(features, cotangent, long_filter, short_filters, skip_gain):
    groups = lax.axis_size("seq")
    if dense_fits(features, short_filters, groups):
        return fused(features, cotangent, long_filter, short_filters, skip_gain, groups)
    seq_index = lax.axis_index("seq")
    channels = features.shape[1]
    per_group = channels // groups
    margin = short_filters.shape[2] - 1
    local_gain = lax.dynamic_slice_in_dim(skip_gain, seq_index * per_group, per_group, 0)
    stacked = jnp.concatenate([features, cotangent[None], long_filter[None]], 0)
    columns = lax.all_to_all(stacked, "seq", split_axis=1, concat_axis=2, tiled=True)
    weights = lax.dynamic_slice_in_dim(short_filters, seq_index * per_group, per_group, 1)
    length = columns.shape[2]
    history = jnp.pad(columns[:3].astype(jnp.float32), ((0, 0), (0, 0), (margin, 0)))
    primed = featurize(history, weights, margin, length)
    mixed_term = (primed[1] * primed[2]).astype(jnp.bfloat16)
    cot_wide = columns[3].astype(jnp.float32)
    gated_grad = (cot_wide * primed[0]).astype(jnp.bfloat16)
    long_out, mixed_grad, kernel_grad = spectral(mixed_term, gated_grad, columns[4], local_gain)
    long_wide = long_out.astype(jnp.float32)
    mixed_back = mixed_grad.astype(jnp.float32)
    gated_out = (primed[0] * long_wide).astype(jnp.bfloat16)
    primed_grad = jnp.stack([cot_wide * long_wide, mixed_back * primed[2], mixed_back * primed[1]])
    padded_grad = jnp.pad(primed_grad, ((0, 0), (0, 0), (0, margin)))
    feature_grad = unfeaturize(padded_grad, weights, length).astype(jnp.bfloat16)
    taps_grad = tap_grads(primed_grad, history, margin, length)
    gain_grad = jnp.sum(gated_grad.astype(jnp.float32) * mixed_term.astype(jnp.float32), axis=-1)
    results = jnp.concatenate([gated_out[None], feature_grad, kernel_grad[None]], 0)
    row_blocks = lax.all_to_all(results, "seq", split_axis=2, concat_axis=1, tiled=True)
    short_grad, skip_grad = (
        lax.all_gather(taps_grad, "seq", axis=1, tiled=True),
        lax.all_gather(gain_grad, "seq", axis=0, tiled=True),
    )
    return (row_blocks[0], row_blocks[1:4], row_blocks[4], short_grad, skip_grad)


def solution(mesh):
    placed = (
        P(None, "chan", "seq"),
        P("chan", "seq"),
        P("chan", "seq"),
        P(None, "chan", None),
        P("chan"),
    )
    return jax.shard_map(
        shards,
        mesh=mesh,
        in_specs=placed,
        out_specs=(
            P("chan", "seq"),
            P(None, "chan", "seq"),
            P("chan", "seq"),
            P(None, "chan", None),
            P("chan"),
        ),
        check_vma=False,
    )
```
